32 devices in a mesh: gx: 8 (over y, x, core), gy: 4 (over z).
Axes of the slice: x: 2, y: 2, z: 4, core: 2. Of those that a mesh axis runs over, the one named last changes fastest.
Arguments:
- tracer: float32 [2, 16, 1792, 1024], P(None, None, 'gx', 'gy'), may hold values from -6 to 6
- zonal_flow: bfloat16 [16, 1792, 1024], P(None, 'gx', 'gy'), may hold values from -3 to 3
- meridional_flow: bfloat16 [16, 1792, 1024], P(None, 'gx', 'gy'), may hold values from -3 to 3
- surface_prev: float32 [1792, 1024], P('gx', 'gy'), may hold values from -6 to 6
- transport_x: float32 [1792, 1024], P('gx', 'gy'), may hold values from -6 to 6
- transport_y: float32 [1792, 1024], P('gx', 'gy'), may hold values from -6 to 6
- land_mask: int32 [1792, 1024], P('gx', 'gy'), may hold values 0 or 1
- levels: int32 [1792, 1024], P('gx', 'gy'), may hold values from 1 to 16
Outputs:
- tracer_next: float32 [2, 16, 1792, 1024], P(None, None, 'gx', 'gy')
- surface: float32 [1792, 1024], P('gx', 'gy')
- transport_x_next: float32 [1792, 1024], P('gx', 'gy')
- transport_y_next: float32 [1792, 1024], P('gx', 'gy')
The draws below stay inside these ranges and needn't reach their ends.
All inputs are finite; a program needn't handle non-finite values. No bound on the sum of `land_mask` on one device may be relied on, other than what follows from the above.
Results may differ from the reference program's by a relative error of at most 0.0003.
Values sent between devices are 32-bit elements; how exact they have to be, the bound alone decides.
No kernel may reach another device: no remote copies, remote signals or barrier semaphores. Data moves between devices by JAX's collectives and lax.ppermute only.
A program may use at most 192 MiB of HBM per device.

```python
import jax
import jax.numpy as jnp
from jax import lax

LEVELS = 16
ITERS = 4
NX = 1792
NY = 1024


def plant(entries, rng, low, largest):
    longest = entries.shape.index(max(entries.shape))
    spots = []
    for shift in (0, 1):
        where = [jax.random.randint(jax.random.fold_in(rng, axis), (), 0, length) for axis, length in enumerate(entries.shape)]
        where[longest] = (where[longest] + shift) % entries.shape[longest]
        spots.append(tuple(where))
    return entries.at[spots[0]].set(low).at[spots[1]].set(largest)


def steps_of(stream_key, shape, cuts, smallest, largest):
    gain, own = 1.0, jax.random.fold_in(stream_key, 6)
    for position, blocks in cuts:
        heights = jnp.exp(jax.random.uniform(jax.random.fold_in(own, position), (blocks,), jnp.float32, smallest / len(cuts), largest / len(cuts)))
        gain = gain * jnp.repeat(heights, shape[position] // blocks).reshape([-1 if axis == position else 1 for axis in range(len(shape))])
    return gain


def gaussian(rng, dims, scale, most, cuts=(), kind=jnp.bfloat16):
    values = jax.random.normal(rng, dims, jnp.float32) * scale
    if len(cuts) > 0:
        values = steps_of(rng, dims, cuts, -0.22, 0.18) * values
    return jnp.clip(values, min=-most, max=most).astype(kind)


def setup_inputs(seed: int = 0) -> dict:
    splits = jax.random.split(jax.random.key(seed), 9)
    tracer = gaussian(splits[0], (2, LEVELS, NX, NY), 1.0, 6.0, ((2, 8), (3, 4)), jnp.float32)
    zonal_flow = gaussian(splits[1], (LEVELS, NX, NY), 0.5, 3.0, ((1, 8), (2, 4)))
    meridional_flow = gaussian(splits[2], (LEVELS, NX, NY), 0.5, 3.0, ((1, 8), (2, 4)))
    surface_prev = gaussian(splits[3], (NX, NY), 1.0, 6.0, ((0, 8), (1, 4)), jnp.float32)
    transport_x = gaussian(splits[4], (NX, NY), 1.0, 6.0, ((0, 8), (1, 4)), jnp.float32)
    transport_y = gaussian(splits[5], (NX, NY), 1.0, 6.0, ((0, 8), (1, 4)), jnp.float32)
    land_mask = plant((jax.random.randint(splits[6], (NX, NY), 0, 4) < 3).astype(jnp.int32), jax.random.fold_in(splits[6], 1), 0, 1)
    levels = plant(jax.random.randint(splits[7], (NX, NY), 1, LEVELS + 1), jax.random.fold_in(splits[7], 1), 1, LEVELS).astype(jnp.int32)
    return {"tracer": tracer, "zonal_flow": zonal_flow, "meridional_flow": meridional_flow, "surface_prev": surface_prev, "transport_x": transport_x, "transport_y": transport_y, "land_mask": land_mask, "levels": levels}


OFFSETS = ((1, 0, 1.0), (-1, 0, 1.0), (0, 1, 1.0), (0, -1, 1.0), (1, 1, 0.5), (1, -1, 0.5), (-1, 1, 0.5), (-1, -1, 0.5))


def cycle_pad(field):
    wide = jnp.concatenate([field[..., -1:, :], field, field[..., :1, :]], -2)
    zero = jnp.zeros_like(wide[..., :1])
    return jnp.concatenate([zero, wide, zero], -1)


def advance(wide, zonal, merid):
    centre = wide[..., 1:-1, 1:-1]
    east = wide[..., 2:, 1:-1]
    west = wide[..., :-2, 1:-1]
    north = wide[..., 1:-1, 2:]
    south = wide[..., 1:-1, :-2]
    values = centre[:2]
    wet_here = centre[2]
    lap = east[2] * (east[:2] - values) + west[2] * (west[:2] - values)
    lap = lap + north[2] * (north[:2] - values) + south[2] * (south[:2] - values)
    speed_x = zonal.astype(jnp.float32)
    speed_y = merid.astype(jnp.float32)
    adv = speed_x * (east[2] * east[:2] - west[2] * west[:2]) * 0.5
    adv = adv + speed_y * (north[2] * north[:2] - south[2] * south[:2]) * 0.5
    return values + wet_here * (0.2 * lap - 0.5 * adv)


def couplings(depth_pad):
    depth = depth_pad[1:-1, 1:-1]
    count_x, count_y = depth.shape
    ocean = (depth > 0).astype(jnp.float32)
    weights = []
    for shift_x, shift_y, factor in OFFSETS:
        other = depth_pad[1 + shift_x:1 + shift_x + count_x, 1 + shift_y:1 + shift_y + count_y]
        weights.append(4.0 * factor * ocean * (other > 0).astype(jnp.float32) * 0.5 * (depth + other))
    diag = 0.5 + sum(weights)
    return weights, diag


def operate(weights, diag, surf_pad):
    count_x, count_y = diag.shape
    total = diag * surf_pad[1:-1, 1:-1]
    for (shift_x, shift_y, factor), weight in zip(OFFSETS, weights):
        total = total - weight * surf_pad[1 + shift_x:1 + shift_x + count_x, 1 + shift_y:1 + shift_y + count_y]
    return total


def reference(tracer, zonal_flow, meridional_flow, surface_prev, transport_x, transport_y, land_mask, levels):
    ocean_col = land_mask == 1

    def level_step(items):
        temp, zonal, merid, level = items
        wet_k = (ocean_col & (level < levels)).astype(jnp.float32)
        wide = cycle_pad(jnp.concatenate([temp, wet_k[None]], 0))
        return advance(wide, zonal, merid)

    level_ids = jnp.arange(LEVELS, dtype=jnp.int32)
    stepped = lax.map(level_step, (jnp.moveaxis(tracer, 1, 0), zonal_flow, meridional_flow, level_ids))
    tracer_next = jnp.moveaxis(stepped, 0, 1)

    def column(carry, items):
        press, accum = carry
        temp, level = items
        wet_k = (ocean_col & (level < levels)).astype(jnp.float32)
        press = press + wet_k * (0.8 * temp[0] - 0.6 * temp[1])
        accum = accum + wet_k * press
        return (press, accum), None

    zero = jnp.zeros(surface_prev.shape, jnp.float32)
    (press, accum), _ = lax.scan(column, (zero, zero), (jnp.moveaxis(tracer, 1, 0), level_ids))
    force = accum / LEVELS
    depth = (levels * land_mask).astype(jnp.float32) / LEVELS
    ocean = (depth > 0).astype(jnp.float32)
    padded = cycle_pad(jnp.stack([depth, transport_x, transport_y]))
    weights, diag = couplings(padded[0])
    ocean_pad = (padded[0] > 0).astype(jnp.float32)
    flux_x = ocean_pad * padded[1]
    flux_y = ocean_pad * padded[2]
    div = (flux_x[2:, 1:-1] - flux_x[:-2, 1:-1]) * 0.5 + (flux_y[1:-1, 2:] - flux_y[1:-1, :-2]) * 0.5
    rhs = 0.5 * surface_prev + force - 0.5 * div
    peak = jnp.max(diag)
    lowest = 0.5 / peak
    scale = 1.0 / (1.0 - lowest)
    surf = surface_prev
    resid = rhs - operate(weights, diag, cycle_pad(surf))
    delta = resid / diag
    omega = 2.0
    surf = surf + delta
    for step in range(1, ITERS):
        resid = rhs - operate(weights, diag, cycle_pad(surf))
        omega = 1.0 / (1.0 - omega / (4.0 * scale * scale))
        delta = omega * resid / diag + (omega - 1.0) * delta
        surf = surf + delta
    surf_pad = cycle_pad(surf)
    next_x = ocean * (transport_x - 0.5 * (surf_pad[2:, 1:-1] - surf_pad[:-2, 1:-1]) * 0.5)
    next_y = ocean * (transport_y - 0.5 * (surf_pad[1:-1, 2:] - surf_pad[1:-1, :-2]) * 0.5)
    return tracer_next, surf, next_x, next_y
```

```python
import functools

import jax
import jax.numpy as jnp
from jax import lax
from jax.experimental import pallas as pl
from jax.experimental.pallas import tpu as pltpu
from jax.sharding import PartitionSpec as P

ITERS = 4
WIDTH = ITERS + 1
LANES = 128
SUB = 8
HALF = LANES // 2
FIELDS = 5
F32 = jnp.float32


def lane_ids(rows):
    return lax.broadcasted_iota(jnp.int32, (rows, LANES), 1)


def put_lane(value, source, target):
    shift = (target - source) % LANES
    return pltpu.roll(value, shift, 1) if shift else value


def column_kernel(tracer, land, levels, force, depth, edge, first, last):
    step = pl.program_id(0)
    count = tracer.shape[1]
    rows, cols = land.shape
    sides = cols // LANES
    lanes = lane_ids(SUB)
    for r in range(0, rows, SUB):
        at = pl.ds(r, SUB)
        packed = jnp.zeros((SUB, LANES), F32)
        for h in range(sides):
            span = pl.ds(h * LANES, LANES)
            deep = (land[at, span] * levels[at, span]).astype(F32)
            total = jnp.zeros((SUB, LANES), F32)
            for k in range(count):
                warm = tracer[0, k, at, span]
                salt = tracer[1, k, at, span]
                total = total + jnp.maximum(deep - k, 0.0) * (0.8 * warm - 0.6 * salt)
                for c, value in ((0, warm), (1, salt)):
                    lane = c * count + k
                    if h == 0:
                        packed = jnp.where(lanes == lane, put_lane(value, 0, lane), packed)
                    if h == sides - 1:
                        there = 2 * count + lane
                        packed = jnp.where(
                            lanes == there, put_lane(value, LANES - 1, there), packed
                        )
            force[at, span] = total * (1.0 / count)
            depth[at, span] = deep
        edge[at, :] = packed

    @pl.when(step == 0)
    def _():
        for c in range(2):
            for k in range(count):
                first[pl.ds(c * count + k, 1), :] = tracer[c, k, pl.ds(0, 1), :]

    @pl.when(step == pl.num_programs(0) - 1)
    def _():
        for c in range(2):
            for k in range(count):
                last[pl.ds(c * count + k, 1), :] = tracer[c, k, pl.ds(rows - 1, 1), :]


def column_pass(tracer, land, levels, chunk):
    two, count, rows, cols = tracer.shape
    flat = pl.BlockSpec((chunk, cols), lambda i: (i, 0))
    whole = pl.BlockSpec((two * count, cols), lambda i: (0, 0))
    return pl.pallas_call(
        column_kernel,
        grid=(rows // chunk,),
        in_specs=[
            pl.BlockSpec((two, count, chunk, cols), lambda i: (0, 0, i, 0)),
            flat,
            flat,
        ],
        out_specs=[flat, flat, pl.BlockSpec((chunk, LANES), lambda i: (i, 0)), whole, whole],
        out_shape=[
            jax.ShapeDtypeStruct((rows, cols), F32),
            jax.ShapeDtypeStruct((rows, cols), F32),
            jax.ShapeDtypeStruct((rows, LANES), F32),
            jax.ShapeDtypeStruct((two * count, cols), F32),
            jax.ShapeDtypeStruct((two * count, cols), F32),
        ],
        cost_estimate=pl.CostEstimate(
            flops=6 * tracer.size, bytes_accessed=4 * tracer.size, transcendentals=0
        ),
        name="columns",
    )(tracer, land, levels)


def pack_kernel(count, edge, depth, surf, flow_x, flow_y, force, west, east, south_out, north_out):
    rows, cols = depth.shape
    sides = cols // LANES
    half = rows // 2
    lanes = lane_ids(SUB)
    fields = (depth, surf, flow_x, flow_y, force)
    base = 2 * count

    def strips(load):
        low = jnp.zeros((SUB, LANES), F32)
        high = jnp.zeros((SUB, LANES), F32)
        for f in range(FIELDS):
            at = base + f * WIDTH
            inside = (lanes >= at) & (lanes < at + WIDTH)
            low = jnp.where(inside, put_lane(load(f, 0), 0, at), low)
            high = jnp.where(inside, put_lane(load(f, sides - 1), LANES - WIDTH, at), high)
        return low, high

    def centre(r):
        def load(f, h):
            return fields[f][pl.ds(r, SUB), pl.ds(h * LANES, LANES)]

        low, high = strips(load)
        both = edge[pl.ds(r, SUB), :]
        low = jnp.where(lanes < base, both, low)
        high = jnp.where(lanes < base, put_lane(both, base, 0), high)
        return low, high

    def beyond(ref):
        def load(f, h):
            return ref[pl.ds(base + f * SUB, SUB), pl.ds(h * LANES, LANES)]

        return strips(load)

    def emit(row, lower, upper):
        for out, index in ((south_out, 0), (north_out, 1)):
            out[pl.ds(row, SUB), :] = jnp.where(
                lanes < HALF, lower[index], pltpu.roll(upper[index], HALF, 1)
            )

    for r in range(0, half, SUB):
        emit(r, centre(r), centre(half + r))
    emit(half, beyond(west), beyond(east))


def pack_pass(count, edge, depth, surf, flow_x, flow_y, force, west, east):
    rows, _ = depth.shape
    shape = jax.ShapeDtypeStruct((rows // 2 + SUB, LANES), F32)
    return pl.pallas_call(
        functools.partial(pack_kernel, count),
        out_shape=[shape, shape],
        cost_estimate=pl.CostEstimate(
            flops=depth.size, bytes_accessed=24 * depth.size, transcendentals=0
        ),
        name="pack",
    )(edge, depth, surf, flow_x, flow_y, force, west, east)


def message_rows(ref, rows, r):
    half = rows // 2
    if r < 0:
        return ref[pl.ds(half, SUB), :]
    if r >= rows:
        return pltpu.roll(ref[pl.ds(half, SUB), :], HALF, 1)
    if r < half:
        return ref[pl.ds(r, SUB), :]
    return pltpu.roll(ref[pl.ds(r - half, SUB), :], HALF, 1)


def outer_tile(south, north, rows, r, at, open_south, open_north, lanes):
    up = put_lane(message_rows(north, rows, r), at, 0)
    down = put_lane(message_rows(south, rows, r), at, LANES - WIDTH)
    up = jnp.where((lanes < WIDTH) & open_north, up, 0.0)
    return jnp.where((lanes >= LANES - WIDTH) & open_south, down, up)


def extend(target, base, f, field, west, east, south, north, open_south, open_north):
    rows, cols = field.shape
    sides = cols // LANES
    lanes = lane_ids(SUB)
    at = base + f * WIDTH
    for r in range(-SUB, rows + 1, SUB):
        to = pl.ds(SUB + r, SUB)
        for h in range(sides):
            span = pl.ds(h * LANES, LANES)
            if r < 0:
                target[h, to, :] = west[pl.ds(base + f * SUB, SUB), span]
            elif r >= rows:
                target[h, to, :] = east[pl.ds(base + f * SUB, SUB), span]
            else:
                target[h, to, :] = field[pl.ds(r, SUB), span]
        target[sides, to, :] = outer_tile(
            south, north, rows, r, at, open_south, open_north, lanes
        )


def latitude_ends():
    place, size = lax.axis_index("gy"), lax.axis_size("gy")
    return place > 0, place < size - 1


def ring_shift(tiles, lanes):
    size = len(tiles)
    after = [pltpu.roll(t, LANES - 1, 1) for t in tiles]
    before = [pltpu.roll(t, 1, 1) for t in tiles]
    nxt = [jnp.where(lanes == LANES - 1, after[(h + 1) % size], after[h]) for h in range(size)]
    prv = [jnp.where(lanes == 0, before[(h - 1) % size], before[h]) for h in range(size)]
    return nxt, prv


def nine_sum(ref, r, lanes):
    sides = [ref[h, pl.ds(r + 1, SUB), :] + ref[h, pl.ds(r - 1, SUB), :] for h in range(ref.shape[0])]
    mixed = [ref[h, pl.ds(r, SUB), :] + 0.5 * sides[h] for h in range(ref.shape[0])]
    nxt, prv = ring_shift(mixed, lanes)
    return [sides[h] + (nxt[h] + prv[h]) for h in range(ref.shape[0])]


def peak_kernel(base, depth, west, east, south, north, peak, deep, wet):
    rows, cols = depth.shape
    sides = cols // LANES
    lanes = lane_ids(SUB)
    open_south, open_north = latitude_ends()
    scale = 1.0 / (base // 2)
    extend(deep, base, 0, depth, west, east, south, north, open_south, open_north)
    for r in range(0, rows + 2 * SUB, SUB):
        for h in range(sides + 1):
            d = deep[h, pl.ds(r, SUB), :] * scale
            deep[h, pl.ds(r, SUB), :] = d
            wet[h, pl.ds(r, SUB), :] = jnp.where(d > 0, 1.0, 0.0)
    best = jnp.full((SUB, LANES), 0.0, F32)
    for r in range(SUB, rows + SUB, SUB):
        sum_wet = nine_sum(wet, r, lanes)
        sum_deep = nine_sum(deep, r, lanes)
        for h in range(sides):
            d = deep[h, pl.ds(r, SUB), :]
            m = wet[h, pl.ds(r, SUB), :]
            best = jnp.maximum(best, 0.5 + 2.0 * (d * sum_wet[h] + m * sum_deep[h]))
    best = jnp.max(jnp.max(best, axis=1, keepdims=True), axis=0, keepdims=True)
    peak[...] = jnp.broadcast_to(best, (SUB, LANES))


def peak_pass(base, depth, west, east, south, north):
    rows, cols = depth.shape
    ext = pltpu.VMEM((cols // LANES + 1, rows + 2 * SUB, LANES), F32)
    return pl.pallas_call(
        functools.partial(peak_kernel, base),
        out_shape=jax.ShapeDtypeStruct((SUB, LANES), F32),
        scratch_shapes=[ext, ext],
        cost_estimate=pl.CostEstimate(
            flops=30 * depth.size, bytes_accessed=4 * depth.size, transcendentals=0
        ),
        name="peak",
    )(depth, west, east, south, north)


def tracer_kernel(
    start, tracer, zonal, merid, depth, west, east, south, north, *rest
):
    out, edge_x, edge_y, around, masked = rest[-5:]
    step = pl.program_id(0)
    count = edge_x.shape[0] // 4
    rows, cols = depth.shape
    sides = cols // LANES
    base = 2 * count
    level = step + start
    lanes = lane_ids(SUB)

    @pl.when(step == 0)
    def _():
        open_south, open_north = latitude_ends()
        kinds = lax.broadcasted_iota(jnp.int32, (base, LANES), 0)
        kinds = jnp.where(kinds < count, kinds, kinds - count).astype(F32)
        for side, (ref, line) in enumerate(((west, SUB - 1), (east, 0))):
            for h in range(sides):
                span = pl.ds(h * LANES, LANES)
                deep = ref[pl.ds(base + line, 1), span]
                value = jnp.where(deep > kinds, ref[pl.ds(0, base), span], 0.0)
                for i in range(base):
                    edge_x[side * base + i, h : h + 1, :] = value[i : i + 1]
        kinds = jnp.where(lanes < count, lanes, lanes - count).astype(F32)
        for side, (ref, column, is_open) in enumerate(
            ((south, base + WIDTH - 1, open_south), (north, base, open_north))
        ):
            for r in range(0, rows, SUB):
                value = message_rows(ref, rows, r)
                deep = jnp.where(is_open, value[:, column : column + 1], 0.0)
                edge_y[side, pl.ds(r, SUB), :] = jnp.where(deep > kinds, value, 0.0)
                deep_lane = put_lane(value, column, LANES - 1 if side else 0)
                deep_lane = jnp.where(is_open, deep_lane, 0.0)
                if side == 0:
                    tile = depth[pl.ds(r, SUB), pl.ds(0, LANES)]
                    prev = jnp.where(lanes == 0, deep_lane, pltpu.roll(tile, 1, 1))
                    around[3, 0, pl.ds(r, SUB), :] = prev
                    for h in range(1, sides):
                        back = pltpu.roll(depth[pl.ds(r, SUB), pl.ds((h - 1) * LANES, LANES)], 1, 1)
                        here = pltpu.roll(depth[pl.ds(r, SUB), pl.ds(h * LANES, LANES)], 1, 1)
                        around[3, h, pl.ds(r, SUB), :] = jnp.where(lanes == 0, back, here)
                else:
                    for h in range(sides):
                        here = pltpu.roll(
                            depth[pl.ds(r, SUB), pl.ds(h * LANES, LANES)], LANES - 1, 1
                        )
                        ahead = deep_lane
                        if h + 1 < sides:
                            ahead = pltpu.roll(
                                depth[pl.ds(r, SUB), pl.ds((h + 1) * LANES, LANES)], LANES - 1, 1
                            )
                        around[2, h, pl.ds(r, SUB), :] = jnp.where(
                            lanes == LANES - 1, ahead, here
                        )
        for h in range(sides):
            span = pl.ds(h * LANES, LANES)
            masked[0, h, pl.ds(0, SUB), :] = west[pl.ds(base, SUB), span]
            masked[0, h, pl.ds(SUB, rows), :] = depth[:, span]
            masked[0, h, pl.ds(SUB + rows, SUB), :] = east[pl.ds(base, SUB), span]
            for r in range(0, rows, SUB):
                around[0, h, pl.ds(r, SUB), :] = masked[0, h, pl.ds(SUB + r + 1, SUB), :]
                around[1, h, pl.ds(r, SUB), :] = masked[0, h, pl.ds(SUB + r - 1, SUB), :]

    mark = level.astype(F32)
    for h in range(sides):
        span = pl.ds(h * LANES, LANES)
        for c in range(2):
            masked[c, h, pl.ds(SUB - 1, 1), :] = edge_x[c * count + level, h : h + 1, :]
            masked[c, h, pl.ds(SUB + rows, 1), :] = edge_x[base + c * count + level, h : h + 1, :]
            for r in range(0, rows, SUB):
                here = depth[pl.ds(r, SUB), span] > mark
                masked[c, h, pl.ds(SUB + r, SUB), :] = jnp.where(
                    here, tracer[c, 0, pl.ds(r, SUB), span], 0.0
                )
    for big in range(0, rows, 2 * SUB):
        speeds = []
        for h in range(sides):
            span = pl.ds(h * LANES, LANES)
            speeds.append(
                (
                    zonal[0, pl.ds(big, 2 * SUB), span].astype(F32),
                    merid[0, pl.ds(big, 2 * SUB), span].astype(F32),
                )
            )
        for sub in range(2):
            r = big + sub * SUB
            at = pl.ds(r, SUB)
            factors = []
            for h in range(sides):
                span = pl.ds(h * LANES, LANES)
                here = depth[at, span] > mark
                near = jnp.zeros((SUB, LANES), F32)
                for n in range(4):
                    near = near + jnp.where(around[n, h, at, :] > mark, 1.0, 0.0)
                mix = jnp.where(here, 0.2, 0.0)
                u = jnp.where(here, 0.25 * speeds[h][0][sub * SUB : (sub + 1) * SUB], 0.0)
                v = jnp.where(here, 0.25 * speeds[h][1][sub * SUB : (sub + 1) * SUB], 0.0)
                factors.append((1.0 - mix * near, mix - u, mix + u, mix - v, mix + v))
            for c in range(2):
                tiles = [masked[c, h, pl.ds(SUB + r, SUB), :] for h in range(sides)]
                lane = c * count + level
                from_south = pltpu.roll(edge_y[0, at, :], LANES - lane, 1)
                from_north = pltpu.roll(edge_y[1, at, :], LANES - 1 - lane, 1)
                after = [pltpu.roll(t, LANES - 1, 1) for t in tiles] + [from_north]
                before = [from_south] + [pltpu.roll(t, 1, 1) for t in tiles]
                for h in range(sides):
                    span = pl.ds(h * LANES, LANES)
                    own, to_e, to_w, to_n, to_s = factors[h]
                    nxt = jnp.where(lanes == LANES - 1, after[h + 1], after[h])
                    prv = jnp.where(lanes == 0, before[h], before[h + 1])
                    value = own * tracer[c, 0, at, span] + to_n * nxt + to_s * prv
                    value = value + to_e * masked[c, h, pl.ds(SUB + r + 1, SUB), :]
                    value = value + to_w * masked[c, h, pl.ds(SUB + r - 1, SUB), :]
                    out[c, 0, at, span] = value


def tracer_pass(start, stop, tracer, zonal, merid, depth, west, east, south, north, into=None):
    two, count, rows, cols = tracer.shape
    sides = cols // LANES
    block = pl.BlockSpec((two, 1, rows, cols), lambda k: (0, k + start, 0, 0))
    speed = pl.BlockSpec((1, rows, cols), lambda k: (k + start, 0, 0))

    def fixed(value):
        return pl.BlockSpec(value.shape, lambda k: (0, 0))

    small = [depth, west, east, south, north]
    operands = [tracer, zonal, merid, *small]
    specs = [block, speed, speed] + [fixed(v) for v in small]
    aliases = {}
    if into is not None:
        aliases = {len(operands): 0}
        operands.append(into)
        specs.append(pl.BlockSpec(memory_space=pl.ANY))
    part = stop - start
    return pl.pallas_call(
        functools.partial(tracer_kernel, start),
        grid=(part,),
        in_specs=specs,
        out_specs=block,
        out_shape=jax.ShapeDtypeStruct(tracer.shape, F32),
        scratch_shapes=[
            pltpu.VMEM((4 * count, sides, LANES), F32),
            pltpu.VMEM((2, rows, LANES), F32),
            pltpu.VMEM((4, sides, rows, LANES), F32),
            pltpu.VMEM((2, sides, rows + 2 * SUB, LANES), F32),
        ],
        input_output_aliases=aliases,
        cost_estimate=pl.CostEstimate(
            flops=40 * tracer.size * part // count,
            bytes_accessed=10 * tracer.size * part // count,
            transcendentals=0,
        ),
        name="tracers",
    )(*operands)


def solve_kernel(
    base, peak, depth, surf, flow_x, flow_y, force, west, east, south, north,
    surf_out, x_out, y_out, deep, wet, surf0, flux_x, flux_y, forced, left, right, start, step_by, total,
):
    rows, cols = depth.shape
    sides = cols // LANES
    tiles = sides + 1
    lanes = lane_ids(SUB)
    open_south, open_north = latitude_ends()
    halo = (west, east, south, north, open_south, open_north)
    scale = 1.0 / (base // 2)
    extend(deep, base, 0, depth, *halo)
    extend(surf0, base, 1, surf, *halo)
    extend(flux_x, base, 2, flow_x, *halo)
    extend(flux_y, base, 3, flow_y, *halo)
    extend(forced, base, 4, force, *halo)
    every = range(0, rows + 2 * SUB, SUB)
    inner = range(SUB, rows + SUB, SUB)

    for r in every:
        at = pl.ds(r, SUB)
        for h in range(tiles):
            d = deep[h, at, :] * scale
            m = jnp.where(d > 0, 1.0, 0.0)
            deep[h, at, :] = d
            wet[h, at, :] = m
            flux_x[h, at, :] = m * flux_x[h, at, :]
            flux_y[h, at, :] = m * flux_y[h, at, :]
            total[h, at, :] = m * surf0[h, at, :]
            step_by[h, at, :] = d * surf0[h, at, :]

    def clamp_rows(r):
        return min(max(r, 1), rows + 2 * SUB - SUB - 1)

    spans = [clamp_rows(r) for r in every]
    for r in spans:
        at = pl.ds(r, SUB)
        sum_wet = nine_sum(wet, r, lanes)
        sum_deep = nine_sum(deep, r, lanes)
        sum_f = nine_sum(total, r, lanes)
        sum_g = nine_sum(step_by, r, lanes)
        nxt, prv = ring_shift([flux_y[h, at, :] for h in range(tiles)], lanes)
        for h in range(tiles):
            d = deep[h, at, :]
            m = wet[h, at, :]
            inverse = 1.0 / (0.5 + 2.0 * (d * sum_wet[h] + m * sum_deep[h]))
            a = 2.0 * d * inverse
            b = 2.0 * m * inverse
            left[h, at, :] = a
            right[h, at, :] = b
            e = surf0[h, at, :]
            div = 0.5 * (
                flux_x[h, pl.ds(r + 1, SUB), :] - flux_x[h, pl.ds(r - 1, SUB), :]
            ) + 0.5 * (nxt[h] - prv[h])
            rhs = 0.5 * e + forced[h, at, :] - 0.5 * div
            start[h, at, :] = rhs * inverse - e + a * sum_f[h] + b * sum_g[h]

    top = peak[...]
    lowest = 0.5 / top
    shrink = (1.0 - lowest) * (1.0 - lowest)
    omega = jnp.full((SUB, LANES), 2.0, F32)
    for r in every:
        at = pl.ds(r, SUB)
        for h in range(tiles):
            z = start[h, at, :]
            total[h, at, :] = z
            step_by[h, at, :] = z
            flux_x[h, at, :] = wet[h, at, :] * z
            flux_y[h, at, :] = deep[h, at, :] * z
    for turn in range(1, ITERS):
        omega = 1.0 / (1.0 - omega * shrink * 0.25)
        for r in spans:
            at = pl.ds(r, SUB)
            sum_f = nine_sum(flux_x, r, lanes)
            sum_g = nine_sum(flux_y, r, lanes)
            for h in range(tiles):
                s = total[h, at, :]
                y = start[h, at, :] - s + left[h, at, :] * sum_f[h] + right[h, at, :] * sum_g[h]
                delta = omega * y + (omega - 1.0) * step_by[h, at, :]
                forced[h, at, :] = delta
        for r in every:
            at = pl.ds(r, SUB)
            for h in range(tiles):
                delta = forced[h, at, :]
                s = total[h, at, :] + delta
                total[h, at, :] = s
                step_by[h, at, :] = delta
                flux_x[h, at, :] = wet[h, at, :] * s
                flux_y[h, at, :] = deep[h, at, :] * s

    for r in every:
        at = pl.ds(r, SUB)
        for h in range(tiles):
            value = surf0[h, at, :] + total[h, at, :]
            if h == sides:
                value = jnp.where((lanes < WIDTH) & open_north, value, jnp.where(
                    (lanes >= LANES - WIDTH) & open_south, value, 0.0))
            total[h, at, :] = value
    for r in inner:
        at = pl.ds(r, SUB)
        back = pl.ds(r - SUB, SUB)
        nxt, prv = ring_shift([total[h, at, :] for h in range(tiles)], lanes)
        for h in range(sides):
            span = pl.ds(h * LANES, LANES)
            m = wet[h, at, :]
            surf_out[back, span] = total[h, at, :]
            slope = total[h, pl.ds(r + 1, SUB), :] - total[h, pl.ds(r - 1, SUB), :]
            x_out[back, span] = m * (flow_x[back, span] - 0.25 * slope)
            y_out[back, span] = m * (flow_y[back, span] - 0.25 * (nxt[h] - prv[h]))


def solve_pass(base, peak, depth, surf, flow_x, flow_y, force, west, east, south, north):
    rows, cols = depth.shape
    ext = pltpu.VMEM((cols // LANES + 1, rows + 2 * SUB, LANES), F32)
    shape = jax.ShapeDtypeStruct((rows, cols), F32)
    return pl.pallas_call(
        functools.partial(solve_kernel, base),
        out_shape=[shape] * 3,
        scratch_shapes=[ext] * 11,
        cost_estimate=pl.CostEstimate(
            flops=200 * depth.size, bytes_accessed=32 * depth.size, transcendentals=0
        ),
        name="solve",
    )(peak, depth, surf, flow_x, flow_y, force, west, east, south, north)


def both_ways(axis, to_next, to_previous):
    size = lax.axis_size(axis)
    up = [(i, (i + 1) % size) for i in range(size)]
    down = [(j, i) for i, j in up]
    return lax.ppermute(to_next, axis, up), lax.ppermute(to_previous, axis, down)


def spread_max(value, axis):
    size = lax.axis_size(axis)
    reach = 1
    while reach < size:
        if size & (size - 1) == 0:
            pairs = [(i, i ^ reach) for i in range(size)]
        else:
            pairs = [(i, (i + reach) % size) for i in range(size)]
        value = jnp.maximum(value, lax.ppermute(value, axis, pairs))
        reach *= 2
    return value


def local(
    tracer, zonal_flow, meridional_flow, surface_prev, transport_x, transport_y, land_mask, levels
):
    _, count, rows, cols = tracer.shape
    base = 2 * count
    force, depth, edge, first, last = column_pass(tracer, land_mask, levels, rows // 4)
    fields = (depth, surface_prev, transport_x, transport_y, force)
    to_next = jnp.concatenate([last] + [f[rows - SUB :] for f in fields], 0)
    to_previous = jnp.concatenate([first] + [f[:SUB] for f in fields], 0)
    west, east = both_ways("gx", to_next, to_previous)
    to_south, to_north = pack_pass(count, edge, *fields, west, east)
    south, north = both_ways("gy", to_north, to_south)
    peak = peak_pass(base, depth, west, east, south, north)
    peak = spread_max(spread_max(peak, "gx"), "gy")
    tracer_next = tracer_pass(
        0, count, tracer, zonal_flow, meridional_flow, depth, west, east, south, north
    )
    surf, next_x, next_y = solve_pass(base, peak, *fields, west, east, south, north)
    return (tracer_next, surf, next_x, next_y)


def solution(mesh):
    cell = P("gx", "gy")
    level = P(None, "gx", "gy")
    stack = P(None, None, "gx", "gy")
    return jax.shard_map(
        local,
        mesh=mesh,
        in_specs=(stack, level, level, cell, cell, cell, cell, cell),
        out_specs=(stack, cell, cell, cell),
        check_vma=False,
    )
```

```python
import functools

import jax
import jax.numpy as jnp
from jax import lax
from jax.experimental import pallas as pl
from jax.experimental.pallas import tpu as pltpu
from jax.sharding import PartitionSpec as P

ITERS = 4
WIDTH = ITERS + 1
LANES = 128
SUB = 8
HALF = LANES // 2
FIELDS = 5
F32 = jnp.float32
BF16 = jnp.bfloat16
VMEM_LIMIT = 12 * 1024 * 1024
LEVELS = 16
BASE = 2 * LEVELS
CODE = 1024.0
PARTS = 4


def lane_ids(rows):
    return lax.broadcasted_iota(jnp.int32, (rows, LANES), 1)


def put_lane(value, source, target):
    shift = (target - source) % LANES
    return pltpu.roll(value, shift, 1) if shift else value


def strip_pair(low, high, lanes, values):
    for f, (begin, end) in enumerate(values):
        at = BASE + (f + 1) * WIDTH
        turned = put_lane(jnp.where(lanes < HALF, begin, end), 0, at)
        low = jnp.where((lanes >= at) & (lanes < at + WIDTH), turned, low)
        high = jnp.where((lanes >= at - WIDTH) & (lanes < at), turned, high)
    return low, high


def column_kernel(
    tracer, land, levels, surf, flow_x, flow_y,
    force, depth, to_south, to_north, to_previous, to_next,
):
    step, steps = pl.program_id(0), pl.num_programs(0)
    count = tracer.shape[1]
    rows, cols = land.shape
    sides = cols // LANES
    base = 2 * count
    lanes = lane_ids(SUB)
    upper = step >= steps // 2
    turn = jnp.where(upper, HALF, 0)
    keep = (lanes < HALF) & upper
    first_row = jnp.where(upper, step - steps // 2, step) * rows
    low_kind = jnp.where((lanes >= 1) & (lanes <= base), lax.rem(lanes - 1 + count, count), -1)
    low_kind = low_kind.astype(F32)
    high_kind = jnp.where(lanes < base, lax.rem(lanes, count), -1).astype(F32)
    for r in range(0, rows, SUB):
        at = pl.ds(r, SUB)
        packed = [jnp.zeros((SUB, LANES), F32)] * 2
        totals = [jnp.zeros((SUB, LANES), F32)] * sides
        deeps = []
        for h in range(sides):
            span = pl.ds(h * LANES, LANES)
            deeps.append((land[at, span] * levels[at, span]).astype(F32))
        for k in range(count):
            values = [
                [tracer[c, k, at, pl.ds(h * LANES, LANES)] for h in range(sides)] for c in range(2)
            ]
            for h in range(sides):
                gain = jnp.maximum(deeps[h] - k, 0.0)
                totals[h] = totals[h] + gain * (values[0][h] - 0.75 * values[1][h])
            for c in range(2):
                i = c * count + k
                both = jnp.where(lanes < HALF, values[c][0], values[c][-1])
                both = put_lane(both, 0, i + 1)
                packed[i % 2] = jnp.where((lanes == i) | (lanes == i + 1), both, packed[i % 2])
        totals = [t * (0.8 / count) for t in totals]
        for h in range(sides):
            span = pl.ds(h * LANES, LANES)
            force[at, span] = totals[h]
            depth[at, span] = deeps[h]
        odd = (lanes & 1) == 1
        low = jnp.where(odd, packed[0], packed[1])
        high = jnp.where(odd, packed[1], packed[0])
        low = jnp.where(deeps[0][:, 0:1] > low_kind, low, 0.0)
        high = jnp.where(deeps[-1][:, LANES - 1 : LANES] > high_kind, high, 0.0)
        ends = [pl.ds(0, LANES), pl.ds((sides - 1) * LANES, LANES)]
        low, high = strip_pair(
            low,
            high,
            lanes,
            [(deeps[0], deeps[-1])]
            + [tuple(ref[at, span] for span in ends) for ref in (surf, flow_x, flow_y)]
            + [(totals[0], totals[-1])],
        )
        to = pl.ds(pl.multiple_of(first_row + r, SUB), SUB)
        for out, value in ((to_south, low), (to_north, high)):
            out[to, :] = jnp.where(keep, out[to, :], pltpu.roll(value, turn, 1))

    def edge_rows(out, line, tile):
        for h in range(sides):
            span = pl.ds(h * LANES, LANES)
            deep = depth[pl.ds(line, 1), span]
            for c in range(2):
                for k in range(count):
                    out[pl.ds(c * count + k, 1), span] = jnp.where(
                        deep > k, tracer[c, k, pl.ds(line, 1), span], 0.0
                    )
            for f, ref in enumerate((depth, surf, flow_x, flow_y, force)):
                out[pl.ds(base + f * SUB, SUB), span] = ref[pl.ds(tile, SUB), span]

    pl.when(step == 0)(lambda: edge_rows(to_previous, 0, 0))
    pl.when(step == steps - 1)(lambda: edge_rows(to_next, rows - 1, rows - SUB))


def column_pass(tracer, land, levels, surf, flow_x, flow_y):
    two, count, rows, cols = tracer.shape
    chunk = rows // 4
    flat = pl.BlockSpec((chunk, cols), lambda i: (i, 0))
    lines = (two * count + FIELDS * SUB, cols)
    strip = (rows // 2 + SUB, LANES)
    plain = jax.ShapeDtypeStruct((rows, cols), F32)
    shapes = [plain, plain] + [jax.ShapeDtypeStruct(s, F32) for s in (strip, strip, lines, lines)]
    return pl.pallas_call(
        column_kernel,
        grid=(rows // chunk,),
        in_specs=[pl.BlockSpec((two, count, chunk, cols), lambda i: (0, 0, i, 0))] + [flat] * 5,
        out_specs=[flat, flat] + [pl.BlockSpec(s.shape, lambda i: (0, 0)) for s in shapes[2:]],
        out_shape=shapes,
        compiler_params=pltpu.CompilerParams(vmem_limit_bytes=VMEM_LIMIT),
        cost_estimate=pl.CostEstimate(
            flops=6 * tracer.size, bytes_accessed=4 * tracer.size, transcendentals=0
        ),
        name="columns",
    )(tracer, land, levels, surf, flow_x, flow_y)


def pack_kernel(south_in, north_in, west, east, south_out, north_out):
    half = south_in.shape[0] - SUB
    sides = west.shape[1] // LANES
    lanes = lane_ids(SUB)
    strips = []
    for ref in (west, east):
        zero = jnp.zeros((SUB, LANES), F32)
        ends = [pl.ds(0, LANES), pl.ds((sides - 1) * LANES, LANES)]
        values = [
            tuple(ref[pl.ds(BASE + f * SUB, SUB), span] for span in ends) for f in range(FIELDS)
        ]
        strips.append(strip_pair(zero, zero, lanes, values))
    for index, (source, out) in enumerate(((south_in, south_out), (north_in, north_out))):
        out[pl.ds(0, half), :] = source[pl.ds(0, half), :]
        out[pl.ds(half, SUB), :] = jnp.where(
            lanes < HALF, strips[0][index], pltpu.roll(strips[1][index], HALF, 1)
        )


def pack_pass(to_south, to_north, west, east):
    shape = jax.ShapeDtypeStruct(to_south.shape, F32)
    return pl.pallas_call(
        pack_kernel,
        out_shape=[shape, shape],
        compiler_params=pltpu.CompilerParams(vmem_limit_bytes=VMEM_LIMIT),
        cost_estimate=pl.CostEstimate(
            flops=to_south.size, bytes_accessed=16 * to_south.size, transcendentals=0
        ),
        name="corners",
    )(to_south, to_north, west, east)


def message_rows(ref, rows, r):
    half = rows // 2
    if r < 0:
        return ref[pl.ds(half, SUB), :]
    if r >= rows:
        return pltpu.roll(ref[pl.ds(half, SUB), :], HALF, 1)
    if r < half:
        return ref[pl.ds(r, SUB), :]
    return pltpu.roll(ref[pl.ds(r - half, SUB), :], HALF, 1)


def outer_tile(south, north, rows, r, f, open_south, open_north, lanes):
    at = BASE + (f + 1) * WIDTH
    mixed = jnp.where(lanes < at, message_rows(south, rows, r), message_rows(north, rows, r))
    mixed = put_lane(mixed, at, 0)
    valid = ((lanes < WIDTH) & open_north) | ((lanes >= LANES - WIDTH) & open_south)
    return jnp.where(valid, mixed, 0.0)


def extend(target, base, f, field, west, east, south, north, open_south, open_north):
    rows, cols = field.shape
    sides = cols // LANES
    lanes = lane_ids(SUB)
    for r in range(-SUB, rows + 1, SUB):
        to = pl.ds(SUB + r, SUB)
        for h in range(sides):
            span = pl.ds(h * LANES, LANES)
            if r < 0:
                target[h, to, :] = west[pl.ds(base + f * SUB, SUB), span]
            elif r >= rows:
                target[h, to, :] = east[pl.ds(base + f * SUB, SUB), span]
            else:
                target[h, to, :] = field[pl.ds(r, SUB), span]
        target[sides, to, :] = outer_tile(
            south, north, rows, r, f, open_south, open_north, lanes
        )


def latitude_ends():
    place, size = lax.axis_index("gy"), lax.axis_size("gy")
    return place > 0, place < size - 1


def ring_shift(tiles, lanes):
    size = len(tiles)
    after = [pltpu.roll(t, LANES - 1, 1) for t in tiles]
    before = [pltpu.roll(t, 1, 1) for t in tiles]
    nxt = [jnp.where(lanes == LANES - 1, after[(h + 1) % size], after[h]) for h in range(size)]
    prv = [jnp.where(lanes == 0, before[(h - 1) % size], before[h]) for h in range(size)]
    return nxt, prv


def nine_sum(ref, r, lanes):
    sides = [ref[h, pl.ds(r + 1, SUB), :] + ref[h, pl.ds(r - 1, SUB), :] for h in range(ref.shape[0])]
    mixed = [ref[h, pl.ds(r, SUB), :] + 0.5 * sides[h] for h in range(ref.shape[0])]
    nxt, prv = ring_shift(mixed, lanes)
    return [sides[h] + (nxt[h] + prv[h]) for h in range(ref.shape[0])]


def peak_kernel(depth, west, east, south, north, peak, coded):
    rows, cols = depth.shape
    sides = cols // LANES
    lanes = lane_ids(SUB)
    open_south, open_north = latitude_ends()
    scale = 2.0 / (BASE // 2)
    extend(coded, BASE, 0, depth, west, east, south, north, open_south, open_north)
    for r in range(0, rows + 2 * SUB, SUB):
        for h in range(sides + 1):
            d = coded[h, pl.ds(r, SUB), :]
            coded[h, pl.ds(r, SUB), :] = d + jnp.where(d > 0, CODE, 0.0)
    best = jnp.full((SUB, LANES), 0.0, F32)
    for r in range(SUB, rows + SUB, SUB):
        sums = nine_sum(coded, r, lanes)
        for h in range(sides):
            wet, deep = decode(sums[h])
            d = depth[pl.ds(r - SUB, SUB), pl.ds(h * LANES, LANES)]
            best = jnp.maximum(best, d * wet + jnp.where(d > 0, deep, 0.0))
    best = jnp.max(jnp.max(best, axis=1, keepdims=True), axis=0, keepdims=True)
    peak[...] = jnp.broadcast_to(0.5 + scale * best, (SUB, LANES))


def decode(sums):
    wet = jnp.floor(sums * (2.0 / CODE)) * 0.5
    return wet, sums - CODE * wet


def peak_pass(depth, west, east, south, north):
    rows, cols = depth.shape
    ext = pltpu.VMEM((cols // LANES + 1, rows + 2 * SUB, LANES), F32)
    return pl.pallas_call(
        peak_kernel,
        out_shape=jax.ShapeDtypeStruct((SUB, LANES), F32),
        scratch_shapes=[ext],
        compiler_params=pltpu.CompilerParams(vmem_limit_bytes=VMEM_LIMIT),
        cost_estimate=pl.CostEstimate(
            flops=30 * depth.size, bytes_accessed=4 * depth.size, transcendentals=0
        ),
        name="peak",
    )(depth, west, east, south, north)


def tracer_kernel(start, tracer, zonal, merid, depth, west, east, south, north, *rest):
    out, edge_y, around, masked = rest[-4:]
    step = pl.program_id(0)
    rows, cols = depth.shape
    sides = cols // LANES
    count = BASE // 2
    level = step + start
    lanes = lane_ids(SUB)
    spans = [pl.ds(h * LANES, LANES) for h in range(sides)]

    @pl.when(step == 0)
    def _():
        open_south, open_north = latitude_ends()
        for h in range(sides):
            masked[0, h, pl.ds(0, SUB), :] = west[pl.ds(BASE, SUB), spans[h]]
            masked[0, h, pl.ds(SUB, rows), :] = depth[:, spans[h]]
            masked[0, h, pl.ds(SUB + rows, SUB), :] = east[pl.ds(BASE, SUB), spans[h]]
        for big in range(0, rows, 2 * SUB):
            shifted = []
            for r in (big, big + SUB):
                low, high = message_rows(south, rows, r), message_rows(north, rows, r)
                edge_y[0, pl.ds(r, SUB), :] = jnp.where(open_south, low, 0.0)
                edge_y[1, pl.ds(r, SUB), :] = jnp.where(
                    open_north, pltpu.roll(high, LANES - 2, 1), 0.0
                )
                tiles = [depth[pl.ds(r, SUB), span] for span in spans]
                tiles.append(
                    outer_tile(south, north, rows, r, 0, open_south, open_north, lanes)
                )
                shifted.append(ring_shift(tiles, lanes))
            at = pl.ds(big, 2 * SUB)
            for h in range(sides):
                around[0, h, at, :] = masked[0, h, pl.ds(SUB + big + 1, 2 * SUB), :].astype(BF16)
                around[1, h, at, :] = masked[0, h, pl.ds(SUB + big - 1, 2 * SUB), :].astype(BF16)
                for n in range(2):
                    pair = jnp.concatenate([shifted[0][n][h], shifted[1][n][h]], 0)
                    around[2 + n, h, at, :] = pair.astype(BF16)

    mark = level.astype(F32)
    for c in range(2):
        line = c * count + level
        group = pl.multiple_of(lax.div(line, SUB) * SUB, SUB)
        place = lax.rem(line, SUB)
        for h in range(sides):
            before = west[pl.ds(group, SUB), spans[h]]
            masked[c, h, pl.ds(0, SUB), :] = pltpu.roll(before, SUB - 1 - place, 0)
            after = east[pl.ds(group, SUB), spans[h]]
            masked[c, h, pl.ds(SUB + rows, SUB), :] = pltpu.roll(after, lax.rem(SUB - place, SUB), 0)
    for r in range(0, rows, SUB):
        for h in range(sides):
            here = depth[pl.ds(r, SUB), spans[h]] > mark
            for c in range(2):
                masked[c, h, pl.ds(SUB + r, SUB), :] = jnp.where(
                    here, tracer[c, 0, pl.ds(r, SUB), spans[h]], 0.0
                )
    mark_pair = jnp.full((2 * SUB, LANES), mark, F32).astype(BF16)
    one, none = jnp.ones((2 * SUB, LANES), BF16), jnp.zeros((2 * SUB, LANES), BF16)
    quarter = jnp.full((2 * SUB, LANES), 0.25, BF16)
    picks = []
    for c in range(2):
        line = c * count + level
        picks.append(((lanes >= line) & (lanes < line + HALF), lax.rem(LANES - line, LANES)))
    for big in range(0, rows, 2 * SUB):
        wide = pl.ds(big, 2 * SUB)
        pairs = []
        for h in range(sides):
            near = none
            for n in range(4):
                near = near + jnp.where(around[n, h, wide, :] > mark_pair, one, none)
            pairs.append(
                (
                    1.0 - 0.2 * near.astype(F32),
                    (zonal[0, wide, spans[h]] * quarter).astype(F32),
                    (merid[0, wide, spans[h]] * quarter).astype(F32),
                )
            )
        for sub in range(2):
            r = big + sub * SUB
            at = pl.ds(r, SUB)
            part = slice(sub * SUB, (sub + 1) * SUB)
            factors = []
            for h in range(sides):
                own, u, v = (value[part] for value in pairs[h])
                here = depth[at, spans[h]] > mark
                factors.append((here, own, 0.2 - u, 0.2 + u, 0.2 - v, 0.2 + v))
            for c in range(2):
                tiles = [masked[c, h, pl.ds(SUB + r, SUB), :] for h in range(sides)]
                pick, turn = picks[c]
                outer = pltpu.roll(jnp.where(pick, edge_y[0, at, :], edge_y[1, at, :]), turn, 1)
                after = [pltpu.roll(t, LANES - 1, 1) for t in tiles] + [outer]
                before = [outer] + [pltpu.roll(t, 1, 1) for t in tiles]
                for h in range(sides):
                    here, own, to_e, to_w, to_n, to_s = factors[h]
                    nxt = jnp.where(lanes == LANES - 1, after[h + 1], after[h])
                    prv = jnp.where(lanes == 0, before[h], before[h + 1])
                    value = own * tiles[h] + to_n * nxt + to_s * prv
                    value = value + to_e * masked[c, h, pl.ds(SUB + r + 1, SUB), :]
                    value = value + to_w * masked[c, h, pl.ds(SUB + r - 1, SUB), :]
                    out[c, 0, at, spans[h]] = jnp.where(
                        here, value, tracer[c, 0, at, spans[h]]
                    )


def tracer_pass(start, stop, tracer, zonal, merid, depth, west, east, south, north, into=None):
    two, count, rows, cols = tracer.shape
    sides = cols // LANES
    block = pl.BlockSpec((two, 1, rows, cols), lambda k: (0, k + start, 0, 0))
    speed = pl.BlockSpec((1, rows, cols), lambda k: (k + start, 0, 0))

    def fixed(value):
        return pl.BlockSpec(value.shape, lambda k: (0, 0))

    small = [depth, west, east, south, north]
    operands = [tracer, zonal, merid, *small]
    specs = [block, speed, speed] + [fixed(v) for v in small]
    aliases = {}
    if into is not None:
        aliases = {len(operands): 0}
        operands.append(into)
        specs.append(pl.BlockSpec(memory_space=pl.ANY))
    part = stop - start
    return pl.pallas_call(
        functools.partial(tracer_kernel, start),
        grid=(part,),
        in_specs=specs,
        out_specs=block,
        out_shape=jax.ShapeDtypeStruct(tracer.shape, F32),
        scratch_shapes=[
            pltpu.VMEM((2, rows, LANES), F32),
            pltpu.VMEM((4, sides, rows, LANES), BF16),
            pltpu.VMEM((2, sides, rows + 2 * SUB, LANES), F32),
        ],
        input_output_aliases=aliases,
        compiler_params=pltpu.CompilerParams(vmem_limit_bytes=VMEM_LIMIT),
        cost_estimate=pl.CostEstimate(
            flops=40 * tracer.size * part // count,
            bytes_accessed=10 * tracer.size * part // count,
            transcendentals=0,
        ),
        name="tracers",
    )(*operands)


def solve_kernel(
    peak, depth, surf, flow_x, flow_y, force, west, east, south, north,
    surf_out, x_out, y_out, deep, wet, surf0, flux_x, flux_y, forced, left, right, start, step_by, total,
):
    rows, cols = depth.shape
    sides = cols // LANES
    tiles = sides + 1
    lanes = lane_ids(SUB)
    open_south, open_north = latitude_ends()
    halo = (west, east, south, north, open_south, open_north)
    base = BASE
    scale = 1.0 / (base // 2)
    extend(deep, base, 0, depth, *halo)
    extend(surf0, base, 1, surf, *halo)
    extend(flux_x, base, 2, flow_x, *halo)
    extend(flux_y, base, 3, flow_y, *halo)
    extend(forced, base, 4, force, *halo)
    every = range(0, rows + 2 * SUB, SUB)
    inner = range(SUB, rows + SUB, SUB)

    for r in every:
        at = pl.ds(r, SUB)
        for h in range(tiles):
            d = deep[h, at, :] * scale
            m = jnp.where(d > 0, 1.0, 0.0)
            deep[h, at, :] = d
            wet[h, at, :] = m
            flux_x[h, at, :] = m * flux_x[h, at, :]
            flux_y[h, at, :] = m * flux_y[h, at, :]
            total[h, at, :] = m * surf0[h, at, :]
            step_by[h, at, :] = d * surf0[h, at, :]

    def clamp_rows(r):
        return min(max(r, 1), rows + 2 * SUB - SUB - 1)

    spans = [clamp_rows(r) for r in every]
    for r in spans:
        at = pl.ds(r, SUB)
        sum_wet = nine_sum(wet, r, lanes)
        sum_deep = nine_sum(deep, r, lanes)
        sum_f = nine_sum(total, r, lanes)
        sum_g = nine_sum(step_by, r, lanes)
        nxt, prv = ring_shift([flux_y[h, at, :] for h in range(tiles)], lanes)
        for h in range(tiles):
            d = deep[h, at, :]
            m = wet[h, at, :]
            inverse = 1.0 / (0.5 + 2.0 * (d * sum_wet[h] + m * sum_deep[h]))
            a = 2.0 * d * inverse
            b = 2.0 * m * inverse
            left[h, at, :] = a
            right[h, at, :] = b
            e = surf0[h, at, :]
            div = 0.5 * (
                flux_x[h, pl.ds(r + 1, SUB), :] - flux_x[h, pl.ds(r - 1, SUB), :]
            ) + 0.5 * (nxt[h] - prv[h])
            rhs = 0.5 * e + forced[h, at, :] - 0.5 * div
            start[h, at, :] = rhs * inverse - e + a * sum_f[h] + b * sum_g[h]

    top = peak[...]
    lowest = 0.5 / top
    shrink = (1.0 - lowest) * (1.0 - lowest)
    omega = jnp.full((SUB, LANES), 2.0, F32)
    for r in every:
        at = pl.ds(r, SUB)
        for h in range(tiles):
            z = start[h, at, :]
            total[h, at, :] = z
            step_by[h, at, :] = z
            flux_x[h, at, :] = wet[h, at, :] * z
            flux_y[h, at, :] = deep[h, at, :] * z
    for turn in range(1, ITERS):
        omega = 1.0 / (1.0 - omega * shrink * 0.25)
        for r in spans:
            at = pl.ds(r, SUB)
            sum_f = nine_sum(flux_x, r, lanes)
            sum_g = nine_sum(flux_y, r, lanes)
            for h in range(tiles):
                s = total[h, at, :]
                y = start[h, at, :] - s + left[h, at, :] * sum_f[h] + right[h, at, :] * sum_g[h]
                delta = omega * y + (omega - 1.0) * step_by[h, at, :]
                forced[h, at, :] = delta
        for r in every:
            at = pl.ds(r, SUB)
            for h in range(tiles):
                delta = forced[h, at, :]
                s = total[h, at, :] + delta
                total[h, at, :] = s
                step_by[h, at, :] = delta
                flux_x[h, at, :] = wet[h, at, :] * s
                flux_y[h, at, :] = deep[h, at, :] * s

    for r in every:
        at = pl.ds(r, SUB)
        for h in range(tiles):
            value = surf0[h, at, :] + total[h, at, :]
            if h == sides:
                value = jnp.where((lanes < WIDTH) & open_north, value, jnp.where(
                    (lanes >= LANES - WIDTH) & open_south, value, 0.0))
            total[h, at, :] = value
    for r in inner:
        at = pl.ds(r, SUB)
        back = pl.ds(r - SUB, SUB)
        nxt, prv = ring_shift([total[h, at, :] for h in range(tiles)], lanes)
        for h in range(sides):
            span = pl.ds(h * LANES, LANES)
            m = wet[h, at, :]
            surf_out[back, span] = total[h, at, :]
            slope = total[h, pl.ds(r + 1, SUB), :] - total[h, pl.ds(r - 1, SUB), :]
            x_out[back, span] = m * (flow_x[back, span] - 0.25 * slope)
            y_out[back, span] = m * (flow_y[back, span] - 0.25 * (nxt[h] - prv[h]))


def solve_pass(peak, depth, surf, flow_x, flow_y, force, west, east, south, north):
    rows, cols = depth.shape
    ext = pltpu.VMEM((cols // LANES + 1, rows + 2 * SUB, LANES), F32)
    shape = jax.ShapeDtypeStruct((rows, cols), F32)
    return pl.pallas_call(
        solve_kernel,
        out_shape=[shape] * 3,
        scratch_shapes=[ext] * 11,
        compiler_params=pltpu.CompilerParams(vmem_limit_bytes=VMEM_LIMIT),
        cost_estimate=pl.CostEstimate(
            flops=200 * depth.size, bytes_accessed=32 * depth.size, transcendentals=0
        ),
        name="solve",
    )(peak, depth, surf, flow_x, flow_y, force, west, east, south, north)


def both_ways(axis, to_next, to_previous):
    size = lax.axis_size(axis)
    up = [(i, (i + 1) % size) for i in range(size)]
    down = [(j, i) for i, j in up]
    return lax.ppermute(to_next, axis, up), lax.ppermute(to_previous, axis, down)


def spread_rounds(axis):
    size = lax.axis_size(axis)
    reach = 1
    while reach < size:
        if size & (size - 1) == 0:
            yield axis, [(i, i ^ reach) for i in range(size)]
        else:
            yield axis, [(i, (i + reach) % size) for i in range(size)]
        reach *= 2


def local(
    tracer, zonal_flow, meridional_flow, surface_prev, transport_x, transport_y, land_mask, levels
):
    count = tracer.shape[1]
    force, depth, to_south, to_north, to_previous, to_next = column_pass(
        tracer, land_mask, levels, surface_prev, transport_x, transport_y
    )
    fields = (depth, surface_prev, transport_x, transport_y, force)
    west, east = both_ways("gx", to_next, to_previous)
    to_south, to_north = pack_pass(to_south, to_north, west, east)
    south, north = both_ways("gy", to_north, to_south)
    halo = (west, east, south, north)
    peak = peak_pass(depth, *halo)
    tracer_next = None
    rounds = [r for axis in ("gx", "gy") for r in spread_rounds(axis)]
    cuts = [count * i // PARTS for i in range(PARTS + 1)]
    first = len(rounds) - PARTS
    for turn, (axis, pairs) in enumerate(rounds):
        moved = lax.ppermute(peak, axis, pairs)
        if turn >= first:
            part = turn - first
            tracer_next = tracer_pass(
                cuts[part], cuts[part + 1], tracer, zonal_flow, meridional_flow, depth, *halo,
                into=tracer_next,
            )
        peak = jnp.maximum(peak, moved)
        if first <= turn < len(rounds) - 1:
            peak, tracer_next = lax.optimization_barrier((peak, tracer_next))
    surf, next_x, next_y = solve_pass(peak, *fields, *halo)
    return (tracer_next, surf, next_x, next_y)


def solution(mesh):
    cell = P("gx", "gy")
    level = P(None, "gx", "gy")
    stack = P(None, None, "gx", "gy")
    return jax.shard_map(
        local,
        mesh=mesh,
        in_specs=(stack, level, level, cell, cell, cell, cell, cell),
        out_specs=(stack, cell, cell, cell),
        check_vma=False,
    )
```

```python
import functools

import jax
import jax.numpy as jnp
from jax import lax
from jax.experimental import pallas as pl
from jax.experimental.pallas import tpu as pltpu
from jax.sharding import PartitionSpec as P

ITERS = 4
WIDTH = ITERS + 1
LANES = 128
SUB = 8
HALF = LANES // 2
FIELDS = 5
F32 = jnp.float32
BF16 = jnp.bfloat16
VMEM_LIMIT = 12 * 1024 * 1024
LEVELS = 16
BASE = 2 * LEVELS
CODE = 1024.0
PARTS = 4
CHUNKS = 4


def lane_ids(rows):
    return lax.broadcasted_iota(jnp.int32, (rows, LANES), 1)


def put_lane(value, source, target):
    shift = (target - source) % LANES
    return pltpu.roll(value, shift, 1) if shift else value


def strip_pair(low, high, lanes, values):
    for f, (begin, end) in enumerate(values):
        at = BASE + (f + 1) * WIDTH
        turned = put_lane(jnp.where(lanes < HALF, begin, end), 0, at)
        low = jnp.where((lanes >= at) & (lanes < at + WIDTH), turned, low)
        high = jnp.where((lanes >= at - WIDTH) & (lanes < at), turned, high)
    return low, high


def column_kernel(
    tracer_hbm, land_hbm, levels_hbm, surf_hbm, flow_x_hbm, flow_y_hbm,
    force, depth, to_south, to_north, to_previous, to_next, tracer, surf, flow_x, flow_y,
    land, levels, flat_sem, chunk_sem,
):
    count = tracer.shape[1]
    rows, cols = land.shape
    sides = cols // LANES
    base = 2 * count
    lanes = lane_ids(SUB)
    size = rows // CHUNKS

    def copy_in(i):
        part = pl.ds(pl.multiple_of(i * size, SUB), size)
        return pltpu.make_async_copy(
            tracer_hbm.at[:, :, part, :], tracer.at[:, :, part, :], chunk_sem.at[i]
        )

    flats = [
        pltpu.make_async_copy(source, target, flat_sem.at[i])
        for i, (source, target) in enumerate(
            (
                (land_hbm, land),
                (levels_hbm, levels),
                (surf_hbm, surf),
                (flow_x_hbm, flow_x),
                (flow_y_hbm, flow_y),
            )
        )
    ]
    for copy in flats:
        copy.start()
    for i in range(CHUNKS):
        copy_in(i).start()
    low_kind = jnp.where((lanes >= 1) & (lanes <= base), lax.rem(lanes - 1 + count, count), -1)
    low_kind = low_kind.astype(F32)
    high_kind = jnp.where(lanes < base, lax.rem(lanes, count), -1).astype(F32)
    odd = (lanes & 1) == 1
    ends = [pl.ds(0, LANES), pl.ds((sides - 1) * LANES, LANES)]
    for copy in flats:
        copy.wait()

    def chunk(i, carry):
        copy_in(i).wait()
        upper = i >= CHUNKS // 2
        turn = jnp.where(upper, HALF, 0)
        keep = (lanes < HALF) & upper
        first_row = jnp.where(upper, i - CHUNKS // 2, i) * size
        for r in range(0, size, SUB):
            at = pl.ds(pl.multiple_of(i * size + r, SUB), SUB)
            packed = [jnp.zeros((SUB, LANES), F32)] * 2
            totals = [jnp.zeros((SUB, LANES), F32)] * sides
            deeps = []
            for h in range(sides):
                span = pl.ds(h * LANES, LANES)
                deeps.append((land[at, span] * levels[at, span]).astype(F32))
            for k in range(count):
                values = [
                    [tracer[c, k, at, pl.ds(h * LANES, LANES)] for h in range(sides)]
                    for c in range(2)
                ]
                for h in range(sides):
                    gain = jnp.maximum(deeps[h] - k, 0.0)
                    totals[h] = totals[h] + gain * (values[0][h] - 0.75 * values[1][h])
                for c in range(2):
                    line = c * count + k
                    both = jnp.where(lanes < HALF, values[c][0], values[c][-1])
                    both = put_lane(both, 0, line + 1)
                    packed[line % 2] = jnp.where(
                        (lanes == line) | (lanes == line + 1), both, packed[line % 2]
                    )
            totals = [t * (0.8 / count) for t in totals]
            for h in range(sides):
                span = pl.ds(h * LANES, LANES)
                force[at, span] = totals[h]
                depth[at, span] = deeps[h]
            low = jnp.where(odd, packed[0], packed[1])
            high = jnp.where(odd, packed[1], packed[0])
            low = jnp.where(deeps[0][:, 0:1] > low_kind, low, 0.0)
            high = jnp.where(deeps[-1][:, LANES - 1 : LANES] > high_kind, high, 0.0)
            low, high = strip_pair(
                low,
                high,
                lanes,
                [(deeps[0], deeps[-1])]
                + [tuple(ref[at, span] for span in ends) for ref in (surf, flow_x, flow_y)]
                + [(totals[0], totals[-1])],
            )
            to = pl.ds(pl.multiple_of(first_row + r, SUB), SUB)
            for out, value in ((to_south, low), (to_north, high)):
                out[to, :] = jnp.where(keep, out[to, :], pltpu.roll(value, turn, 1))
        return carry

    lax.fori_loop(0, CHUNKS, chunk, 0)
    for out, line, tile in ((to_previous, 0, 0), (to_next, rows - 1, rows - SUB)):
        for h in range(sides):
            span = pl.ds(h * LANES, LANES)
            deep = depth[pl.ds(line, 1), span]
            for c in range(2):
                for k in range(count):
                    out[pl.ds(c * count + k, 1), span] = jnp.where(
                        deep > k, tracer[c, k, pl.ds(line, 1), span], 0.0
                    )
            for f, ref in enumerate((depth, surf, flow_x, flow_y, force)):
                out[pl.ds(base + f * SUB, SUB), span] = ref[pl.ds(tile, SUB), span]


IN_HBM = pl.BlockSpec(memory_space=pltpu.HBM)
IN_VMEM = pl.BlockSpec(memory_space=pltpu.VMEM)


def column_pass(tracer, land, levels, surf, flow_x, flow_y):
    two, count, rows, cols = tracer.shape
    lines = (two * count + FIELDS * SUB, cols)
    strip = (rows // 2 + SUB, LANES)
    plain = (rows, cols)
    shapes = [plain, plain, strip, strip, lines, lines, tracer.shape, plain, plain, plain]
    return pl.pallas_call(
        column_kernel,
        in_specs=[IN_HBM] * 6,
        out_specs=[IN_VMEM] * len(shapes),
        out_shape=[jax.ShapeDtypeStruct(shape, F32) for shape in shapes],
        scratch_shapes=[
            pltpu.VMEM(plain, jnp.int32),
            pltpu.VMEM(plain, jnp.int32),
            pltpu.SemaphoreType.DMA((5,)),
            pltpu.SemaphoreType.DMA((CHUNKS,)),
        ],
        compiler_params=pltpu.CompilerParams(vmem_limit_bytes=VMEM_LIMIT),
        cost_estimate=pl.CostEstimate(
            flops=6 * tracer.size, bytes_accessed=4 * tracer.size, transcendentals=0
        ),
        name="columns",
    )(
        *(
            pltpu.with_memory_space_constraint(value, pltpu.HBM)
            for value in (tracer, land, levels, surf, flow_x, flow_y)
        )
    )


def pack_kernel(south_in, north_in, west, east, south_out, north_out):
    half = south_in.shape[0] - SUB
    sides = west.shape[1] // LANES
    lanes = lane_ids(SUB)
    strips = []
    for ref in (west, east):
        zero = jnp.zeros((SUB, LANES), F32)
        ends = [pl.ds(0, LANES), pl.ds((sides - 1) * LANES, LANES)]
        values = [
            tuple(ref[pl.ds(BASE + f * SUB, SUB), span] for span in ends) for f in range(FIELDS)
        ]
        strips.append(strip_pair(zero, zero, lanes, values))
    for index, (source, out) in enumerate(((south_in, south_out), (north_in, north_out))):
        out[pl.ds(0, half), :] = source[pl.ds(0, half), :]
        out[pl.ds(half, SUB), :] = jnp.where(
            lanes < HALF, strips[0][index], pltpu.roll(strips[1][index], HALF, 1)
        )


def pack_pass(to_south, to_north, west, east):
    shape = jax.ShapeDtypeStruct(to_south.shape, F32)
    return pl.pallas_call(
        pack_kernel,
        out_shape=[shape, shape],
        compiler_params=pltpu.CompilerParams(vmem_limit_bytes=VMEM_LIMIT),
        cost_estimate=pl.CostEstimate(
            flops=to_south.size, bytes_accessed=16 * to_south.size, transcendentals=0
        ),
        name="corners",
    )(to_south, to_north, west, east)


def message_rows(ref, rows, r):
    half = rows // 2
    if r < 0:
        return ref[pl.ds(half, SUB), :]
    if r >= rows:
        return pltpu.roll(ref[pl.ds(half, SUB), :], HALF, 1)
    if r < half:
        return ref[pl.ds(r, SUB), :]
    return pltpu.roll(ref[pl.ds(r - half, SUB), :], HALF, 1)


def outer_tile(south, north, rows, r, f, open_south, open_north, lanes):
    at = BASE + (f + 1) * WIDTH
    mixed = jnp.where(lanes < at, message_rows(south, rows, r), message_rows(north, rows, r))
    mixed = put_lane(mixed, at, 0)
    valid = ((lanes < WIDTH) & open_north) | ((lanes >= LANES - WIDTH) & open_south)
    return jnp.where(valid, mixed, 0.0)


def extend(target, base, f, field, west, east, south, north, open_south, open_north):
    rows, cols = field.shape
    sides = cols // LANES
    lanes = lane_ids(SUB)
    for r in range(-SUB, rows + 1, SUB):
        to = pl.ds(SUB + r, SUB)
        for h in range(sides):
            span = pl.ds(h * LANES, LANES)
            if r < 0:
                target[h, to, :] = west[pl.ds(base + f * SUB, SUB), span]
            elif r >= rows:
                target[h, to, :] = east[pl.ds(base + f * SUB, SUB), span]
            else:
                target[h, to, :] = field[pl.ds(r, SUB), span]
        target[sides, to, :] = outer_tile(
            south, north, rows, r, f, open_south, open_north, lanes
        )


def latitude_ends():
    place, size = lax.axis_index("gy"), lax.axis_size("gy")
    return place > 0, place < size - 1


def ring_shift(tiles, lanes):
    size = len(tiles)
    after = [pltpu.roll(t, LANES - 1, 1) for t in tiles]
    before = [pltpu.roll(t, 1, 1) for t in tiles]
    nxt = [jnp.where(lanes == LANES - 1, after[(h + 1) % size], after[h]) for h in range(size)]
    prv = [jnp.where(lanes == 0, before[(h - 1) % size], before[h]) for h in range(size)]
    return nxt, prv


def nine_sum(ref, r, lanes):
    sides = [ref[h, pl.ds(r + 1, SUB), :] + ref[h, pl.ds(r - 1, SUB), :] for h in range(ref.shape[0])]
    mixed = [ref[h, pl.ds(r, SUB), :] + 0.5 * sides[h] for h in range(ref.shape[0])]
    nxt, prv = ring_shift(mixed, lanes)
    return [sides[h] + (nxt[h] + prv[h]) for h in range(ref.shape[0])]


def peak_kernel(depth, west, east, south, north, peak, coded):
    rows, cols = depth.shape
    sides = cols // LANES
    lanes = lane_ids(SUB)
    open_south, open_north = latitude_ends()
    scale = 2.0 / (BASE // 2)
    extend(coded, BASE, 0, depth, west, east, south, north, open_south, open_north)
    for r in range(0, rows + 2 * SUB, SUB):
        for h in range(sides + 1):
            d = coded[h, pl.ds(r, SUB), :]
            coded[h, pl.ds(r, SUB), :] = d + jnp.where(d > 0, CODE, 0.0)
    best = jnp.full((SUB, LANES), 0.0, F32)
    for r in range(SUB, rows + SUB, SUB):
        sums = nine_sum(coded, r, lanes)
        for h in range(sides):
            wet, deep = decode(sums[h])
            d = depth[pl.ds(r - SUB, SUB), pl.ds(h * LANES, LANES)]
            best = jnp.maximum(best, d * wet + jnp.where(d > 0, deep, 0.0))
    best = jnp.max(jnp.max(best, axis=1, keepdims=True), axis=0, keepdims=True)
    peak[...] = jnp.broadcast_to(0.5 + scale * best, (SUB, LANES))


def decode(sums):
    wet = jnp.floor(sums * (2.0 / CODE)) * 0.5
    return wet, sums - CODE * wet


def peak_pass(depth, west, east, south, north):
    rows, cols = depth.shape
    ext = pltpu.VMEM((cols // LANES + 1, rows + 2 * SUB, LANES), F32)
    return pl.pallas_call(
        peak_kernel,
        out_shape=jax.ShapeDtypeStruct((SUB, LANES), F32),
        scratch_shapes=[ext],
        compiler_params=pltpu.CompilerParams(vmem_limit_bytes=VMEM_LIMIT),
        cost_estimate=pl.CostEstimate(
            flops=30 * depth.size, bytes_accessed=4 * depth.size, transcendentals=0
        ),
        name="peak",
    )(depth, west, east, south, north)


def tracer_kernel(start, stop, tracer, zonal, merid, depth, west, east, south, north, *rest):
    out, edge_y, around, masked = rest[-4:]
    rows, cols = depth.shape
    sides = cols // LANES
    count = BASE // 2
    lanes = lane_ids(SUB)
    spans = [pl.ds(h * LANES, LANES) for h in range(sides)]

    if start == 0:
        open_south, open_north = latitude_ends()
        for h in range(sides):
            masked[0, h, pl.ds(0, SUB), :] = west[pl.ds(BASE, SUB), spans[h]]
            masked[0, h, pl.ds(SUB, rows), :] = depth[:, spans[h]]
            masked[0, h, pl.ds(SUB + rows, SUB), :] = east[pl.ds(BASE, SUB), spans[h]]
        for big in range(0, rows, 2 * SUB):
            shifted = []
            for r in (big, big + SUB):
                low, high = message_rows(south, rows, r), message_rows(north, rows, r)
                edge_y[0, pl.ds(r, SUB), :] = jnp.where(open_south, low, 0.0)
                edge_y[1, pl.ds(r, SUB), :] = jnp.where(
                    open_north, pltpu.roll(high, LANES - 2, 1), 0.0
                )
                tiles = [depth[pl.ds(r, SUB), span] for span in spans]
                tiles.append(
                    outer_tile(south, north, rows, r, 0, open_south, open_north, lanes)
                )
                shifted.append(ring_shift(tiles, lanes))
            at = pl.ds(big, 2 * SUB)
            for h in range(sides):
                around[0, h, at, :] = masked[0, h, pl.ds(SUB + big + 1, 2 * SUB), :].astype(BF16)
                around[1, h, at, :] = masked[0, h, pl.ds(SUB + big - 1, 2 * SUB), :].astype(BF16)
                for n in range(2):
                    pair = jnp.concatenate([shifted[0][n][h], shifted[1][n][h]], 0)
                    around[2 + n, h, at, :] = pair.astype(BF16)

    def one_level(level, carry):
        mark = lax.convert_element_type(level, F32)
        for c in range(2):
            line = c * count + level
            group = pl.multiple_of(lax.div(line, SUB) * SUB, SUB)
            place = lax.rem(line, SUB)
            for h in range(sides):
                before = west[pl.ds(group, SUB), spans[h]]
                masked[c, h, pl.ds(0, SUB), :] = pltpu.roll(before, SUB - 1 - place, 0)
                after = east[pl.ds(group, SUB), spans[h]]
                masked[c, h, pl.ds(SUB + rows, SUB), :] = pltpu.roll(after, lax.rem(SUB - place, SUB), 0)
        for r in range(0, rows, SUB):
            for h in range(sides):
                here = depth[pl.ds(r, SUB), spans[h]] > mark
                for c in range(2):
                    masked[c, h, pl.ds(SUB + r, SUB), :] = jnp.where(
                        here, tracer[c, level, pl.ds(r, SUB), spans[h]], 0.0
                    )
        mark_pair = jnp.full((2 * SUB, LANES), mark, F32).astype(BF16)
        one, none = jnp.ones((2 * SUB, LANES), BF16), jnp.zeros((2 * SUB, LANES), BF16)
        quarter = jnp.full((2 * SUB, LANES), 0.25, BF16)
        picks = []
        for c in range(2):
            line = c * count + level
            picks.append(((lanes >= line) & (lanes < line + HALF), lax.rem(LANES - line, LANES)))
        for big in range(0, rows, 2 * SUB):
            wide = pl.ds(big, 2 * SUB)
            pairs = []
            for h in range(sides):
                near = none
                for n in range(4):
                    near = near + jnp.where(around[n, h, wide, :] > mark_pair, one, none)
                pairs.append(
                    (
                        1.0 - 0.2 * near.astype(F32),
                        (zonal[level, wide, spans[h]] * quarter).astype(F32),
                        (merid[level, wide, spans[h]] * quarter).astype(F32),
                    )
                )
            for sub in range(2):
                r = big + sub * SUB
                at = pl.ds(r, SUB)
                part = slice(sub * SUB, (sub + 1) * SUB)
                factors = []
                for h in range(sides):
                    own, u, v = (value[part] for value in pairs[h])
                    here = depth[at, spans[h]] > mark
                    factors.append((here, own, 0.2 - u, 0.2 + u, 0.2 - v, 0.2 + v))
                for c in range(2):
                    tiles = [masked[c, h, pl.ds(SUB + r, SUB), :] for h in range(sides)]
                    pick, turn = picks[c]
                    outer = pltpu.roll(jnp.where(pick, edge_y[0, at, :], edge_y[1, at, :]), turn, 1)
                    after = [pltpu.roll(t, LANES - 1, 1) for t in tiles] + [outer]
                    before = [outer] + [pltpu.roll(t, 1, 1) for t in tiles]
                    for h in range(sides):
                        here, own, to_e, to_w, to_n, to_s = factors[h]
                        nxt = jnp.where(lanes == LANES - 1, after[h + 1], after[h])
                        prv = jnp.where(lanes == 0, before[h], before[h + 1])
                        value = own * tiles[h] + to_n * nxt + to_s * prv
                        value = value + to_e * masked[c, h, pl.ds(SUB + r + 1, SUB), :]
                        value = value + to_w * masked[c, h, pl.ds(SUB + r - 1, SUB), :]
                        out[c, level, at, spans[h]] = jnp.where(
                            here, value, tracer[c, level, at, spans[h]]
                        )
        return carry

    lax.fori_loop(start, stop, one_level, 0)


def tracer_pass(start, stop, tracer, zonal, merid, depth, west, east, south, north, before=()):
    two, count, rows, cols = tracer.shape
    sides = cols // LANES
    operands = [tracer, zonal, merid, depth, west, east, south, north, *before]
    first = len(operands) - len(before)
    shapes = [
        jax.ShapeDtypeStruct(tracer.shape, F32),
        jax.ShapeDtypeStruct((2, rows, LANES), F32),
        jax.ShapeDtypeStruct((4, sides, rows, LANES), BF16),
    ]
    part = stop - start
    return pl.pallas_call(
        functools.partial(tracer_kernel, start, stop),
        in_specs=[IN_VMEM] * len(operands),
        out_specs=[IN_VMEM] * 3,
        out_shape=shapes,
        scratch_shapes=[pltpu.VMEM((2, sides, rows + 2 * SUB, LANES), F32)],
        input_output_aliases={first + i: i for i in range(len(before))},
        compiler_params=pltpu.CompilerParams(vmem_limit_bytes=VMEM_LIMIT),
        cost_estimate=pl.CostEstimate(
            flops=40 * tracer.size * part // count,
            bytes_accessed=10 * tracer.size * part // count,
            transcendentals=0,
        ),
        name="tracers",
    )(*operands)


def group_of(tiles):
    return max(n for n in range(1, 8) if tiles % n == 0)


def solve_kernel(
    tracer_in, peak, depth, surf, flow_x, flow_y, force, west, east, south, north,
    tracer_hbm, surf_out, x_out, y_out,
    old, deep, deep_n, deep_s, coded, flux, part, ease, pairs, now, then, total, sem,
):
    rows, cols = depth.shape
    sides = cols // LANES
    tiles = sides + 1
    lanes = lane_ids(SUB)
    scale = 2.0 / BASE
    open_south, open_north = latitude_ends()
    beyond = ((lanes < WIDTH) & open_north) | ((lanes >= LANES - WIDTH) & open_south)
    outward = pltpu.make_async_copy(tracer_in, tracer_hbm, sem)
    outward.start()

    lowest = 0.5 / peak[...]
    shrink = (1.0 - lowest) * (1.0 - lowest)
    omega = jnp.full((SUB, LANES), 2.0, F32)
    weights, change = [jnp.ones((SUB, LANES), F32)], [jnp.ones((SUB, LANES), F32)]
    for _ in range(1, ITERS):
        omega = 1.0 / (1.0 - omega * shrink * 0.25)
        resid = [1.0 - weights[0]] + [p - w for p, w in zip(weights, weights[1:])] + [weights[-1]]
        held = change + [jnp.zeros((SUB, LANES), F32)]
        change = [omega * y + (omega - 1.0) * d for y, d in zip(resid, held)]
        weights = [w + d for w, d in zip(weights + [jnp.zeros((SUB, LANES), F32)], change)]

    edge = (pl.ds(0, SUB), pl.ds(rows + 3 * SUB, SUB))
    for ref in (deep, deep_n, deep_s, coded, flux):
        for at in edge:
            for h in range(tiles):
                ref[h, at, :] = jnp.zeros((SUB, LANES), F32)
    for ref in (pairs, now, then):
        for i in range(ref.shape[0]):
            for at in edge:
                for h in range(tiles):
                    ref[i, h, at, :] = jnp.zeros((SUB, LANES), F32)

    def spread(ref, at, values):
        nxt, prv = ring_shift(values, lanes)
        for h in range(tiles):
            ref[0, h, at, :] = values[h]
            ref[1, h, at, :] = nxt[h]
            ref[2, h, at, :] = prv[h]

    def load_tile(to, field, low, high):
        def ring(f):
            at = BASE + (f + 1) * WIDTH
            outer = put_lane(jnp.where(lanes < at, low, high), at, 0)
            return [field(f, h) for h in range(sides)] + [jnp.where(beyond, outer, 0.0)]

        levels = ring(0)
        deeps = [v * scale for v in levels]
        wets = [jnp.where(v > 0, 1.0, 0.0) for v in levels]
        nxt, prv = ring_shift(deeps, lanes)
        surfs, drives = ring(1), ring(4)
        cross, crosses = ring_shift([m * v for m, v in zip(wets, ring(3))], lanes)
        along = ring(2)
        for h in range(tiles):
            deep[h, to, :] = deeps[h]
            deep_n[h, to, :] = nxt[h]
            deep_s[h, to, :] = prv[h]
            coded[h, to, :] = levels[h] + CODE * wets[h]
            old[h, to, :] = surfs[h]
            flux[h, to, :] = wets[h] * along[h]
            part[h, to, :] = 0.5 * surfs[h] + drives[h] - 0.25 * (cross[h] - crosses[h])
        spread(now, to, [m * v for m, v in zip(wets, surfs)])

    fields = (depth, surf, flow_x, flow_y, force)
    half = rows // 2
    for ref, to, turn in ((west, SUB, 0), (east, rows + 2 * SUB, HALF)):
        tail = [message[pl.ds(half, SUB), :] for message in (south, north)]
        if turn:
            tail = [pltpu.roll(v, turn, 1) for v in tail]
        load_tile(
            pl.ds(to, SUB),
            lambda f, h, ref=ref: ref[pl.ds(BASE + f * SUB, SUB), pl.ds(h * LANES, LANES)],
            *tail,
        )
    size = rows // CHUNKS

    def load_chunk(i, carry):
        upper = i >= CHUNKS // 2
        turn = jnp.where(upper, HALF, 0)
        first_row = jnp.where(upper, i - CHUNKS // 2, i) * size
        for r in range(0, size, SUB):
            at = pl.ds(pl.multiple_of(i * size + r, SUB), SUB)
            line = pl.ds(pl.multiple_of(first_row + r, SUB), SUB)
            load_tile(
                pl.ds(pl.multiple_of(i * size + r + 2 * SUB, SUB), SUB),
                lambda f, h, at=at: fields[f][at, pl.ds(h * LANES, LANES)],
                *(pltpu.roll(message[line, :], turn, 1) for message in (south, north)),
            )
        return carry

    lax.fori_loop(0, CHUNKS, load_chunk, 0)

    count = rows // SUB + 2
    group = group_of(count)

    def over_tiles(body):
        def step(i, carry):
            window = pl.ds(pl.multiple_of(i * (group * SUB), SUB), (group + 2) * SUB)

            def view(ref, *index):
                return ref.at[(*index, window, slice(None))]

            for j in range(SUB, (group + 1) * SUB, SUB):
                body(view, j)
            return carry

        lax.fori_loop(0, count // group, step, 0)

    def nine(view, source, j, near, far):
        result = []
        for h in range(tiles):
            def value(i, shift):
                return view(source, i, h)[pl.ds(j + shift, SUB), :]

            side = near[h][0] * value(0, 1) + near[h][1] * value(0, -1)
            side = side + near[h][2] * value(1, 0) + near[h][3] * value(2, 0)
            corner = far[h][0] * value(1, 1) + far[h][1] * value(1, -1)
            corner = corner + far[h][2] * value(2, 1) + far[h][3] * value(2, -1)
            result.append(side + corner)
        return result

    def prepare(view, j):
        mixed, sides_of = [], []
        for h in range(tiles):
            code = view(coded, h)
            sides_of.append(code[pl.ds(j + 1, SUB), :] + code[pl.ds(j - 1, SUB), :])
            mixed.append(code[pl.ds(j, SUB), :] + 0.5 * sides_of[h])
        nxt, prv = ring_shift(mixed, lanes)
        near, far, inverses, masks = [], [], [], []
        for h in range(tiles):
            own = view(deep, h)[pl.ds(j, SUB), :]
            wet_sum, deep_sum = decode(sides_of[h] + (nxt[h] + prv[h]))
            wet = jnp.where(own > 0, 1.0, 0.0)
            diag = 0.5 + 2.0 * (own * wet_sum + wet * (deep_sum * scale))
            inverse = 1.0 / diag
            inverses.append(inverse)
            masks.append(wet)
            ease_h = wet * inverse
            view(ease, h)[pl.ds(j, SUB), :] = ease_h
            twice = own + own
            e = twice + 2.0 * view(deep, h)[pl.ds(j + 1, SUB), :]
            w = twice + 2.0 * view(deep, h)[pl.ds(j - 1, SUB), :]
            n = twice + 2.0 * view(deep_n, h)[pl.ds(j, SUB), :]
            s = twice + 2.0 * view(deep_s, h)[pl.ds(j, SUB), :]
            ne = own + view(deep_n, h)[pl.ds(j + 1, SUB), :]
            nw = own + view(deep_n, h)[pl.ds(j - 1, SUB), :]
            se = own + view(deep_s, h)[pl.ds(j + 1, SUB), :]
            sw = own + view(deep_s, h)[pl.ds(j - 1, SUB), :]
            for i, value in enumerate((e, n, s, ne, nw, se, sw)):
                view(pairs, i, h)[pl.ds(j, SUB), :] = value
            near.append((e, w, n, s))
            far.append((ne, nw, se, sw))
        sums = nine(view, now, j, near, far)
        firsts = []
        for h in range(tiles):
            e = view(old, h)[pl.ds(j, SUB), :]
            across = view(flux, h)[pl.ds(j + 1, SUB), :] - view(flux, h)[pl.ds(j - 1, SUB), :]
            drive = view(part, h)[pl.ds(j, SUB), :] - 0.25 * across
            z = drive * inverses[h] - e + masks[h] * inverses[h] * sums[h]
            view(total, h)[pl.ds(j, SUB), :] = e + weights[0] * z
            firsts.append(masks[h] * z)
        nxt, prv = ring_shift(firsts, lanes)
        for h in range(tiles):
            for i, value in enumerate((firsts[h], nxt[h], prv[h])):
                view(then, i, h)[pl.ds(j, SUB), :] = value

    over_tiles(prepare)

    source, target = then, now
    for k in range(1, ITERS):
        def apply(view, j, k=k, source=source, target=target):
            near, far = [], []
            for h in range(tiles):
                def pair(i, shift=0):
                    return view(pairs, i, h)[pl.ds(j + shift, SUB), :]

                near.append((pair(0), pair(0, -1), pair(1), pair(2)))
                far.append((pair(3), pair(4), pair(5), pair(6)))
            sums = nine(view, source, j, near, far)
            values = [view(ease, h)[pl.ds(j, SUB), :] * sums[h] for h in range(tiles)]
            for h in range(tiles):
                here = view(total, h)
                here[pl.ds(j, SUB), :] = here[pl.ds(j, SUB), :] + weights[k] * values[h]
            if k < ITERS - 1:
                nxt, prv = ring_shift(values, lanes)
                for h in range(tiles):
                    for i, value in enumerate((values[h], nxt[h], prv[h])):
                        view(target, i, h)[pl.ds(j, SUB), :] = value

        over_tiles(apply)
        source, target = target, source

    def finish(i, carry):
        window = pl.ds(pl.multiple_of(i * size + SUB, SUB), size + 2 * SUB)
        for r in range(0, size, SUB):
            j = r + SUB
            at = pl.ds(pl.multiple_of(i * size + r, SUB), SUB)
            views = [total.at[h, window, :] for h in range(tiles)]
            here = [v[pl.ds(j, SUB), :] for v in views]
            here[sides] = jnp.where(beyond, here[sides], 0.0)
            nxt, prv = ring_shift(here, lanes)
            for h in range(sides):
                span = pl.ds(h * LANES, LANES)
                wet = depth[at, span] > 0
                slope = views[h][pl.ds(j + 1, SUB), :] - views[h][pl.ds(j - 1, SUB), :]
                surf_out[at, span] = here[h]
                x_out[at, span] = jnp.where(wet, flow_x[at, span] - 0.25 * slope, 0.0)
                y_out[at, span] = jnp.where(
                    wet, flow_y[at, span] - 0.25 * (nxt[h] - prv[h]), 0.0
                )
        return carry

    lax.fori_loop(0, CHUNKS, finish, 0)
    outward.wait()


def solve_pass(tracer, peak, depth, surf, flow_x, flow_y, force, west, east, south, north):
    rows, cols = depth.shape
    shape = (cols // LANES + 1, rows + 4 * SUB, LANES)
    ext = pltpu.VMEM(shape, F32)
    three = pltpu.VMEM((3, *shape), F32)
    plain = jax.ShapeDtypeStruct((rows, cols), F32)
    return pl.pallas_call(
        solve_kernel,
        in_specs=[IN_VMEM] * 11,
        out_specs=[IN_HBM] + [IN_VMEM] * 3,
        out_shape=[jax.ShapeDtypeStruct(tracer.shape, F32)] + [plain] * 3,
        scratch_shapes=[ext] * 8
        + [pltpu.VMEM((7, *shape), F32), three, three, ext, pltpu.SemaphoreType.DMA],
        compiler_params=pltpu.CompilerParams(vmem_limit_bytes=VMEM_LIMIT),
        cost_estimate=pl.CostEstimate(
            flops=200 * depth.size, bytes_accessed=32 * depth.size, transcendentals=0
        ),
        name="solve",
    )(tracer, peak, depth, surf, flow_x, flow_y, force, west, east, south, north)


def both_ways(axis, to_next, to_previous):
    size = lax.axis_size(axis)
    up = [(i, (i + 1) % size) for i in range(size)]
    down = [(j, i) for i, j in up]
    return lax.ppermute(to_next, axis, up), lax.ppermute(to_previous, axis, down)


def spread_rounds(axis):
    size = lax.axis_size(axis)
    reach = 1
    while reach < size:
        if size & (size - 1) == 0:
            yield axis, [(i, i ^ reach) for i in range(size)]
        else:
            yield axis, [(i, (i + reach) % size) for i in range(size)]
        reach *= 2


def local(
    tracer, zonal_flow, meridional_flow, surface_prev, transport_x, transport_y, land_mask, levels
):
    count = tracer.shape[1]
    (
        force, depth, to_south, to_north, to_previous, to_next,
        tracer, surface_prev, transport_x, transport_y,
    ) = column_pass(tracer, land_mask, levels, surface_prev, transport_x, transport_y)
    west, east = both_ways("gx", to_next, to_previous)
    to_south, to_north = pack_pass(to_south, to_north, west, east)
    south, north = both_ways("gy", to_north, to_south)
    halo = (west, east, south, north)
    peak = peak_pass(depth, *halo)
    state = ()
    rounds = [r for axis in ("gx", "gy") for r in spread_rounds(axis)]
    cuts = [count * i // PARTS for i in range(PARTS + 1)]
    first = len(rounds) - PARTS
    for turn, (axis, pairs) in enumerate(rounds):
        moved = lax.ppermute(peak, axis, pairs)
        if turn >= first:
            part = turn - first
            state = tracer_pass(
                cuts[part], cuts[part + 1], tracer, zonal_flow, meridional_flow, depth, *halo,
                before=state,
            )
        peak = jnp.maximum(peak, moved)
        if first <= turn < len(rounds) - 1:
            peak, state = lax.optimization_barrier((peak, state))
    return solve_pass(
        state[0], peak, depth, surface_prev, transport_x, transport_y, force, *halo
    )


def solution(mesh):
    cell = P("gx", "gy")
    level = P(None, "gx", "gy")
    stack = P(None, None, "gx", "gy")
    return jax.shard_map(
        local,
        mesh=mesh,
        in_specs=(stack, level, level, cell, cell, cell, cell, cell),
        out_specs=(stack, cell, cell, cell),
        check_vma=False,
    )
```

```python
import functools

import jax
import jax.numpy as jnp
from jax import lax
from jax.experimental import pallas as pl
from jax.experimental.pallas import tpu as pltpu
from jax.sharding import PartitionSpec as P

ITERS = 4
WIDTH = ITERS + 1
LANES = 128
SUB = 8
HALF = LANES // 2
FIELDS = 5
F32 = jnp.float32
BF16 = jnp.bfloat16
VMEM_LIMIT = 12 * 1024 * 1024
LEVELS = 16
BASE = 2 * LEVELS
CODE = 1024.0
PARTS = 4
CHUNKS = 4


def lane_ids(rows):
    return lax.broadcasted_iota(jnp.int32, (rows, LANES), 1)


def put_lane(value, source, target):
    shift = (target - source) % LANES
    return pltpu.roll(value, shift, 1) if shift else value


def strip_pair(low, high, lanes, values):
    for f, (begin, end) in enumerate(values):
        at = BASE + (f + 1) * WIDTH
        turned = put_lane(jnp.where(lanes < HALF, begin, end), 0, at)
        low = jnp.where((lanes >= at) & (lanes < at + WIDTH), turned, low)
        high = jnp.where((lanes >= at - WIDTH) & (lanes < at), turned, high)
    return low, high


def column_kernel(
    tracer_hbm, land_hbm, levels_hbm, surf_hbm, flow_x_hbm, flow_y_hbm,
    force, depth, to_south, to_north, to_twin, to_other, tracer, surf, flow_x, flow_y,
    land, levels, flat_sem, chunk_sem,
):
    count = tracer.shape[1]
    rows, cols = land.shape
    sides = cols // LANES
    base = 2 * count
    lanes = lane_ids(SUB)
    size = rows // CHUNKS

    def copy_in(i):
        part = pl.ds(pl.multiple_of(i * size, SUB), size)
        return pltpu.make_async_copy(
            tracer_hbm.at[:, :, part, :], tracer.at[:, :, part, :], chunk_sem.at[i]
        )

    flats = [
        pltpu.make_async_copy(source, target, flat_sem.at[i])
        for i, (source, target) in enumerate(
            (
                (land_hbm, land),
                (levels_hbm, levels),
                (surf_hbm, surf),
                (flow_x_hbm, flow_x),
                (flow_y_hbm, flow_y),
            )
        )
    ]
    for copy in flats:
        copy.start()
    for i in range(CHUNKS):
        copy_in(i).start()
    low_kind = jnp.where((lanes >= 1) & (lanes <= base), lax.rem(lanes - 1 + count, count), -1)
    low_kind = low_kind.astype(F32)
    high_kind = jnp.where(lanes < base, lax.rem(lanes, count), -1).astype(F32)
    odd = (lanes & 1) == 1
    ends = [pl.ds(0, LANES), pl.ds((sides - 1) * LANES, LANES)]
    for copy in flats:
        copy.wait()

    def chunk(i, carry):
        copy_in(i).wait()
        upper = i >= CHUNKS // 2
        turn = jnp.where(upper, HALF, 0)
        keep = (lanes < HALF) & upper
        first_row = jnp.where(upper, i - CHUNKS // 2, i) * size
        for r in range(0, size, SUB):
            at = pl.ds(pl.multiple_of(i * size + r, SUB), SUB)
            packed = [jnp.zeros((SUB, LANES), F32)] * 2
            totals = [jnp.zeros((SUB, LANES), F32)] * sides
            deeps = []
            for h in range(sides):
                span = pl.ds(h * LANES, LANES)
                deeps.append((land[at, span] * levels[at, span]).astype(F32))
            for k in range(count):
                values = [
                    [tracer[c, k, at, pl.ds(h * LANES, LANES)] for h in range(sides)]
                    for c in range(2)
                ]
                for h in range(sides):
                    gain = jnp.maximum(deeps[h] - k, 0.0)
                    totals[h] = totals[h] + gain * (values[0][h] - 0.75 * values[1][h])
                for c in range(2):
                    line = c * count + k
                    both = jnp.where(lanes < HALF, values[c][0], values[c][-1])
                    both = put_lane(both, 0, line + 1)
                    packed[line % 2] = jnp.where(
                        (lanes == line) | (lanes == line + 1), both, packed[line % 2]
                    )
            totals = [t * (0.8 / count) for t in totals]
            for h in range(sides):
                span = pl.ds(h * LANES, LANES)
                force[at, span] = totals[h]
                depth[at, span] = deeps[h]
            low = jnp.where(odd, packed[0], packed[1])
            high = jnp.where(odd, packed[1], packed[0])
            low = jnp.where(deeps[0][:, 0:1] > low_kind, low, 0.0)
            high = jnp.where(deeps[-1][:, LANES - 1 : LANES] > high_kind, high, 0.0)
            low, high = strip_pair(
                low,
                high,
                lanes,
                [(deeps[0], deeps[-1])]
                + [tuple(ref[at, span] for span in ends) for ref in (surf, flow_x, flow_y)]
                + [(totals[0], totals[-1])],
            )
            to = pl.ds(pl.multiple_of(first_row + r, SUB), SUB)
            for out, value in ((to_south, low), (to_north, high)):
                out[to, :] = jnp.where(keep, out[to, :], pltpu.roll(value, turn, 1))
        return carry

    lax.fori_loop(0, CHUNKS, chunk, 0)

    def edge_rows(out, line, tile):
        for h in range(sides):
            span = pl.ds(h * LANES, LANES)
            deep = depth[pl.ds(line, 1), span]
            for c in range(2):
                for k in range(count):
                    out[pl.ds(c * count + k, 1), span] = jnp.where(
                        deep > k, tracer[c, k, pl.ds(line, 1), span], 0.0
                    )
            for f, ref in enumerate((depth, surf, flow_x, flow_y, force)):
                out[pl.ds(base + f * SUB, SUB), span] = ref[pl.ds(tile, SUB), span]

    even = is_even("gx")

    @pl.when(even)
    def _():
        edge_rows(to_twin, rows - 1, rows - SUB)
        edge_rows(to_other, 0, 0)

    @pl.when(jnp.logical_not(even))
    def _():
        edge_rows(to_twin, 0, 0)
        edge_rows(to_other, rows - 1, rows - SUB)


def is_even(axis):
    return lax.rem(lax.axis_index(axis), 2) == 0


IN_HBM = pl.BlockSpec(memory_space=pltpu.HBM)
IN_VMEM = pl.BlockSpec(memory_space=pltpu.VMEM)


def column_pass(tracer, land, levels, surf, flow_x, flow_y):
    two, count, rows, cols = tracer.shape
    lines = (two * count + FIELDS * SUB, cols)
    strip = (rows // 2 + SUB, LANES)
    plain = (rows, cols)
    shapes = [plain, plain, strip, strip, lines, lines, tracer.shape, plain, plain, plain]
    return pl.pallas_call(
        column_kernel,
        in_specs=[IN_HBM] * 6,
        out_specs=[IN_VMEM] * len(shapes),
        out_shape=[jax.ShapeDtypeStruct(shape, F32) for shape in shapes],
        scratch_shapes=[
            pltpu.VMEM(plain, jnp.int32),
            pltpu.VMEM(plain, jnp.int32),
            pltpu.SemaphoreType.DMA((5,)),
            pltpu.SemaphoreType.DMA((CHUNKS,)),
        ],
        compiler_params=pltpu.CompilerParams(vmem_limit_bytes=VMEM_LIMIT),
        cost_estimate=pl.CostEstimate(
            flops=6 * tracer.size, bytes_accessed=4 * tracer.size, transcendentals=0
        ),
        name="columns",
    )(
        *(
            pltpu.with_memory_space_constraint(value, pltpu.HBM)
            for value in (tracer, land, levels, surf, flow_x, flow_y)
        )
    )


def pack_kernel(to_south, to_north, from_twin, from_other, to_twin, to_other, west, east):
    half = to_south.shape[0] - SUB
    sides = west.shape[1] // LANES
    lanes = lane_ids(SUB)
    even_x, even_y = is_even("gx"), is_even("gy")
    for r in range(0, west.shape[0], SUB):
        for h in range(sides):
            at = (pl.ds(r, SUB), pl.ds(h * LANES, LANES))
            first, second = from_twin[at], from_other[at]
            east[at] = jnp.where(even_x, first, second)
            west[at] = jnp.where(even_x, second, first)
    strips = []
    for ref in (west, east):
        zero = jnp.zeros((SUB, LANES), F32)
        ends = [pl.ds(0, LANES), pl.ds((sides - 1) * LANES, LANES)]
        values = [
            tuple(ref[pl.ds(BASE + f * SUB, SUB), span] for span in ends) for f in range(FIELDS)
        ]
        strips.append(strip_pair(zero, zero, lanes, values))
    for r in range(0, half + SUB, SUB):
        at = pl.ds(r, SUB)
        if r < half:
            low, high = to_south[at, :], to_north[at, :]
        else:
            low, high = (
                jnp.where(lanes < HALF, before, pltpu.roll(after, HALF, 1))
                for before, after in zip(*strips)
            )
        to_twin[at, :] = jnp.where(even_y, high, low)
        to_other[at, :] = jnp.where(even_y, low, high)


def pack_pass(to_south, to_north, from_twin, from_other):
    strip = jax.ShapeDtypeStruct(to_south.shape, F32)
    lines = jax.ShapeDtypeStruct(from_twin.shape, F32)
    return pl.pallas_call(
        pack_kernel,
        in_specs=[IN_VMEM] * 4,
        out_specs=[IN_VMEM] * 4,
        out_shape=[strip, strip, lines, lines],
        compiler_params=pltpu.CompilerParams(vmem_limit_bytes=VMEM_LIMIT),
        cost_estimate=pl.CostEstimate(
            flops=to_south.size, bytes_accessed=16 * to_south.size, transcendentals=0
        ),
        name="corners",
    )(to_south, to_north, from_twin, from_other)


def message_rows(ref, rows, r):
    half = rows // 2
    if r < 0:
        return ref[pl.ds(half, SUB), :]
    if r >= rows:
        return pltpu.roll(ref[pl.ds(half, SUB), :], HALF, 1)
    if r < half:
        return ref[pl.ds(r, SUB), :]
    return pltpu.roll(ref[pl.ds(r - half, SUB), :], HALF, 1)


def outer_tile(south, north, rows, r, f, open_south, open_north, lanes):
    at = BASE + (f + 1) * WIDTH
    mixed = jnp.where(lanes < at, message_rows(south, rows, r), message_rows(north, rows, r))
    mixed = put_lane(mixed, at, 0)
    valid = ((lanes < WIDTH) & open_north) | ((lanes >= LANES - WIDTH) & open_south)
    return jnp.where(valid, mixed, 0.0)


def extend(target, base, f, field, west, east, south, north, open_south, open_north):
    rows, cols = field.shape
    sides = cols // LANES
    lanes = lane_ids(SUB)
    for r in range(-SUB, rows + 1, SUB):
        to = pl.ds(SUB + r, SUB)
        for h in range(sides):
            span = pl.ds(h * LANES, LANES)
            if r < 0:
                target[h, to, :] = west[pl.ds(base + f * SUB, SUB), span]
            elif r >= rows:
                target[h, to, :] = east[pl.ds(base + f * SUB, SUB), span]
            else:
                target[h, to, :] = field[pl.ds(r, SUB), span]
        target[sides, to, :] = outer_tile(
            south, north, rows, r, f, open_south, open_north, lanes
        )


def latitude_ends():
    place, size = lax.axis_index("gy"), lax.axis_size("gy")
    return place > 0, place < size - 1


def ring_shift(tiles, lanes):
    size = len(tiles)
    after = [pltpu.roll(t, LANES - 1, 1) for t in tiles]
    before = [pltpu.roll(t, 1, 1) for t in tiles]
    nxt = [jnp.where(lanes == LANES - 1, after[(h + 1) % size], after[h]) for h in range(size)]
    prv = [jnp.where(lanes == 0, before[(h - 1) % size], before[h]) for h in range(size)]
    return nxt, prv


def nine_sum(ref, r, lanes):
    sides = [ref[h, pl.ds(r + 1, SUB), :] + ref[h, pl.ds(r - 1, SUB), :] for h in range(ref.shape[0])]
    mixed = [ref[h, pl.ds(r, SUB), :] + 0.5 * sides[h] for h in range(ref.shape[0])]
    nxt, prv = ring_shift(mixed, lanes)
    return [sides[h] + (nxt[h] + prv[h]) for h in range(ref.shape[0])]


def peak_kernel(depth, west, east, from_twin, from_other, peak, south, north, coded):
    rows, cols = depth.shape
    sides = cols // LANES
    lanes = lane_ids(SUB)
    open_south, open_north = latitude_ends()
    scale = 2.0 / (BASE // 2)
    even = is_even("gy")
    for r in range(0, south.shape[0], SUB):
        at = pl.ds(r, SUB)
        first, second = from_twin[at, :], from_other[at, :]
        north[at, :] = jnp.where(even, first, second)
        south[at, :] = jnp.where(even, second, first)
    extend(coded, BASE, 0, depth, west, east, south, north, open_south, open_north)
    for r in range(0, rows + 2 * SUB, SUB):
        for h in range(sides + 1):
            d = coded[h, pl.ds(r, SUB), :]
            coded[h, pl.ds(r, SUB), :] = d + jnp.where(d > 0, CODE, 0.0)
    best = jnp.full((SUB, LANES), 0.0, F32)
    for r in range(SUB, rows + SUB, SUB):
        sums = nine_sum(coded, r, lanes)
        for h in range(sides):
            wet, deep = decode(sums[h])
            d = depth[pl.ds(r - SUB, SUB), pl.ds(h * LANES, LANES)]
            best = jnp.maximum(best, d * wet + jnp.where(d > 0, deep, 0.0))
    best = jnp.max(jnp.max(best, axis=1, keepdims=True), axis=0, keepdims=True)
    peak[...] = jnp.broadcast_to(0.5 + scale * best, (SUB, LANES))


def decode(sums):
    wet = jnp.floor(sums * (2.0 / CODE)) * 0.5
    return wet, sums - CODE * wet


def peak_pass(depth, west, east, from_twin, from_other):
    rows, cols = depth.shape
    strip = jax.ShapeDtypeStruct(from_twin.shape, F32)
    ext = pltpu.VMEM((cols // LANES + 1, rows + 2 * SUB, LANES), F32)
    return pl.pallas_call(
        peak_kernel,
        in_specs=[IN_VMEM] * 5,
        out_specs=[IN_VMEM] * 3,
        out_shape=[jax.ShapeDtypeStruct((SUB, LANES), F32), strip, strip],
        scratch_shapes=[ext],
        compiler_params=pltpu.CompilerParams(vmem_limit_bytes=VMEM_LIMIT),
        cost_estimate=pl.CostEstimate(
            flops=30 * depth.size, bytes_accessed=4 * depth.size, transcendentals=0
        ),
        name="peak",
    )(depth, west, east, from_twin, from_other)


def around_kernel(depth, west, east, south, north, edge_y, around, masked):
    rows, cols = depth.shape
    sides = cols // LANES
    lanes = lane_ids(SUB)
    spans = [pl.ds(h * LANES, LANES) for h in range(sides)]
    open_south, open_north = latitude_ends()
    for h in range(sides):
        masked[h, pl.ds(0, SUB), :] = west[pl.ds(BASE, SUB), spans[h]]
        masked[h, pl.ds(SUB, rows), :] = depth[:, spans[h]]
        masked[h, pl.ds(SUB + rows, SUB), :] = east[pl.ds(BASE, SUB), spans[h]]
    for big in range(0, rows, 2 * SUB):
        shifted = []
        for r in (big, big + SUB):
            low, high = message_rows(south, rows, r), message_rows(north, rows, r)
            edge_y[0, pl.ds(r, SUB), :] = jnp.where(open_south, low, 0.0)
            edge_y[1, pl.ds(r, SUB), :] = jnp.where(
                open_north, pltpu.roll(high, LANES - 2, 1), 0.0
            )
            tiles = [depth[pl.ds(r, SUB), span] for span in spans]
            tiles.append(outer_tile(south, north, rows, r, 0, open_south, open_north, lanes))
            shifted.append(ring_shift(tiles, lanes))
        at = pl.ds(big, 2 * SUB)
        for h in range(sides):
            around[0, h, at, :] = masked[h, pl.ds(SUB + big + 1, 2 * SUB), :].astype(BF16)
            around[1, h, at, :] = masked[h, pl.ds(SUB + big - 1, 2 * SUB), :].astype(BF16)
            for n in range(2):
                pair = jnp.concatenate([shifted[0][n][h], shifted[1][n][h]], 0)
                around[2 + n, h, at, :] = pair.astype(BF16)


def around_pass(depth, west, east, south, north):
    rows, cols = depth.shape
    sides = cols // LANES
    return pl.pallas_call(
        around_kernel,
        in_specs=[IN_VMEM] * 5,
        out_specs=[IN_VMEM] * 2,
        out_shape=[
            jax.ShapeDtypeStruct((2, rows, LANES), F32),
            jax.ShapeDtypeStruct((4, sides, rows, LANES), BF16),
        ],
        scratch_shapes=[pltpu.VMEM((sides, rows + 2 * SUB, LANES), F32)],
        compiler_params=pltpu.CompilerParams(vmem_limit_bytes=VMEM_LIMIT),
        cost_estimate=pl.CostEstimate(
            flops=30 * depth.size, bytes_accessed=16 * depth.size, transcendentals=0
        ),
        name="around",
    )(depth, west, east, south, north)


def tracer_kernel(start, stop, tracer, zonal, merid, depth, west, east, edge_y, around, *rest):
    out, masked = rest[-2:]
    rows, cols = depth.shape
    sides = cols // LANES
    count = BASE // 2
    lanes = lane_ids(SUB)
    spans = [pl.ds(h * LANES, LANES) for h in range(sides)]

    def one_level(level, carry):
        mark = lax.convert_element_type(level, F32)
        for c in range(2):
            line = c * count + level
            group = pl.multiple_of(lax.div(line, SUB) * SUB, SUB)
            place = lax.rem(line, SUB)
            for h in range(sides):
                before = west[pl.ds(group, SUB), spans[h]]
                masked[c, h, pl.ds(0, SUB), :] = pltpu.roll(before, SUB - 1 - place, 0)
                after = east[pl.ds(group, SUB), spans[h]]
                masked[c, h, pl.ds(SUB + rows, SUB), :] = pltpu.roll(after, lax.rem(SUB - place, SUB), 0)
        for r in range(0, rows, SUB):
            for h in range(sides):
                here = depth[pl.ds(r, SUB), spans[h]] > mark
                for c in range(2):
                    masked[c, h, pl.ds(SUB + r, SUB), :] = jnp.where(
                        here, tracer[c, level, pl.ds(r, SUB), spans[h]], 0.0
                    )
        mark_pair = jnp.full((2 * SUB, LANES), mark, F32).astype(BF16)
        one, none = jnp.ones((2 * SUB, LANES), BF16), jnp.zeros((2 * SUB, LANES), BF16)
        quarter = jnp.full((2 * SUB, LANES), 0.25, BF16)
        picks = []
        for c in range(2):
            line = c * count + level
            picks.append(((lanes >= line) & (lanes < line + HALF), lax.rem(LANES - line, LANES)))
        for big in range(0, rows, 2 * SUB):
            wide = pl.ds(big, 2 * SUB)
            pairs = []
            for h in range(sides):
                near = none
                for n in range(4):
                    near = near + jnp.where(around[n, h, wide, :] > mark_pair, one, none)
                pairs.append(
                    (
                        1.0 - 0.2 * near.astype(F32),
                        (zonal[level, wide, spans[h]] * quarter).astype(F32),
                        (merid[level, wide, spans[h]] * quarter).astype(F32),
                    )
                )
            for sub in range(2):
                r = big + sub * SUB
                at = pl.ds(r, SUB)
                part = slice(sub * SUB, (sub + 1) * SUB)
                factors = []
                for h in range(sides):
                    own, u, v = (value[part] for value in pairs[h])
                    here = depth[at, spans[h]] > mark
                    factors.append((here, own, 0.2 - u, 0.2 + u, 0.2 - v, 0.2 + v))
                for c in range(2):
                    tiles = [masked[c, h, pl.ds(SUB + r, SUB), :] for h in range(sides)]
                    pick, turn = picks[c]
                    outer = pltpu.roll(jnp.where(pick, edge_y[0, at, :], edge_y[1, at, :]), turn, 1)
                    after = [pltpu.roll(t, LANES - 1, 1) for t in tiles] + [outer]
                    before = [outer] + [pltpu.roll(t, 1, 1) for t in tiles]
                    for h in range(sides):
                        here, own, to_e, to_w, to_n, to_s = factors[h]
                        nxt = jnp.where(lanes == LANES - 1, after[h + 1], after[h])
                        prv = jnp.where(lanes == 0, before[h], before[h + 1])
                        value = own * tiles[h] + to_n * nxt + to_s * prv
                        value = value + to_e * masked[c, h, pl.ds(SUB + r + 1, SUB), :]
                        value = value + to_w * masked[c, h, pl.ds(SUB + r - 1, SUB), :]
                        out[c, level, at, spans[h]] = jnp.where(
                            here, value, tracer[c, level, at, spans[h]]
                        )
        return carry

    lax.fori_loop(start, stop, one_level, 0)


def tracer_pass(start, stop, tracer, zonal, merid, depth, west, east, edge_y, around, before=()):
    two, count, rows, cols = tracer.shape
    sides = cols // LANES
    operands = [tracer, zonal, merid, depth, west, east, edge_y, around, *before]
    part = stop - start
    return pl.pallas_call(
        functools.partial(tracer_kernel, start, stop),
        in_specs=[IN_VMEM] * len(operands),
        out_specs=IN_VMEM,
        out_shape=jax.ShapeDtypeStruct(tracer.shape, F32),
        scratch_shapes=[pltpu.VMEM((2, sides, rows + 2 * SUB, LANES), F32)],
        input_output_aliases={len(operands) - 1: 0} if before else {},
        compiler_params=pltpu.CompilerParams(vmem_limit_bytes=VMEM_LIMIT),
        cost_estimate=pl.CostEstimate(
            flops=40 * tracer.size * part // count,
            bytes_accessed=10 * tracer.size * part // count,
            transcendentals=0,
        ),
        name="tracers",
    )(*operands)


def group_of(tiles):
    return max(n for n in range(1, 17) if tiles % n == 0)


def solve_kernel(
    tracer_in, peak, depth, surf, flow_x, flow_y, force, west, east, south, north,
    tracer_hbm, surf_hbm, x_hbm, y_hbm,
    surf_out, x_out, y_out, old, deep, deep_n, deep_s, coded, flux, part, ease, pairs, now, then, total, sem, out_sem,
):
    rows, cols = depth.shape
    sides = cols // LANES
    tiles = sides + 1
    lanes = lane_ids(SUB)
    scale = 2.0 / BASE
    open_south, open_north = latitude_ends()
    beyond = ((lanes < WIDTH) & open_north) | ((lanes >= LANES - WIDTH) & open_south)
    outward = [
        pltpu.make_async_copy(tracer_in.at[:, k], tracer_hbm.at[:, k], sem.at[k])
        for k in range(BASE // 2)
    ]
    for copy in outward:
        copy.start()

    lowest = 0.5 / peak[...]
    shrink = (1.0 - lowest) * (1.0 - lowest)
    omega = jnp.full((SUB, LANES), 2.0, F32)
    weights, change = [jnp.ones((SUB, LANES), F32)], [jnp.ones((SUB, LANES), F32)]
    for _ in range(1, ITERS):
        omega = 1.0 / (1.0 - omega * shrink * 0.25)
        resid = [1.0 - weights[0]] + [p - w for p, w in zip(weights, weights[1:])] + [weights[-1]]
        held = change + [jnp.zeros((SUB, LANES), F32)]
        change = [omega * y + (omega - 1.0) * d for y, d in zip(resid, held)]
        weights = [w + d for w, d in zip(weights + [jnp.zeros((SUB, LANES), F32)], change)]

    edge = (pl.ds(0, SUB), pl.ds(rows + 3 * SUB, SUB))
    for ref in (deep, deep_n, deep_s, coded, flux):
        for at in edge:
            for h in range(tiles):
                ref[h, at, :] = jnp.zeros((SUB, LANES), F32)
    for ref in (pairs, now, then):
        for i in range(ref.shape[0]):
            for at in edge:
                for h in range(tiles):
                    ref[i, h, at, :] = jnp.zeros((SUB, LANES), F32)

    def spread(ref, at, values):
        nxt, prv = ring_shift(values, lanes)
        for h in range(tiles):
            ref[0, h, at, :] = values[h]
            ref[1, h, at, :] = nxt[h]
            ref[2, h, at, :] = prv[h]

    def load_tile(to, field, low, high):
        def ring(f):
            at = BASE + (f + 1) * WIDTH
            outer = put_lane(jnp.where(lanes < at, low, high), at, 0)
            return [field(f, h) for h in range(sides)] + [jnp.where(beyond, outer, 0.0)]

        levels = ring(0)
        deeps = [v * scale for v in levels]
        wets = [jnp.where(v > 0, 1.0, 0.0) for v in levels]
        nxt, prv = ring_shift(deeps, lanes)
        surfs, drives = ring(1), ring(4)
        cross, crosses = ring_shift([m * v for m, v in zip(wets, ring(3))], lanes)
        along = ring(2)
        for h in range(tiles):
            deep[h, to, :] = deeps[h]
            deep_n[h, to, :] = nxt[h]
            deep_s[h, to, :] = prv[h]
            coded[h, to, :] = levels[h] + CODE * wets[h]
            old[h, to, :] = surfs[h]
            flux[h, to, :] = wets[h] * along[h]
            part[h, to, :] = 0.5 * surfs[h] + drives[h] - 0.25 * (cross[h] - crosses[h])
        spread(now, to, [m * v for m, v in zip(wets, surfs)])

    fields = (depth, surf, flow_x, flow_y, force)
    half = rows // 2
    for ref, to, turn in ((west, SUB, 0), (east, rows + 2 * SUB, HALF)):
        tail = [message[pl.ds(half, SUB), :] for message in (south, north)]
        if turn:
            tail = [pltpu.roll(v, turn, 1) for v in tail]
        load_tile(
            pl.ds(to, SUB),
            lambda f, h, ref=ref: ref[pl.ds(BASE + f * SUB, SUB), pl.ds(h * LANES, LANES)],
            *tail,
        )
    size = rows // CHUNKS

    def load_chunk(i, carry):
        upper = i >= CHUNKS // 2
        turn = jnp.where(upper, HALF, 0)
        first_row = jnp.where(upper, i - CHUNKS // 2, i) * size
        for r in range(0, size, SUB):
            at = pl.ds(pl.multiple_of(i * size + r, SUB), SUB)
            line = pl.ds(pl.multiple_of(first_row + r, SUB), SUB)
            load_tile(
                pl.ds(pl.multiple_of(i * size + r + 2 * SUB, SUB), SUB),
                lambda f, h, at=at: fields[f][at, pl.ds(h * LANES, LANES)],
                *(pltpu.roll(message[line, :], turn, 1) for message in (south, north)),
            )
        return carry

    lax.fori_loop(0, CHUNKS, load_chunk, 0)

    count = rows // SUB + 2
    group = group_of(count)

    def over_tiles(body):
        def step(i, carry):
            window = pl.ds(pl.multiple_of(i * (group * SUB), SUB), (group + 2) * SUB)

            def view(ref, *index):
                return ref.at[(*index, window, slice(None))]

            for j in range(SUB, (group + 1) * SUB, SUB):
                body(view, j)
            return carry

        lax.fori_loop(0, count // group, step, 0)

    def nine(view, source, j, near, far):
        result = []
        for h in range(tiles):
            def value(i, shift):
                return view(source, i, h)[pl.ds(j + shift, SUB), :]

            side = near[h][0] * value(0, 1) + near[h][1] * value(0, -1)
            side = side + near[h][2] * value(1, 0) + near[h][3] * value(2, 0)
            corner = far[h][0] * value(1, 1) + far[h][1] * value(1, -1)
            corner = corner + far[h][2] * value(2, 1) + far[h][3] * value(2, -1)
            result.append(side + corner)
        return result

    def prepare(view, j):
        mixed, sides_of = [], []
        for h in range(tiles):
            code = view(coded, h)
            sides_of.append(code[pl.ds(j + 1, SUB), :] + code[pl.ds(j - 1, SUB), :])
            mixed.append(code[pl.ds(j, SUB), :] + 0.5 * sides_of[h])
        nxt, prv = ring_shift(mixed, lanes)
        near, far, inverses, masks = [], [], [], []
        for h in range(tiles):
            own = view(deep, h)[pl.ds(j, SUB), :]
            wet_sum, deep_sum = decode(sides_of[h] + (nxt[h] + prv[h]))
            wet = jnp.where(own > 0, 1.0, 0.0)
            diag = 0.5 + 2.0 * (own * wet_sum + wet * (deep_sum * scale))
            inverse = 1.0 / diag
            inverses.append(inverse)
            masks.append(wet)
            ease_h = wet * inverse
            view(ease, h)[pl.ds(j, SUB), :] = ease_h
            twice = own + own
            e = twice + 2.0 * view(deep, h)[pl.ds(j + 1, SUB), :]
            w = twice + 2.0 * view(deep, h)[pl.ds(j - 1, SUB), :]
            n = twice + 2.0 * view(deep_n, h)[pl.ds(j, SUB), :]
            s = twice + 2.0 * view(deep_s, h)[pl.ds(j, SUB), :]
            ne = own + view(deep_n, h)[pl.ds(j + 1, SUB), :]
            nw = own + view(deep_n, h)[pl.ds(j - 1, SUB), :]
            se = own + view(deep_s, h)[pl.ds(j + 1, SUB), :]
            sw = own + view(deep_s, h)[pl.ds(j - 1, SUB), :]
            for i, value in enumerate((e, n, s, ne, nw, se, sw)):
                view(pairs, i, h)[pl.ds(j, SUB), :] = value
            near.append((e, w, n, s))
            far.append((ne, nw, se, sw))
        sums = nine(view, now, j, near, far)
        firsts = []
        for h in range(tiles):
            e = view(old, h)[pl.ds(j, SUB), :]
            across = view(flux, h)[pl.ds(j + 1, SUB), :] - view(flux, h)[pl.ds(j - 1, SUB), :]
            drive = view(part, h)[pl.ds(j, SUB), :] - 0.25 * across
            z = drive * inverses[h] - e + masks[h] * inverses[h] * sums[h]
            view(total, h)[pl.ds(j, SUB), :] = e + weights[0] * z
            firsts.append(masks[h] * z)
        nxt, prv = ring_shift(firsts, lanes)
        for h in range(tiles):
            for i, value in enumerate((firsts[h], nxt[h], prv[h])):
                view(then, i, h)[pl.ds(j, SUB), :] = value

    over_tiles(prepare)

    source, target = then, now
    for k in range(1, ITERS):
        def apply(view, j, k=k, source=source, target=target):
            near, far = [], []
            for h in range(tiles):
                def pair(i, shift=0):
                    return view(pairs, i, h)[pl.ds(j + shift, SUB), :]

                near.append((pair(0), pair(0, -1), pair(1), pair(2)))
                far.append((pair(3), pair(4), pair(5), pair(6)))
            sums = nine(view, source, j, near, far)
            values = [view(ease, h)[pl.ds(j, SUB), :] * sums[h] for h in range(tiles)]
            for h in range(tiles):
                here = view(total, h)
                here[pl.ds(j, SUB), :] = here[pl.ds(j, SUB), :] + weights[k] * values[h]
            if k < ITERS - 1:
                nxt, prv = ring_shift(values, lanes)
                for h in range(tiles):
                    for i, value in enumerate((values[h], nxt[h], prv[h])):
                        view(target, i, h)[pl.ds(j, SUB), :] = value

        over_tiles(apply)
        source, target = target, source

    def results(i):
        part_of = pl.ds(pl.multiple_of(i * size, SUB), size)
        return [
            pltpu.make_async_copy(
                value.at[part_of, :], place.at[part_of, :], out_sem.at[n * CHUNKS + i]
            )
            for n, (value, place) in enumerate(
                ((surf_out, surf_hbm), (x_out, x_hbm), (y_out, y_hbm))
            )
        ]

    def finish(i, carry):
        window = pl.ds(pl.multiple_of(i * size + SUB, SUB), size + 2 * SUB)
        for r in range(0, size, SUB):
            j = r + SUB
            at = pl.ds(pl.multiple_of(i * size + r, SUB), SUB)
            views = [total.at[h, window, :] for h in range(tiles)]
            here = [v[pl.ds(j, SUB), :] for v in views]
            here[sides] = jnp.where(beyond, here[sides], 0.0)
            nxt, prv = ring_shift(here, lanes)
            for h in range(sides):
                span = pl.ds(h * LANES, LANES)
                wet = depth[at, span] > 0
                slope = views[h][pl.ds(j + 1, SUB), :] - views[h][pl.ds(j - 1, SUB), :]
                surf_out[at, span] = here[h]
                x_out[at, span] = jnp.where(wet, flow_x[at, span] - 0.25 * slope, 0.0)
                y_out[at, span] = jnp.where(
                    wet, flow_y[at, span] - 0.25 * (nxt[h] - prv[h]), 0.0
                )
        for copy in results(i):
            copy.start()
        return carry

    lax.fori_loop(0, CHUNKS, finish, 0)
    for i in range(CHUNKS):
        for copy in results(i):
            copy.wait()
    for copy in outward:
        copy.wait()


def solve_pass(tracer, peak, depth, surf, flow_x, flow_y, force, west, east, south, north):
    rows, cols = depth.shape
    shape = (cols // LANES + 1, rows + 4 * SUB, LANES)
    ext = pltpu.VMEM(shape, F32)
    three = pltpu.VMEM((3, *shape), F32)
    plain = jax.ShapeDtypeStruct((rows, cols), F32)
    return pl.pallas_call(
        solve_kernel,
        in_specs=[IN_VMEM] * 11,
        out_specs=[IN_HBM] * 4,
        out_shape=[jax.ShapeDtypeStruct(tracer.shape, F32)] + [plain] * 3,
        scratch_shapes=[pltpu.VMEM((rows, cols), F32)] * 3
        + [ext] * 8
        + [pltpu.VMEM((7, *shape), F32), three, three, ext]
        + [pltpu.SemaphoreType.DMA((BASE // 2,)), pltpu.SemaphoreType.DMA((3 * CHUNKS,))],
        compiler_params=pltpu.CompilerParams(vmem_limit_bytes=VMEM_LIMIT),
        cost_estimate=pl.CostEstimate(
            flops=200 * depth.size, bytes_accessed=32 * depth.size, transcendentals=0
        ),
        name="solve",
    )(tracer, peak, depth, surf, flow_x, flow_y, force, west, east, south, north)


def twin_pairs(axis):
    return [(i, i ^ 1) for i in range(lax.axis_size(axis))]


def other_x_pairs():
    size = lax.axis_size("gx")
    return [(i, (i + 1 if i % 2 else i - 1) % size) for i in range(size)]


def other_y_pairs():
    size_x, size_y = lax.axis_size("gx"), lax.axis_size("gy")
    pairs = []
    for i in range(size_x):
        for j in range(size_y):
            if j in (0, size_y - 1):
                target = (i ^ 1, j)
            else:
                target = (i, j + 1 if j % 2 else j - 1)
            pairs.append((i * size_y + j, target[0] * size_y + target[1]))
    return pairs


def spread_rounds(axis):
    size = lax.axis_size(axis)
    reach = 1
    while reach < size:
        if size & (size - 1) == 0:
            yield axis, [(i, i ^ reach) for i in range(size)]
        else:
            yield axis, [(i, (i + reach) % size) for i in range(size)]
        reach *= 2


def local(
    tracer, zonal_flow, meridional_flow, surface_prev, transport_x, transport_y, land_mask, levels
):
    count = tracer.shape[1]
    (
        force, depth, to_south, to_north, to_twin, to_other,
        tracer, surface_prev, transport_x, transport_y,
    ) = column_pass(tracer, land_mask, levels, surface_prev, transport_x, transport_y)
    to_twin, to_other, zonal_flow, meridional_flow = lax.optimization_barrier(
        (to_twin, to_other, zonal_flow, meridional_flow)
    )
    from_other = lax.ppermute(to_other, "gx", other_x_pairs())
    from_twin = lax.ppermute(to_twin, "gx", twin_pairs("gx"))
    to_twin, to_other, west, east = pack_pass(to_south, to_north, from_twin, from_other)
    from_twin = lax.ppermute(to_twin, "gy", twin_pairs("gy"))
    from_other = lax.ppermute(to_other, ("gx", "gy"), other_y_pairs())
    peak, south, north = peak_pass(depth, west, east, from_twin, from_other)
    halo = (west, east, south, north)
    rounds = [r for axis in ("gx", "gy") for r in spread_rounds(axis)]
    cuts = [count * i // PARTS for i in range(PARTS + 1)]
    first = len(rounds) - PARTS
    known, tracer_next = (), ()
    for turn, (axis, pairs) in enumerate(rounds):
        moved = lax.ppermute(peak, axis, pairs)
        if turn == 0:
            known = around_pass(depth, *halo)
            moved, known = lax.optimization_barrier((moved, known))
        if turn >= first:
            part = turn - first
            tracer_next = tracer_pass(
                cuts[part], cuts[part + 1], tracer, zonal_flow, meridional_flow, depth,
                west, east, *known, before=(tracer_next,) if part else (),
            )
        peak = jnp.maximum(peak, moved)
        if first <= turn < len(rounds) - 1:
            peak, tracer_next = lax.optimization_barrier((peak, tracer_next))
    return solve_pass(
        tracer_next, peak, depth, surface_prev, transport_x, transport_y, force, *halo
    )


def solution(mesh):
    cell = P("gx", "gy")
    level = P(None, "gx", "gy")
    stack = P(None, None, "gx", "gy")
    return jax.shard_map(
        local,
        mesh=mesh,
        in_specs=(stack, level, level, cell, cell, cell, cell, cell),
        out_specs=(stack, cell, cell, cell),
        check_vma=False,
    )
```

```python
import functools

import jax
import jax.numpy as jnp
from jax import lax
from jax.experimental import pallas as pl
from jax.experimental.pallas import tpu as pltpu
from jax.sharding import PartitionSpec as P

ITERS = 4
WIDTH = ITERS + 1
LANES = 128
SUB = 8
HALF = LANES // 2
FIELDS = 5
F32 = jnp.float32
BF16 = jnp.bfloat16
VMEM_LIMIT = 12 * 1024 * 1024
LEVELS = 16
BASE = 2 * LEVELS
CODE = 1024.0
PARTS = 4
CHUNKS = 4


def lane_ids(rows):
    return lax.broadcasted_iota(jnp.int32, (rows, LANES), 1)


def put_lane(value, source, target):
    shift = (target - source) % LANES
    return pltpu.roll(value, shift, 1) if shift else value


def strip_pair(low, high, lanes, values):
    for f, (begin, end) in enumerate(values):
        at = BASE + (f + 1) * WIDTH
        turned = put_lane(jnp.where(lanes < HALF, begin, end), 0, at)
        low = jnp.where((lanes >= at) & (lanes < at + WIDTH), turned, low)
        high = jnp.where((lanes >= at - WIDTH) & (lanes < at), turned, high)
    return low, high


def column_kernel(
    tracer_hbm, land_hbm, levels_hbm, surf_hbm, flow_x_hbm, flow_y_hbm,
    force, depth, to_south, to_north, to_twin, to_other, tracer, surf, flow_x, flow_y,
    land, levels, flat_sem, chunk_sem,
):
    count = tracer.shape[1]
    rows, cols = land.shape
    sides = cols // LANES
    base = 2 * count
    lanes = lane_ids(SUB)
    size = rows // CHUNKS

    def copy_in(i):
        part = pl.ds(pl.multiple_of(i * size, SUB), size)
        return pltpu.make_async_copy(
            tracer_hbm.at[:, :, part, :], tracer.at[:, :, part, :], chunk_sem.at[i]
        )

    flats = [
        pltpu.make_async_copy(source, target, flat_sem.at[i])
        for i, (source, target) in enumerate(
            (
                (land_hbm, land),
                (levels_hbm, levels),
                (surf_hbm, surf),
                (flow_x_hbm, flow_x),
                (flow_y_hbm, flow_y),
            )
        )
    ]
    for copy in flats:
        copy.start()
    for i in range(CHUNKS):
        copy_in(i).start()
    low_kind = jnp.where((lanes >= 1) & (lanes <= base), lax.rem(lanes - 1 + count, count), -1)
    low_kind = low_kind.astype(F32)
    high_kind = jnp.where(lanes < base, lax.rem(lanes, count), -1).astype(F32)
    odd = (lanes & 1) == 1
    ends = [pl.ds(0, LANES), pl.ds((sides - 1) * LANES, LANES)]
    for copy in flats:
        copy.wait()

    def chunk(i, carry):
        copy_in(i).wait()
        upper = i >= CHUNKS // 2
        turn = jnp.where(upper, HALF, 0)
        keep = (lanes < HALF) & upper
        first_row = jnp.where(upper, i - CHUNKS // 2, i) * size
        for r in range(0, size, SUB):
            at = pl.ds(pl.multiple_of(i * size + r, SUB), SUB)
            packed = [jnp.zeros((SUB, LANES), F32)] * 2
            totals = [jnp.zeros((SUB, LANES), F32)] * sides
            deeps = []
            for h in range(sides):
                span = pl.ds(h * LANES, LANES)
                deeps.append((land[at, span] * levels[at, span]).astype(F32))
            for k in range(count):
                values = [
                    [tracer[c, k, at, pl.ds(h * LANES, LANES)] for h in range(sides)]
                    for c in range(2)
                ]
                for h in range(sides):
                    gain = jnp.maximum(deeps[h] - k, 0.0)
                    totals[h] = totals[h] + gain * (values[0][h] - 0.75 * values[1][h])
                for c in range(2):
                    line = c * count + k
                    both = jnp.where(lanes < HALF, values[c][0], values[c][-1])
                    both = put_lane(both, 0, line + 1)
                    packed[line % 2] = jnp.where(
                        (lanes == line) | (lanes == line + 1), both, packed[line % 2]
                    )
            totals = [t * (0.8 / count) for t in totals]
            for h in range(sides):
                span = pl.ds(h * LANES, LANES)
                force[at, span] = totals[h]
                depth[at, span] = deeps[h]
            low = jnp.where(odd, packed[0], packed[1])
            high = jnp.where(odd, packed[1], packed[0])
            low = jnp.where(deeps[0][:, 0:1] > low_kind, low, 0.0)
            high = jnp.where(deeps[-1][:, LANES - 1 : LANES] > high_kind, high, 0.0)
            low, high = strip_pair(
                low,
                high,
                lanes,
                [(deeps[0], deeps[-1])]
                + [tuple(ref[at, span] for span in ends) for ref in (surf, flow_x, flow_y)]
                + [(totals[0], totals[-1])],
            )
            to = pl.ds(pl.multiple_of(first_row + r, SUB), SUB)
            for out, value in ((to_south, low), (to_north, high)):
                out[to, :] = jnp.where(keep, out[to, :], pltpu.roll(value, turn, 1))
        return carry

    lax.fori_loop(0, CHUNKS, chunk, 0)

    def edge_rows(out, line, tile):
        for h in range(sides):
            span = pl.ds(h * LANES, LANES)
            deep = depth[pl.ds(line, 1), span]
            for c in range(2):
                for k in range(count):
                    out[pl.ds(c * count + k, 1), span] = jnp.where(
                        deep > k, tracer[c, k, pl.ds(line, 1), span], 0.0
                    )
            for f, ref in enumerate((depth, surf, flow_x, flow_y, force)):
                out[pl.ds(base + f * SUB, SUB), span] = ref[pl.ds(tile, SUB), span]

    even = is_even("gx")

    @pl.when(even)
    def _():
        edge_rows(to_twin, rows - 1, rows - SUB)
        edge_rows(to_other, 0, 0)

    @pl.when(jnp.logical_not(even))
    def _():
        edge_rows(to_twin, 0, 0)
        edge_rows(to_other, rows - 1, rows - SUB)


def is_even(axis):
    return lax.rem(lax.axis_index(axis), 2) == 0


IN_HBM = pl.BlockSpec(memory_space=pltpu.HBM)
IN_VMEM = pl.BlockSpec(memory_space=pltpu.VMEM)


def column_pass(tracer, land, levels, surf, flow_x, flow_y):
    two, count, rows, cols = tracer.shape
    lines = (two * count + FIELDS * SUB, cols)
    strip = (rows // 2 + SUB, LANES)
    plain = (rows, cols)
    shapes = [plain, plain, strip, strip, lines, lines, tracer.shape, plain, plain, plain]
    return pl.pallas_call(
        column_kernel,
        in_specs=[IN_HBM] * 6,
        out_specs=[IN_VMEM] * len(shapes),
        out_shape=[jax.ShapeDtypeStruct(shape, F32) for shape in shapes],
        scratch_shapes=[
            pltpu.VMEM(plain, jnp.int32),
            pltpu.VMEM(plain, jnp.int32),
            pltpu.SemaphoreType.DMA((5,)),
            pltpu.SemaphoreType.DMA((CHUNKS,)),
        ],
        compiler_params=pltpu.CompilerParams(vmem_limit_bytes=VMEM_LIMIT),
        cost_estimate=pl.CostEstimate(
            flops=6 * tracer.size, bytes_accessed=4 * tracer.size, transcendentals=0
        ),
        name="columns",
    )(
        *(
            pltpu.with_memory_space_constraint(value, pltpu.HBM)
            for value in (tracer, land, levels, surf, flow_x, flow_y)
        )
    )


def pack_kernel(to_south, to_north, from_twin, from_other, to_twin, to_other, west, east):
    half = to_south.shape[0] - SUB
    sides = west.shape[1] // LANES
    lanes = lane_ids(SUB)
    even_x, even_y = is_even("gx"), is_even("gy")
    for r in range(0, west.shape[0], SUB):
        for h in range(sides):
            at = (pl.ds(r, SUB), pl.ds(h * LANES, LANES))
            first, second = from_twin[at], from_other[at]
            east[at] = jnp.where(even_x, first, second)
            west[at] = jnp.where(even_x, second, first)
    strips = []
    for ref in (west, east):
        zero = jnp.zeros((SUB, LANES), F32)
        ends = [pl.ds(0, LANES), pl.ds((sides - 1) * LANES, LANES)]
        values = [
            tuple(ref[pl.ds(BASE + f * SUB, SUB), span] for span in ends) for f in range(FIELDS)
        ]
        strips.append(strip_pair(zero, zero, lanes, values))
    for r in range(0, half + SUB, SUB):
        at = pl.ds(r, SUB)
        if r < half:
            low, high = to_south[at, :], to_north[at, :]
        else:
            low, high = (
                jnp.where(lanes < HALF, before, pltpu.roll(after, HALF, 1))
                for before, after in zip(*strips)
            )
        to_twin[at, :] = jnp.where(even_y, high, low)
        to_other[at, :] = jnp.where(even_y, low, high)


def pack_pass(to_south, to_north, from_twin, from_other):
    strip = jax.ShapeDtypeStruct(to_south.shape, F32)
    lines = jax.ShapeDtypeStruct(from_twin.shape, F32)
    return pl.pallas_call(
        pack_kernel,
        in_specs=[IN_VMEM] * 4,
        out_specs=[IN_VMEM] * 4,
        out_shape=[strip, strip, lines, lines],
        compiler_params=pltpu.CompilerParams(vmem_limit_bytes=VMEM_LIMIT),
        cost_estimate=pl.CostEstimate(
            flops=to_south.size, bytes_accessed=16 * to_south.size, transcendentals=0
        ),
        name="corners",
    )(to_south, to_north, from_twin, from_other)


def message_rows(ref, rows, r):
    half = rows // 2
    if r < 0:
        return ref[pl.ds(half, SUB), :]
    if r >= rows:
        return pltpu.roll(ref[pl.ds(half, SUB), :], HALF, 1)
    if r < half:
        return ref[pl.ds(r, SUB), :]
    return pltpu.roll(ref[pl.ds(r - half, SUB), :], HALF, 1)


def outer_tile(south, north, rows, r, f, open_south, open_north, lanes):
    at = BASE + (f + 1) * WIDTH
    mixed = jnp.where(lanes < at, message_rows(south, rows, r), message_rows(north, rows, r))
    mixed = put_lane(mixed, at, 0)
    valid = ((lanes < WIDTH) & open_north) | ((lanes >= LANES - WIDTH) & open_south)
    return jnp.where(valid, mixed, 0.0)


def extend(target, base, f, field, west, east, south, north, open_south, open_north):
    rows, cols = field.shape
    sides = cols // LANES
    lanes = lane_ids(SUB)
    for r in range(-SUB, rows + 1, SUB):
        to = pl.ds(SUB + r, SUB)
        for h in range(sides):
            span = pl.ds(h * LANES, LANES)
            if r < 0:
                target[h, to, :] = west[pl.ds(base + f * SUB, SUB), span]
            elif r >= rows:
                target[h, to, :] = east[pl.ds(base + f * SUB, SUB), span]
            else:
                target[h, to, :] = field[pl.ds(r, SUB), span]
        target[sides, to, :] = outer_tile(
            south, north, rows, r, f, open_south, open_north, lanes
        )


def latitude_ends():
    place, size = lax.axis_index("gy"), lax.axis_size("gy")
    return place > 0, place < size - 1


def ring_shift(tiles, lanes):
    size = len(tiles)
    after = [pltpu.roll(t, LANES - 1, 1) for t in tiles]
    before = [pltpu.roll(t, 1, 1) for t in tiles]
    nxt = [jnp.where(lanes == LANES - 1, after[(h + 1) % size], after[h]) for h in range(size)]
    prv = [jnp.where(lanes == 0, before[(h - 1) % size], before[h]) for h in range(size)]
    return nxt, prv


def nine_sum(ref, r, lanes):
    sides = [ref[h, pl.ds(r + 1, SUB), :] + ref[h, pl.ds(r - 1, SUB), :] for h in range(ref.shape[0])]
    mixed = [ref[h, pl.ds(r, SUB), :] + 0.5 * sides[h] for h in range(ref.shape[0])]
    nxt, prv = ring_shift(mixed, lanes)
    return [sides[h] + (nxt[h] + prv[h]) for h in range(ref.shape[0])]


def peak_kernel(depth, west, east, from_twin, from_other, peak, south, north, coded):
    rows, cols = depth.shape
    sides = cols // LANES
    lanes = lane_ids(SUB)
    open_south, open_north = latitude_ends()
    scale = 2.0 / (BASE // 2)
    even = is_even("gy")
    for r in range(0, south.shape[0], SUB):
        at = pl.ds(r, SUB)
        first, second = from_twin[at, :], from_other[at, :]
        north[at, :] = jnp.where(even, first, second)
        south[at, :] = jnp.where(even, second, first)
    extend(coded, BASE, 0, depth, west, east, south, north, open_south, open_north)
    for r in range(0, rows + 2 * SUB, SUB):
        for h in range(sides + 1):
            d = coded[h, pl.ds(r, SUB), :]
            coded[h, pl.ds(r, SUB), :] = d + jnp.where(d > 0, CODE, 0.0)
    best = jnp.full((SUB, LANES), 0.0, F32)
    for r in range(SUB, rows + SUB, SUB):
        sums = nine_sum(coded, r, lanes)
        for h in range(sides):
            wet, deep = decode(sums[h])
            d = depth[pl.ds(r - SUB, SUB), pl.ds(h * LANES, LANES)]
            best = jnp.maximum(best, d * wet + jnp.where(d > 0, deep, 0.0))
    best = jnp.max(jnp.max(best, axis=1, keepdims=True), axis=0, keepdims=True)
    peak[...] = jnp.broadcast_to(0.5 + scale * best, (SUB, LANES))


def decode(sums):
    wet = jnp.floor(sums * (2.0 / CODE)) * 0.5
    return wet, sums - CODE * wet


def peak_pass(depth, west, east, from_twin, from_other):
    rows, cols = depth.shape
    strip = jax.ShapeDtypeStruct(from_twin.shape, F32)
    ext = pltpu.VMEM((cols // LANES + 1, rows + 2 * SUB, LANES), F32)
    return pl.pallas_call(
        peak_kernel,
        in_specs=[IN_VMEM] * 5,
        out_specs=[IN_VMEM] * 3,
        out_shape=[jax.ShapeDtypeStruct((SUB, LANES), F32), strip, strip],
        scratch_shapes=[ext],
        compiler_params=pltpu.CompilerParams(vmem_limit_bytes=VMEM_LIMIT),
        cost_estimate=pl.CostEstimate(
            flops=30 * depth.size, bytes_accessed=4 * depth.size, transcendentals=0
        ),
        name="peak",
    )(depth, west, east, from_twin, from_other)


def around_kernel(
    part, depth, west, east, south, north, zonal_hbm, merid_hbm,
    edge_y, around, zonal, merid, masked, sem,
):
    rows, cols = depth.shape
    sides = cols // LANES
    lanes = lane_ids(SUB)
    spans = [pl.ds(h * LANES, LANES) for h in range(sides)]
    flows = flow_copies(part, zonal_hbm, merid_hbm, zonal, merid, sem)
    for copy in flows:
        copy.start()
    open_south, open_north = latitude_ends()
    for h in range(sides):
        masked[h, pl.ds(0, SUB), :] = west[pl.ds(BASE, SUB), spans[h]]
        masked[h, pl.ds(SUB, rows), :] = depth[:, spans[h]]
        masked[h, pl.ds(SUB + rows, SUB), :] = east[pl.ds(BASE, SUB), spans[h]]
    for big in range(0, rows, 2 * SUB):
        shifted = []
        for r in (big, big + SUB):
            low, high = message_rows(south, rows, r), message_rows(north, rows, r)
            edge_y[0, pl.ds(r, SUB), :] = jnp.where(open_south, low, 0.0)
            edge_y[1, pl.ds(r, SUB), :] = jnp.where(
                open_north, pltpu.roll(high, LANES - 2, 1), 0.0
            )
            tiles = [depth[pl.ds(r, SUB), span] for span in spans]
            tiles.append(outer_tile(south, north, rows, r, 0, open_south, open_north, lanes))
            shifted.append(ring_shift(tiles, lanes))
        at = pl.ds(big, 2 * SUB)
        for h in range(sides):
            around[0, h, at, :] = masked[h, pl.ds(SUB + big + 1, 2 * SUB), :].astype(BF16)
            around[1, h, at, :] = masked[h, pl.ds(SUB + big - 1, 2 * SUB), :].astype(BF16)
            for n in range(2):
                pair = jnp.concatenate([shifted[0][n][h], shifted[1][n][h]], 0)
                around[2 + n, h, at, :] = pair.astype(BF16)
    for copy in flows:
        copy.wait()


def flow_copies(part, zonal_hbm, merid_hbm, zonal, merid, sem):
    levels = pl.ds(part[0], part[1] - part[0])
    return [
        pltpu.make_async_copy(source.at[levels], target, sem.at[i])
        for i, (source, target) in enumerate(((zonal_hbm, zonal), (merid_hbm, merid)))
    ]


def in_hbm(*values):
    return [pltpu.with_memory_space_constraint(value, pltpu.HBM) for value in values]


def around_pass(part, depth, west, east, south, north, zonal, merid):
    rows, cols = depth.shape
    sides = cols // LANES
    return pl.pallas_call(
        functools.partial(around_kernel, part),
        in_specs=[IN_VMEM] * 5 + [IN_HBM] * 2,
        out_specs=[IN_VMEM] * 4,
        out_shape=[
            jax.ShapeDtypeStruct((2, rows, LANES), F32),
            jax.ShapeDtypeStruct((4, sides, rows, LANES), BF16),
        ]
        + [jax.ShapeDtypeStruct((part[1] - part[0], rows, cols), BF16)] * 2,
        scratch_shapes=[
            pltpu.VMEM((sides, rows + 2 * SUB, LANES), F32),
            pltpu.SemaphoreType.DMA((2,)),
        ],
        compiler_params=pltpu.CompilerParams(vmem_limit_bytes=VMEM_LIMIT),
        cost_estimate=pl.CostEstimate(
            flops=30 * depth.size, bytes_accessed=16 * depth.size, transcendentals=0
        ),
        name="around",
    )(depth, west, east, south, north, *in_hbm(zonal, merid))


def tracer_kernel(parts, index, tracer, zonal, merid, depth, west, east, edge_y, around, *rest):
    start, stop = parts[index]
    rest = list(rest)
    later = index + 1 < len(parts)
    flows_hbm = [rest.pop(0), rest.pop(0)] if later else []
    earlier = rest.pop(0) if index else None
    if index > 1:
        rest.pop(0)
    out = rest.pop(0)
    flows = [rest.pop(0), rest.pop(0)] if later else []
    placed = rest.pop(0) if index else None
    masked, sem = rest
    copies = []
    if later:
        copies += flow_copies(parts[index + 1], *flows_hbm, *flows, sem)
    if index:
        first, last = parts[index - 1]
        for c in range(2):
            target = placed.at[c, pl.ds(first, last - first)]
            copies.append(pltpu.make_async_copy(earlier.at[c], target, sem.at[2 + c]))
    for copy in copies:
        copy.start()
    rows, cols = depth.shape
    sides = cols // LANES
    count = BASE // 2
    lanes = lane_ids(SUB)
    spans = [pl.ds(h * LANES, LANES) for h in range(sides)]

    def one_level(level, carry):
        mark = lax.convert_element_type(level, F32)
        for c in range(2):
            line = c * count + level
            group = pl.multiple_of(lax.div(line, SUB) * SUB, SUB)
            place = lax.rem(line, SUB)
            for h in range(sides):
                before = west[pl.ds(group, SUB), spans[h]]
                masked[c, h, pl.ds(0, SUB), :] = pltpu.roll(before, SUB - 1 - place, 0)
                after = east[pl.ds(group, SUB), spans[h]]
                masked[c, h, pl.ds(SUB + rows, SUB), :] = pltpu.roll(after, lax.rem(SUB - place, SUB), 0)
        for r in range(0, rows, SUB):
            for h in range(sides):
                here = depth[pl.ds(r, SUB), spans[h]] > mark
                for c in range(2):
                    masked[c, h, pl.ds(SUB + r, SUB), :] = jnp.where(
                        here, tracer[c, level, pl.ds(r, SUB), spans[h]], 0.0
                    )
        mark_pair = jnp.full((2 * SUB, LANES), mark, F32).astype(BF16)
        one, none = jnp.ones((2 * SUB, LANES), BF16), jnp.zeros((2 * SUB, LANES), BF16)
        quarter = jnp.full((2 * SUB, LANES), 0.25, BF16)
        picks = []
        for c in range(2):
            line = c * count + level
            picks.append(((lanes >= line) & (lanes < line + HALF), lax.rem(LANES - line, LANES)))
        for big in range(0, rows, 2 * SUB):
            wide = pl.ds(big, 2 * SUB)
            pairs = []
            for h in range(sides):
                near = none
                for n in range(4):
                    near = near + jnp.where(around[n, h, wide, :] > mark_pair, one, none)
                pairs.append(
                    (
                        1.0 - 0.2 * near.astype(F32),
                        (zonal[level - start, wide, spans[h]] * quarter).astype(F32),
                        (merid[level - start, wide, spans[h]] * quarter).astype(F32),
                    )
                )
            for sub in range(2):
                r = big + sub * SUB
                at = pl.ds(r, SUB)
                part = slice(sub * SUB, (sub + 1) * SUB)
                factors = []
                for h in range(sides):
                    own, u, v = (value[part] for value in pairs[h])
                    here = depth[at, spans[h]] > mark
                    factors.append((here, own, 0.2 - u, 0.2 + u, 0.2 - v, 0.2 + v))
                for c in range(2):
                    tiles = [masked[c, h, pl.ds(SUB + r, SUB), :] for h in range(sides)]
                    pick, turn = picks[c]
                    outer = pltpu.roll(jnp.where(pick, edge_y[0, at, :], edge_y[1, at, :]), turn, 1)
                    after = [pltpu.roll(t, LANES - 1, 1) for t in tiles] + [outer]
                    before = [outer] + [pltpu.roll(t, 1, 1) for t in tiles]
                    for h in range(sides):
                        here, own, to_e, to_w, to_n, to_s = factors[h]
                        nxt = jnp.where(lanes == LANES - 1, after[h + 1], after[h])
                        prv = jnp.where(lanes == 0, before[h], before[h + 1])
                        value = own * tiles[h] + to_n * nxt + to_s * prv
                        value = value + to_e * masked[c, h, pl.ds(SUB + r + 1, SUB), :]
                        value = value + to_w * masked[c, h, pl.ds(SUB + r - 1, SUB), :]
                        out[c, level - start, at, spans[h]] = jnp.where(
                            here, value, tracer[c, level, at, spans[h]]
                        )
        return carry

    lax.fori_loop(start, stop, one_level, 0)
    for copy in copies:
        copy.wait()


def tracer_pass(parts, index, tracer, flows, depth, west, east, known, flows_hbm, earlier, placed):
    two, count, rows, cols = tracer.shape
    sides = cols // LANES
    part = parts[index][1] - parts[index][0]
    later = index + 1 < len(parts)
    operands = [tracer, *flows, depth, west, east, *known]
    specs = [IN_VMEM] * len(operands)
    shapes = [jax.ShapeDtypeStruct((two, part, rows, cols), F32)]
    outs = [IN_VMEM]
    aliases = {}
    if later:
        after = parts[index + 1][1] - parts[index + 1][0]
        operands += in_hbm(*flows_hbm)
        specs += [IN_HBM] * 2
        shapes += [jax.ShapeDtypeStruct((after, rows, cols), BF16)] * 2
        outs += [IN_VMEM] * 2
    if index:
        operands.append(earlier)
        specs.append(IN_VMEM)
        if index > 1:
            aliases = {len(operands): len(shapes)}
            operands.append(placed)
            specs.append(IN_HBM)
        shapes.append(jax.ShapeDtypeStruct(tracer.shape, F32))
        outs.append(IN_HBM)
    results = pl.pallas_call(
        functools.partial(tracer_kernel, parts, index),
        in_specs=specs,
        out_specs=outs,
        out_shape=shapes,
        scratch_shapes=[
            pltpu.VMEM((2, sides, rows + 2 * SUB, LANES), F32),
            pltpu.SemaphoreType.DMA((4,)),
        ],
        input_output_aliases=aliases,
        compiler_params=pltpu.CompilerParams(vmem_limit_bytes=VMEM_LIMIT),
        cost_estimate=pl.CostEstimate(
            flops=40 * tracer.size * part // count,
            bytes_accessed=10 * tracer.size * part // count,
            transcendentals=0,
        ),
        name="tracers",
    )(*operands)
    results = list(results)
    made = results.pop(0)
    flows = (results.pop(0), results.pop(0)) if later else ()
    return made, flows, results.pop(0) if index else None


def group_of(tiles):
    return max(n for n in range(1, 17) if tiles % n == 0)


def solve_kernel(
    last_part, tracer_in, _, peak, depth, surf, flow_x, flow_y, force, west, east, south, north,
    tracer_hbm, surf_hbm, x_hbm, y_hbm,
    surf_out, x_out, y_out, old, deep, deep_n, deep_s, coded, flux, part, ease, pairs, now, then, total, sem, out_sem,
):
    rows, cols = depth.shape
    sides = cols // LANES
    tiles = sides + 1
    lanes = lane_ids(SUB)
    scale = 2.0 / BASE
    open_south, open_north = latitude_ends()
    beyond = ((lanes < WIDTH) & open_north) | ((lanes >= LANES - WIDTH) & open_south)
    part_at = pl.ds(last_part[0], last_part[1] - last_part[0])
    outward = [
        pltpu.make_async_copy(tracer_in.at[c], tracer_hbm.at[c, part_at], sem.at[c])
        for c in range(2)
    ]
    for copy in outward:
        copy.start()

    lowest = 0.5 / peak[...]
    shrink = (1.0 - lowest) * (1.0 - lowest)
    omega = jnp.full((SUB, LANES), 2.0, F32)
    weights, change = [jnp.ones((SUB, LANES), F32)], [jnp.ones((SUB, LANES), F32)]
    for _ in range(1, ITERS):
        omega = 1.0 / (1.0 - omega * shrink * 0.25)
        resid = [1.0 - weights[0]] + [p - w for p, w in zip(weights, weights[1:])] + [weights[-1]]
        held = change + [jnp.zeros((SUB, LANES), F32)]
        change = [omega * y + (omega - 1.0) * d for y, d in zip(resid, held)]
        weights = [w + d for w, d in zip(weights + [jnp.zeros((SUB, LANES), F32)], change)]

    edge = (pl.ds(0, SUB), pl.ds(rows + 3 * SUB, SUB))
    for ref in (deep, deep_n, deep_s, coded, flux):
        for at in edge:
            for h in range(tiles):
                ref[h, at, :] = jnp.zeros((SUB, LANES), F32)
    for ref in (pairs, now, then):
        for i in range(ref.shape[0]):
            for at in edge:
                for h in range(tiles):
                    ref[i, h, at, :] = jnp.zeros((SUB, LANES), F32)

    def spread(ref, at, values):
        nxt, prv = ring_shift(values, lanes)
        for h in range(tiles):
            ref[0, h, at, :] = values[h]
            ref[1, h, at, :] = nxt[h]
            ref[2, h, at, :] = prv[h]

    def load_tile(to, field, low, high):
        def ring(f):
            at = BASE + (f + 1) * WIDTH
            outer = put_lane(jnp.where(lanes < at, low, high), at, 0)
            return [field(f, h) for h in range(sides)] + [jnp.where(beyond, outer, 0.0)]

        levels = ring(0)
        deeps = [v * scale for v in levels]
        wets = [jnp.where(v > 0, 1.0, 0.0) for v in levels]
        nxt, prv = ring_shift(deeps, lanes)
        surfs, drives = ring(1), ring(4)
        cross, crosses = ring_shift([m * v for m, v in zip(wets, ring(3))], lanes)
        along = ring(2)
        for h in range(tiles):
            deep[h, to, :] = deeps[h]
            deep_n[h, to, :] = nxt[h]
            deep_s[h, to, :] = prv[h]
            coded[h, to, :] = levels[h] + CODE * wets[h]
            old[h, to, :] = surfs[h]
            flux[h, to, :] = wets[h] * along[h]
            part[h, to, :] = 0.5 * surfs[h] + drives[h] - 0.25 * (cross[h] - crosses[h])
        spread(now, to, [m * v for m, v in zip(wets, surfs)])

    fields = (depth, surf, flow_x, flow_y, force)
    half = rows // 2
    for ref, to, turn in ((west, SUB, 0), (east, rows + 2 * SUB, HALF)):
        tail = [message[pl.ds(half, SUB), :] for message in (south, north)]
        if turn:
            tail = [pltpu.roll(v, turn, 1) for v in tail]
        load_tile(
            pl.ds(to, SUB),
            lambda f, h, ref=ref: ref[pl.ds(BASE + f * SUB, SUB), pl.ds(h * LANES, LANES)],
            *tail,
        )
    size = rows // CHUNKS

    def load_chunk(i, carry):
        upper = i >= CHUNKS // 2
        turn = jnp.where(upper, HALF, 0)
        first_row = jnp.where(upper, i - CHUNKS // 2, i) * size
        for r in range(0, size, SUB):
            at = pl.ds(pl.multiple_of(i * size + r, SUB), SUB)
            line = pl.ds(pl.multiple_of(first_row + r, SUB), SUB)
            load_tile(
                pl.ds(pl.multiple_of(i * size + r + 2 * SUB, SUB), SUB),
                lambda f, h, at=at: fields[f][at, pl.ds(h * LANES, LANES)],
                *(pltpu.roll(message[line, :], turn, 1) for message in (south, north)),
            )
        return carry

    lax.fori_loop(0, CHUNKS, load_chunk, 0)

    count = rows // SUB + 2
    group = group_of(count)

    def over_tiles(body):
        def step(i, carry):
            window = pl.ds(pl.multiple_of(i * (group * SUB), SUB), (group + 2) * SUB)

            def view(ref, *index):
                return ref.at[(*index, window, slice(None))]

            for j in range(SUB, (group + 1) * SUB, SUB):
                body(view, j)
            return carry

        lax.fori_loop(0, count // group, step, 0)

    def nine(view, source, j, near, far):
        result = []
        for h in range(tiles):
            def value(i, shift):
                return view(source, i, h)[pl.ds(j + shift, SUB), :]

            side = near[h][0] * value(0, 1) + near[h][1] * value(0, -1)
            side = side + near[h][2] * value(1, 0) + near[h][3] * value(2, 0)
            corner = far[h][0] * value(1, 1) + far[h][1] * value(1, -1)
            corner = corner + far[h][2] * value(2, 1) + far[h][3] * value(2, -1)
            result.append(side + corner)
        return result

    def prepare(view, j):
        mixed, sides_of = [], []
        for h in range(tiles):
            code = view(coded, h)
            sides_of.append(code[pl.ds(j + 1, SUB), :] + code[pl.ds(j - 1, SUB), :])
            mixed.append(code[pl.ds(j, SUB), :] + 0.5 * sides_of[h])
        nxt, prv = ring_shift(mixed, lanes)
        near, far, inverses, masks = [], [], [], []
        for h in range(tiles):
            own = view(deep, h)[pl.ds(j, SUB), :]
            wet_sum, deep_sum = decode(sides_of[h] + (nxt[h] + prv[h]))
            wet = jnp.where(own > 0, 1.0, 0.0)
            diag = 0.5 + 2.0 * (own * wet_sum + wet * (deep_sum * scale))
            inverse = 1.0 / diag
            inverses.append(inverse)
            masks.append(wet)
            ease_h = wet * inverse
            view(ease, h)[pl.ds(j, SUB), :] = ease_h
            twice = own + own
            e = twice + 2.0 * view(deep, h)[pl.ds(j + 1, SUB), :]
            w = twice + 2.0 * view(deep, h)[pl.ds(j - 1, SUB), :]
            n = twice + 2.0 * view(deep_n, h)[pl.ds(j, SUB), :]
            s = twice + 2.0 * view(deep_s, h)[pl.ds(j, SUB), :]
            ne = own + view(deep_n, h)[pl.ds(j + 1, SUB), :]
            nw = own + view(deep_n, h)[pl.ds(j - 1, SUB), :]
            se = own + view(deep_s, h)[pl.ds(j + 1, SUB), :]
            sw = own + view(deep_s, h)[pl.ds(j - 1, SUB), :]
            for i, value in enumerate((e, n, s, ne, nw, se, sw)):
                view(pairs, i, h)[pl.ds(j, SUB), :] = value
            near.append((e, w, n, s))
            far.append((ne, nw, se, sw))
        sums = nine(view, now, j, near, far)
        firsts = []
        for h in range(tiles):
            e = view(old, h)[pl.ds(j, SUB), :]
            across = view(flux, h)[pl.ds(j + 1, SUB), :] - view(flux, h)[pl.ds(j - 1, SUB), :]
            drive = view(part, h)[pl.ds(j, SUB), :] - 0.25 * across
            z = drive * inverses[h] - e + masks[h] * inverses[h] * sums[h]
            view(total, h)[pl.ds(j, SUB), :] = e + weights[0] * z
            firsts.append(masks[h] * z)
        nxt, prv = ring_shift(firsts, lanes)
        for h in range(tiles):
            for i, value in enumerate((firsts[h], nxt[h], prv[h])):
                view(then, i, h)[pl.ds(j, SUB), :] = value

    over_tiles(prepare)

    source, target = then, now
    for k in range(1, ITERS):
        def apply(view, j, k=k, source=source, target=target):
            near, far = [], []
            for h in range(tiles):
                def pair(i, shift=0):
                    return view(pairs, i, h)[pl.ds(j + shift, SUB), :]

                near.append((pair(0), pair(0, -1), pair(1), pair(2)))
                far.append((pair(3), pair(4), pair(5), pair(6)))
            sums = nine(view, source, j, near, far)
            values = [view(ease, h)[pl.ds(j, SUB), :] * sums[h] for h in range(tiles)]
            for h in range(tiles):
                here = view(total, h)
                here[pl.ds(j, SUB), :] = here[pl.ds(j, SUB), :] + weights[k] * values[h]
            if k < ITERS - 1:
                nxt, prv = ring_shift(values, lanes)
                for h in range(tiles):
                    for i, value in enumerate((values[h], nxt[h], prv[h])):
                        view(target, i, h)[pl.ds(j, SUB), :] = value

        over_tiles(apply)
        source, target = target, source

    def results(i):
        part_of = pl.ds(pl.multiple_of(i * size, SUB), size)
        return [
            pltpu.make_async_copy(
                value.at[part_of, :], place.at[part_of, :], out_sem.at[n * CHUNKS + i]
            )
            for n, (value, place) in enumerate(
                ((surf_out, surf_hbm), (x_out, x_hbm), (y_out, y_hbm))
            )
        ]

    def finish(i, carry):
        window = pl.ds(pl.multiple_of(i * size + SUB, SUB), size + 2 * SUB)
        for r in range(0, size, SUB):
            j = r + SUB
            at = pl.ds(pl.multiple_of(i * size + r, SUB), SUB)
            views = [total.at[h, window, :] for h in range(tiles)]
            here = [v[pl.ds(j, SUB), :] for v in views]
            here[sides] = jnp.where(beyond, here[sides], 0.0)
            nxt, prv = ring_shift(here, lanes)
            for h in range(sides):
                span = pl.ds(h * LANES, LANES)
                wet = depth[at, span] > 0
                slope = views[h][pl.ds(j + 1, SUB), :] - views[h][pl.ds(j - 1, SUB), :]
                surf_out[at, span] = here[h]
                x_out[at, span] = jnp.where(wet, flow_x[at, span] - 0.25 * slope, 0.0)
                y_out[at, span] = jnp.where(
                    wet, flow_y[at, span] - 0.25 * (nxt[h] - prv[h]), 0.0
                )
        for copy in results(i):
            copy.start()
        return carry

    lax.fori_loop(0, CHUNKS, finish, 0)
    for i in range(CHUNKS):
        for copy in results(i):
            copy.wait()
    for copy in outward:
        copy.wait()


def solve_pass(last_part, made, placed, peak, depth, surf, flow_x, flow_y, force, west, east, south, north):
    rows, cols = depth.shape
    shape = (cols // LANES + 1, rows + 4 * SUB, LANES)
    ext = pltpu.VMEM(shape, F32)
    three = pltpu.VMEM((3, *shape), F32)
    plain = jax.ShapeDtypeStruct((rows, cols), F32)
    return pl.pallas_call(
        functools.partial(solve_kernel, last_part),
        in_specs=[IN_VMEM, IN_HBM] + [IN_VMEM] * 10,
        out_specs=[IN_HBM] * 4,
        out_shape=[jax.ShapeDtypeStruct(placed.shape, F32)] + [plain] * 3,
        input_output_aliases={1: 0},
        scratch_shapes=[pltpu.VMEM((rows, cols), F32)] * 3
        + [ext] * 8
        + [pltpu.VMEM((7, *shape), F32), three, three, ext]
        + [pltpu.SemaphoreType.DMA((2,)), pltpu.SemaphoreType.DMA((3 * CHUNKS,))],
        compiler_params=pltpu.CompilerParams(vmem_limit_bytes=VMEM_LIMIT),
        cost_estimate=pl.CostEstimate(
            flops=200 * depth.size, bytes_accessed=32 * depth.size, transcendentals=0
        ),
        name="solve",
    )(made, placed, peak, depth, surf, flow_x, flow_y, force, west, east, south, north)


def twin_pairs(axis):
    return [(i, i ^ 1) for i in range(lax.axis_size(axis))]


def other_x_pairs():
    size = lax.axis_size("gx")
    return [(i, (i + 1 if i % 2 else i - 1) % size) for i in range(size)]


def other_y_pairs():
    size_x, size_y = lax.axis_size("gx"), lax.axis_size("gy")
    pairs = []
    for i in range(size_x):
        for j in range(size_y):
            if j in (0, size_y - 1):
                target = (i ^ 1, j)
            else:
                target = (i, j + 1 if j % 2 else j - 1)
            pairs.append((i * size_y + j, target[0] * size_y + target[1]))
    return pairs


def spread_rounds(axis):
    size = lax.axis_size(axis)
    reach = 1
    while reach < size:
        if size & (size - 1) == 0:
            yield axis, [(i, i ^ reach) for i in range(size)]
        else:
            yield axis, [(i, (i + reach) % size) for i in range(size)]
        reach *= 2


def local(
    tracer, zonal_flow, meridional_flow, surface_prev, transport_x, transport_y, land_mask, levels
):
    count = tracer.shape[1]
    (
        force, depth, to_south, to_north, to_twin, to_other,
        tracer, surface_prev, transport_x, transport_y,
    ) = column_pass(tracer, land_mask, levels, surface_prev, transport_x, transport_y)
    from_other = lax.ppermute(to_other, "gx", other_x_pairs())
    from_twin = lax.ppermute(to_twin, "gx", twin_pairs("gx"))
    to_twin, to_other, west, east = pack_pass(to_south, to_north, from_twin, from_other)
    from_twin = lax.ppermute(to_twin, "gy", twin_pairs("gy"))
    from_other = lax.ppermute(to_other, ("gx", "gy"), other_y_pairs())
    peak, south, north = peak_pass(depth, west, east, from_twin, from_other)
    halo = (west, east, south, north)
    rounds = [r for axis in ("gx", "gy") for r in spread_rounds(axis)]
    cuts = [count * i // PARTS for i in range(PARTS + 1)]
    parts = tuple(zip(cuts, cuts[1:]))
    flows_hbm = (zonal_flow, meridional_flow)
    first = len(rounds) - PARTS
    known, flows, made, placed = (), (), None, None
    for turn, (axis, pairs) in enumerate(rounds):
        moved = lax.ppermute(peak, axis, pairs)
        if turn == 0:
            *known, zonal, merid = around_pass(parts[0], depth, *halo, *flows_hbm)
            moved, known, flows = lax.optimization_barrier((moved, known, (zonal, merid)))
        if turn >= first:
            made, flows, placed = tracer_pass(
                parts, turn - first, tracer, flows, depth, west, east, known, flows_hbm, made, placed
            )
        peak = jnp.maximum(peak, moved)
        if first <= turn < len(rounds) - 1:
            peak, made, flows = lax.optimization_barrier((peak, made, flows))
    return solve_pass(
        parts[-1], made, placed, peak, depth, surface_prev, transport_x, transport_y, force, *halo
    )


def solution(mesh):
    cell = P("gx", "gy")
    level = P(None, "gx", "gy")
    stack = P(None, None, "gx", "gy")
    return jax.shard_map(
        local,
        mesh=mesh,
        in_specs=(stack, level, level, cell, cell, cell, cell, cell),
        out_specs=(stack, cell, cell, cell),
        check_vma=False,
    )
```

```python
import functools

import jax
import jax.numpy as jnp
from jax import lax
from jax.experimental import pallas as pl
from jax.experimental.pallas import tpu as pltpu
from jax.sharding import PartitionSpec as P

ITERS = 4
WIDTH = ITERS + 1
LANES = 128
SUB = 8
HALF = LANES // 2
FIELDS = 5
F32 = jnp.float32
BF16 = jnp.bfloat16
VMEM_LIMIT = 12 * 1024 * 1024
LEVELS = 16
BASE = 2 * LEVELS
CODE = 1024.0
PARTS = 4
CHUNKS = 4


def lane_ids(rows):
    return lax.broadcasted_iota(jnp.int32, (rows, LANES), 1)


def put_lane(value, source, target):
    shift = (target - source) % LANES
    return pltpu.roll(value, shift, 1) if shift else value


def strip_pair(low, high, lanes, values):
    for f, (begin, end) in enumerate(values):
        at = BASE + (f + 1) * WIDTH
        turned = put_lane(jnp.where(lanes < HALF, begin, end), 0, at)
        low = jnp.where((lanes >= at) & (lanes < at + WIDTH), turned, low)
        high = jnp.where((lanes >= at - WIDTH) & (lanes < at), turned, high)
    return low, high


def column_kernel(
    tracer_hbm, land_hbm, levels_hbm, surf_hbm, flow_x_hbm, flow_y_hbm,
    force, depth, to_twin, to_other, tracer, surf, flow_x, flow_y,
    land, levels, flat_sem, chunk_sem,
):
    count = tracer.shape[1]
    rows, cols = land.shape
    sides = cols // LANES
    base = 2 * count
    size = rows // CHUNKS

    def copy_in(i):
        part = pl.ds(pl.multiple_of(i * size, SUB), size)
        return pltpu.make_async_copy(
            tracer_hbm.at[:, :, part, :], tracer.at[:, :, part, :], chunk_sem.at[i]
        )

    flats = [
        pltpu.make_async_copy(source, target, flat_sem.at[i])
        for i, (source, target) in enumerate(
            (
                (land_hbm, land),
                (levels_hbm, levels),
                (surf_hbm, surf),
                (flow_x_hbm, flow_x),
                (flow_y_hbm, flow_y),
            )
        )
    ]
    for copy in flats:
        copy.start()
    for i in range(CHUNKS):
        copy_in(i).start()
    for copy in flats:
        copy.wait()

    def chunk(i, carry):
        copy_in(i).wait()
        for r in range(0, size, SUB):
            at = pl.ds(pl.multiple_of(i * size + r, SUB), SUB)
            for h in range(sides):
                span = pl.ds(h * LANES, LANES)
                deep = (land[at, span] * levels[at, span]).astype(F32)
                total = jnp.zeros((SUB, LANES), F32)
                for k in range(count):
                    gain = jnp.maximum(deep - k, 0.0)
                    total = total + gain * (
                        tracer[0, k, at, span] - 0.75 * tracer[1, k, at, span]
                    )
                force[at, span] = total * (0.8 / count)
                depth[at, span] = deep
        return carry

    lax.fori_loop(0, CHUNKS, chunk, 0)

    def edge_rows(out, line, tile):
        for h in range(sides):
            span = pl.ds(h * LANES, LANES)
            deep = depth[pl.ds(line, 1), span]
            for c in range(2):
                for k in range(count):
                    out[pl.ds(c * count + k, 1), span] = jnp.where(
                        deep > k, tracer[c, k, pl.ds(line, 1), span], 0.0
                    )
            for f, ref in enumerate((depth, surf, flow_x, flow_y, force)):
                out[pl.ds(base + f * SUB, SUB), span] = ref[pl.ds(tile, SUB), span]

    even = is_even("gx")

    @pl.when(even)
    def _():
        edge_rows(to_twin, rows - 1, rows - SUB)
        edge_rows(to_other, 0, 0)

    @pl.when(jnp.logical_not(even))
    def _():
        edge_rows(to_twin, 0, 0)
        edge_rows(to_other, rows - 1, rows - SUB)


def is_even(axis):
    return lax.rem(lax.axis_index(axis), 2) == 0


IN_HBM = pl.BlockSpec(memory_space=pltpu.HBM)
IN_VMEM = pl.BlockSpec(memory_space=pltpu.VMEM)


def column_pass(tracer, land, levels, surf, flow_x, flow_y):
    two, count, rows, cols = tracer.shape
    lines = (two * count + FIELDS * SUB, cols)
    plain = (rows, cols)
    shapes = [plain, plain, lines, lines, tracer.shape, plain, plain, plain]
    return pl.pallas_call(
        column_kernel,
        in_specs=[IN_HBM] * 6,
        out_specs=[IN_VMEM] * len(shapes),
        out_shape=[jax.ShapeDtypeStruct(shape, F32) for shape in shapes],
        scratch_shapes=[
            pltpu.VMEM(plain, jnp.int32),
            pltpu.VMEM(plain, jnp.int32),
            pltpu.SemaphoreType.DMA((5,)),
            pltpu.SemaphoreType.DMA((CHUNKS,)),
        ],
        compiler_params=pltpu.CompilerParams(vmem_limit_bytes=VMEM_LIMIT),
        cost_estimate=pl.CostEstimate(
            flops=6 * tracer.size, bytes_accessed=4 * tracer.size, transcendentals=0
        ),
        name="columns",
    )(
        *(
            pltpu.with_memory_space_constraint(value, pltpu.HBM)
            for value in (tracer, land, levels, surf, flow_x, flow_y)
        )
    )


def strip_kernel(
    tracer, depth, surf, flow_x, flow_y, force, zonal_hbm, merid_hbm,
    to_south, to_north, zonal, merid, sem,
):
    flows = [
        pltpu.make_async_copy(source, target, sem.at[i])
        for i, (source, target) in enumerate(((zonal_hbm, zonal), (merid_hbm, merid)))
    ]
    for copy in flows:
        copy.start()
    count = tracer.shape[1]
    rows, cols = depth.shape
    base = 2 * count
    lanes = lane_ids(SUB)
    size = rows // CHUNKS
    low_kind = jnp.where((lanes >= 1) & (lanes <= base), lax.rem(lanes - 1 + count, count), -1)
    low_kind = low_kind.astype(F32)
    high_kind = jnp.where(lanes < base, lax.rem(lanes, count), -1).astype(F32)
    odd = (lanes & 1) == 1
    ends = [pl.ds(0, LANES), pl.ds(cols - LANES, LANES)]

    def chunk(i, carry):
        upper = i >= CHUNKS // 2
        turn = jnp.where(upper, HALF, 0)
        keep = (lanes < HALF) & upper
        first_row = jnp.where(upper, i - CHUNKS // 2, i) * size
        for r in range(0, size, SUB):
            at = pl.ds(pl.multiple_of(i * size + r, SUB), SUB)
            packed = [jnp.zeros((SUB, LANES), F32)] * 2
            for line in range(base):
                c, k = divmod(line, count)
                both = jnp.where(lanes < HALF, tracer[c, k, at, ends[0]], tracer[c, k, at, ends[1]])
                both = put_lane(both, 0, line + 1)
                packed[line % 2] = jnp.where(
                    (lanes == line) | (lanes == line + 1), both, packed[line % 2]
                )
            pairs = [
                tuple(ref[at, span] for span in ends)
                for ref in (depth, surf, flow_x, flow_y, force)
            ]
            low = jnp.where(odd, packed[0], packed[1])
            high = jnp.where(odd, packed[1], packed[0])
            low = jnp.where(pairs[0][0][:, 0:1] > low_kind, low, 0.0)
            high = jnp.where(pairs[0][1][:, LANES - 1 : LANES] > high_kind, high, 0.0)
            low, high = strip_pair(low, high, lanes, pairs)
            to = pl.ds(pl.multiple_of(first_row + r, SUB), SUB)
            for out, value in ((to_south, low), (to_north, high)):
                out[to, :] = jnp.where(keep, out[to, :], pltpu.roll(value, turn, 1))
        return carry

    lax.fori_loop(0, CHUNKS, chunk, 0)
    for out in (to_south, to_north):
        out[pl.ds(rows // 2, SUB), :] = jnp.zeros((SUB, LANES), F32)
    for copy in flows:
        copy.wait()


def strip_pass(zonal, merid, tracer, depth, surf, flow_x, flow_y, force):
    shape = jax.ShapeDtypeStruct((depth.shape[0] // 2 + SUB, LANES), F32)
    return pl.pallas_call(
        strip_kernel,
        in_specs=[IN_VMEM] * 6 + [IN_HBM] * 2,
        out_specs=[IN_VMEM] * 4,
        out_shape=[shape, shape]
        + [jax.ShapeDtypeStruct(value.shape, BF16) for value in (zonal, merid)],
        scratch_shapes=[pltpu.SemaphoreType.DMA((2,))],
        compiler_params=pltpu.CompilerParams(vmem_limit_bytes=VMEM_LIMIT),
        cost_estimate=pl.CostEstimate(
            flops=6 * tracer.size, bytes_accessed=4 * tracer.size, transcendentals=0
        ),
        name="strips",
    )(
        tracer, depth, surf, flow_x, flow_y, force,
        *(pltpu.with_memory_space_constraint(value, pltpu.HBM) for value in (zonal, merid)),
    )


def pack_kernel(to_south, to_north, from_twin, from_other, to_twin, to_other, west, east):
    half = to_south.shape[0] - SUB
    sides = west.shape[1] // LANES
    lanes = lane_ids(SUB)
    even_x, even_y = is_even("gx"), is_even("gy")
    for r in range(0, west.shape[0], SUB):
        for h in range(sides):
            at = (pl.ds(r, SUB), pl.ds(h * LANES, LANES))
            first, second = from_twin[at], from_other[at]
            east[at] = jnp.where(even_x, first, second)
            west[at] = jnp.where(even_x, second, first)
    strips = []
    for ref in (west, east):
        zero = jnp.zeros((SUB, LANES), F32)
        ends = [pl.ds(0, LANES), pl.ds((sides - 1) * LANES, LANES)]
        values = [
            tuple(ref[pl.ds(BASE + f * SUB, SUB), span] for span in ends) for f in range(FIELDS)
        ]
        strips.append(strip_pair(zero, zero, lanes, values))
    for r in range(0, half + SUB, SUB):
        at = pl.ds(r, SUB)
        if r < half:
            low, high = to_south[at, :], to_north[at, :]
        else:
            low, high = (
                jnp.where(lanes < HALF, before, pltpu.roll(after, HALF, 1))
                for before, after in zip(*strips)
            )
        to_twin[at, :] = jnp.where(even_y, high, low)
        to_other[at, :] = jnp.where(even_y, low, high)


def pack_pass(to_south, to_north, from_twin, from_other):
    strip = jax.ShapeDtypeStruct(to_south.shape, F32)
    lines = jax.ShapeDtypeStruct(from_twin.shape, F32)
    return pl.pallas_call(
        pack_kernel,
        in_specs=[IN_VMEM] * 4,
        out_specs=[IN_VMEM] * 4,
        out_shape=[strip, strip, lines, lines],
        compiler_params=pltpu.CompilerParams(vmem_limit_bytes=VMEM_LIMIT),
        cost_estimate=pl.CostEstimate(
            flops=to_south.size, bytes_accessed=16 * to_south.size, transcendentals=0
        ),
        name="corners",
    )(to_south, to_north, from_twin, from_other)


def message_rows(ref, rows, r):
    half = rows // 2
    if r < 0:
        return ref[pl.ds(half, SUB), :]
    if r >= rows:
        return pltpu.roll(ref[pl.ds(half, SUB), :], HALF, 1)
    if r < half:
        return ref[pl.ds(r, SUB), :]
    return pltpu.roll(ref[pl.ds(r - half, SUB), :], HALF, 1)


def outer_tile(south, north, rows, r, f, open_south, open_north, lanes):
    at = BASE + (f + 1) * WIDTH
    mixed = jnp.where(lanes < at, message_rows(south, rows, r), message_rows(north, rows, r))
    mixed = put_lane(mixed, at, 0)
    valid = ((lanes < WIDTH) & open_north) | ((lanes >= LANES - WIDTH) & open_south)
    return jnp.where(valid, mixed, 0.0)


def extend(target, base, f, field, west, east, south, north, open_south, open_north):
    rows, cols = field.shape
    sides = cols // LANES
    lanes = lane_ids(SUB)
    for r in range(-SUB, rows + 1, SUB):
        to = pl.ds(SUB + r, SUB)
        for h in range(sides):
            span = pl.ds(h * LANES, LANES)
            if r < 0:
                target[h, to, :] = west[pl.ds(base + f * SUB, SUB), span]
            elif r >= rows:
                target[h, to, :] = east[pl.ds(base + f * SUB, SUB), span]
            else:
                target[h, to, :] = field[pl.ds(r, SUB), span]
        target[sides, to, :] = outer_tile(
            south, north, rows, r, f, open_south, open_north, lanes
        )


def latitude_ends():
    place, size = lax.axis_index("gy"), lax.axis_size("gy")
    return place > 0, place < size - 1


def ring_shift(tiles, lanes):
    size = len(tiles)
    after = [pltpu.roll(t, LANES - 1, 1) for t in tiles]
    before = [pltpu.roll(t, 1, 1) for t in tiles]
    nxt = [jnp.where(lanes == LANES - 1, after[(h + 1) % size], after[h]) for h in range(size)]
    prv = [jnp.where(lanes == 0, before[(h - 1) % size], before[h]) for h in range(size)]
    return nxt, prv


def nine_sum(ref, r, lanes):
    sides = [ref[h, pl.ds(r + 1, SUB), :] + ref[h, pl.ds(r - 1, SUB), :] for h in range(ref.shape[0])]
    mixed = [ref[h, pl.ds(r, SUB), :] + 0.5 * sides[h] for h in range(ref.shape[0])]
    nxt, prv = ring_shift(mixed, lanes)
    return [sides[h] + (nxt[h] + prv[h]) for h in range(ref.shape[0])]


def peak_kernel(depth, west, east, from_twin, from_other, peak, south, north, coded):
    rows, cols = depth.shape
    sides = cols // LANES
    lanes = lane_ids(SUB)
    open_south, open_north = latitude_ends()
    scale = 2.0 / (BASE // 2)
    even = is_even("gy")
    for r in range(0, south.shape[0], SUB):
        at = pl.ds(r, SUB)
        first, second = from_twin[at, :], from_other[at, :]
        north[at, :] = jnp.where(even, first, second)
        south[at, :] = jnp.where(even, second, first)
    extend(coded, BASE, 0, depth, west, east, south, north, open_south, open_north)
    for r in range(0, rows + 2 * SUB, SUB):
        for h in range(sides + 1):
            d = coded[h, pl.ds(r, SUB), :]
            coded[h, pl.ds(r, SUB), :] = d + jnp.where(d > 0, CODE, 0.0)
    best = jnp.full((SUB, LANES), 0.0, F32)
    for r in range(SUB, rows + SUB, SUB):
        sums = nine_sum(coded, r, lanes)
        for h in range(sides):
            wet, deep = decode(sums[h])
            d = depth[pl.ds(r - SUB, SUB), pl.ds(h * LANES, LANES)]
            best = jnp.maximum(best, d * wet + jnp.where(d > 0, deep, 0.0))
    best = jnp.max(jnp.max(best, axis=1, keepdims=True), axis=0, keepdims=True)
    peak[...] = jnp.broadcast_to(0.5 + scale * best, (SUB, LANES))


def decode(sums):
    wet = jnp.floor(sums * (2.0 / CODE)) * 0.5
    return wet, sums - CODE * wet


def peak_pass(depth, west, east, from_twin, from_other):
    rows, cols = depth.shape
    strip = jax.ShapeDtypeStruct(from_twin.shape, F32)
    ext = pltpu.VMEM((cols // LANES + 1, rows + 2 * SUB, LANES), F32)
    return pl.pallas_call(
        peak_kernel,
        in_specs=[IN_VMEM] * 5,
        out_specs=[IN_VMEM] * 3,
        out_shape=[jax.ShapeDtypeStruct((SUB, LANES), F32), strip, strip],
        scratch_shapes=[ext],
        compiler_params=pltpu.CompilerParams(vmem_limit_bytes=VMEM_LIMIT),
        cost_estimate=pl.CostEstimate(
            flops=30 * depth.size, bytes_accessed=4 * depth.size, transcendentals=0
        ),
        name="peak",
    )(depth, west, east, from_twin, from_other)


def around_kernel(depth, west, east, south, north, edge_y, around, masked):
    rows, cols = depth.shape
    sides = cols // LANES
    lanes = lane_ids(SUB)
    spans = [pl.ds(h * LANES, LANES) for h in range(sides)]
    open_south, open_north = latitude_ends()
    for h in range(sides):
        masked[h, pl.ds(0, SUB), :] = west[pl.ds(BASE, SUB), spans[h]]
        masked[h, pl.ds(SUB, rows), :] = depth[:, spans[h]]
        masked[h, pl.ds(SUB + rows, SUB), :] = east[pl.ds(BASE, SUB), spans[h]]
    for big in range(0, rows, 2 * SUB):
        shifted = []
        for r in (big, big + SUB):
            low, high = message_rows(south, rows, r), message_rows(north, rows, r)
            edge_y[0, pl.ds(r, SUB), :] = jnp.where(open_south, low, 0.0)
            edge_y[1, pl.ds(r, SUB), :] = jnp.where(
                open_north, pltpu.roll(high, LANES - 2, 1), 0.0
            )
            tiles = [depth[pl.ds(r, SUB), span] for span in spans]
            tiles.append(outer_tile(south, north, rows, r, 0, open_south, open_north, lanes))
            shifted.append(ring_shift(tiles, lanes))
        at = pl.ds(big, 2 * SUB)
        for h in range(sides):
            around[0, h, at, :] = masked[h, pl.ds(SUB + big + 1, 2 * SUB), :].astype(BF16)
            around[1, h, at, :] = masked[h, pl.ds(SUB + big - 1, 2 * SUB), :].astype(BF16)
            for n in range(2):
                pair = jnp.concatenate([shifted[0][n][h], shifted[1][n][h]], 0)
                around[2 + n, h, at, :] = pair.astype(BF16)


def around_pass(depth, west, east, south, north):
    rows, cols = depth.shape
    sides = cols // LANES
    return pl.pallas_call(
        around_kernel,
        in_specs=[IN_VMEM] * 5,
        out_specs=[IN_VMEM] * 2,
        out_shape=[
            jax.ShapeDtypeStruct((2, rows, LANES), F32),
            jax.ShapeDtypeStruct((4, sides, rows, LANES), BF16),
        ],
        scratch_shapes=[pltpu.VMEM((sides, rows + 2 * SUB, LANES), F32)],
        compiler_params=pltpu.CompilerParams(vmem_limit_bytes=VMEM_LIMIT),
        cost_estimate=pl.CostEstimate(
            flops=30 * depth.size, bytes_accessed=16 * depth.size, transcendentals=0
        ),
        name="around",
    )(depth, west, east, south, north)


def tracer_kernel(parts, index, tracer, zonal, merid, depth, west, east, edge_y, around, *rest):
    start, stop = parts[index]
    copies = []
    if index:
        earlier, placed = rest[0], rest[-3]
        first, last = parts[index - 1]
        for c in range(2):
            target = placed.at[c, pl.ds(first, last - first)]
            copies.append(pltpu.make_async_copy(earlier.at[c], target, rest[-1].at[c]))
    out, masked = rest[-4 if index else -3], rest[-2]
    for copy in copies:
        copy.start()
    rows, cols = depth.shape
    sides = cols // LANES
    count = BASE // 2
    lanes = lane_ids(SUB)
    spans = [pl.ds(h * LANES, LANES) for h in range(sides)]

    def one_level(level, carry):
        mark = lax.convert_element_type(level, F32)
        for c in range(2):
            line = c * count + level
            group = pl.multiple_of(lax.div(line, SUB) * SUB, SUB)
            place = lax.rem(line, SUB)
            for h in range(sides):
                before = west[pl.ds(group, SUB), spans[h]]
                masked[c, h, pl.ds(0, SUB), :] = pltpu.roll(before, SUB - 1 - place, 0)
                after = east[pl.ds(group, SUB), spans[h]]
                masked[c, h, pl.ds(SUB + rows, SUB), :] = pltpu.roll(after, lax.rem(SUB - place, SUB), 0)
        for r in range(0, rows, SUB):
            for h in range(sides):
                here = depth[pl.ds(r, SUB), spans[h]] > mark
                for c in range(2):
                    masked[c, h, pl.ds(SUB + r, SUB), :] = jnp.where(
                        here, tracer[c, level, pl.ds(r, SUB), spans[h]], 0.0
                    )
        mark_pair = jnp.full((2 * SUB, LANES), mark, F32).astype(BF16)
        one, none = jnp.ones((2 * SUB, LANES), BF16), jnp.zeros((2 * SUB, LANES), BF16)
        quarter = jnp.full((2 * SUB, LANES), 0.25, BF16)
        picks = []
        for c in range(2):
            line = c * count + level
            picks.append(((lanes >= line) & (lanes < line + HALF), lax.rem(LANES - line, LANES)))
        for big in range(0, rows, 2 * SUB):
            wide = pl.ds(big, 2 * SUB)
            pairs = []
            for h in range(sides):
                near = none
                for n in range(4):
                    near = near + jnp.where(around[n, h, wide, :] > mark_pair, one, none)
                pairs.append(
                    (
                        1.0 - 0.2 * near.astype(F32),
                        (zonal[level, wide, spans[h]] * quarter).astype(F32),
                        (merid[level, wide, spans[h]] * quarter).astype(F32),
                    )
                )
            for sub in range(2):
                r = big + sub * SUB
                at = pl.ds(r, SUB)
                part = slice(sub * SUB, (sub + 1) * SUB)
                factors = []
                for h in range(sides):
                    own, u, v = (value[part] for value in pairs[h])
                    here = depth[at, spans[h]] > mark
                    factors.append((here, own, 0.2 - u, 0.2 + u, 0.2 - v, 0.2 + v))
                for c in range(2):
                    tiles = [masked[c, h, pl.ds(SUB + r, SUB), :] for h in range(sides)]
                    pick, turn = picks[c]
                    outer = pltpu.roll(jnp.where(pick, edge_y[0, at, :], edge_y[1, at, :]), turn, 1)
                    after = [pltpu.roll(t, LANES - 1, 1) for t in tiles] + [outer]
                    before = [outer] + [pltpu.roll(t, 1, 1) for t in tiles]
                    for h in range(sides):
                        here, own, to_e, to_w, to_n, to_s = factors[h]
                        nxt = jnp.where(lanes == LANES - 1, after[h + 1], after[h])
                        prv = jnp.where(lanes == 0, before[h], before[h + 1])
                        value = own * tiles[h] + to_n * nxt + to_s * prv
                        value = value + to_e * masked[c, h, pl.ds(SUB + r + 1, SUB), :]
                        value = value + to_w * masked[c, h, pl.ds(SUB + r - 1, SUB), :]
                        out[c, level - start, at, spans[h]] = jnp.where(
                            here, value, tracer[c, level, at, spans[h]]
                        )
        return carry

    lax.fori_loop(start, stop, one_level, 0)
    for copy in copies:
        copy.wait()


def tracer_pass(parts, index, tracer, zonal, merid, depth, west, east, known, earlier, placed):
    two, count, rows, cols = tracer.shape
    sides = cols // LANES
    part = parts[index][1] - parts[index][0]
    operands = [tracer, zonal, merid, depth, west, east, *known]
    specs = [IN_VMEM] * len(operands)
    shapes = [jax.ShapeDtypeStruct((two, part, rows, cols), F32)]
    outs = [IN_VMEM]
    aliases = {}
    if index:
        operands.append(earlier)
        specs.append(IN_VMEM)
        if index > 1:
            aliases = {len(operands): len(shapes)}
            operands.append(placed)
            specs.append(IN_HBM)
        shapes.append(jax.ShapeDtypeStruct(tracer.shape, F32))
        outs.append(IN_HBM)
    results = pl.pallas_call(
        functools.partial(tracer_kernel, parts, index),
        in_specs=specs,
        out_specs=outs,
        out_shape=shapes,
        scratch_shapes=[
            pltpu.VMEM((2, sides, rows + 2 * SUB, LANES), F32),
            pltpu.SemaphoreType.DMA((2,)),
        ],
        input_output_aliases=aliases,
        compiler_params=pltpu.CompilerParams(vmem_limit_bytes=VMEM_LIMIT),
        cost_estimate=pl.CostEstimate(
            flops=40 * tracer.size * part // count,
            bytes_accessed=10 * tracer.size * part // count,
            transcendentals=0,
        ),
        name="tracers",
    )(*operands)
    return results if index else (results[0], None)


def group_of(tiles):
    return max(n for n in range(1, 17) if tiles % n == 0)


def solve_kernel(
    last_part, tracer_in, _, peak, depth, surf, flow_x, flow_y, force, west, east, south, north,
    tracer_hbm, surf_hbm, x_hbm, y_hbm,
    surf_out, x_out, y_out, old, deep, deep_n, deep_s, coded, flux, part, ease, pairs, now, then, total, sem, out_sem,
):
    rows, cols = depth.shape
    sides = cols // LANES
    tiles = sides + 1
    lanes = lane_ids(SUB)
    scale = 2.0 / BASE
    open_south, open_north = latitude_ends()
    beyond = ((lanes < WIDTH) & open_north) | ((lanes >= LANES - WIDTH) & open_south)
    part_at = pl.ds(last_part[0], last_part[1] - last_part[0])
    outward = [
        pltpu.make_async_copy(tracer_in.at[c], tracer_hbm.at[c, part_at], sem.at[c])
        for c in range(2)
    ]
    for copy in outward:
        copy.start()

    lowest = 0.5 / peak[...]
    shrink = (1.0 - lowest) * (1.0 - lowest)
    omega = jnp.full((SUB, LANES), 2.0, F32)
    weights, change = [jnp.ones((SUB, LANES), F32)], [jnp.ones((SUB, LANES), F32)]
    for _ in range(1, ITERS):
        omega = 1.0 / (1.0 - omega * shrink * 0.25)
        resid = [1.0 - weights[0]] + [p - w for p, w in zip(weights, weights[1:])] + [weights[-1]]
        held = change + [jnp.zeros((SUB, LANES), F32)]
        change = [omega * y + (omega - 1.0) * d for y, d in zip(resid, held)]
        weights = [w + d for w, d in zip(weights + [jnp.zeros((SUB, LANES), F32)], change)]

    edge = (pl.ds(0, SUB), pl.ds(rows + 3 * SUB, SUB))
    for ref in (deep, deep_n, deep_s, coded, flux):
        for at in edge:
            for h in range(tiles):
                ref[h, at, :] = jnp.zeros((SUB, LANES), F32)
    for ref in (pairs, now, then):
        for i in range(ref.shape[0]):
            for at in edge:
                for h in range(tiles):
                    ref[i, h, at, :] = jnp.zeros((SUB, LANES), F32)

    def spread(ref, at, values):
        nxt, prv = ring_shift(values, lanes)
        for h in range(tiles):
            ref[0, h, at, :] = values[h]
            ref[1, h, at, :] = nxt[h]
            ref[2, h, at, :] = prv[h]

    def load_tile(to, field, low, high):
        def ring(f):
            at = BASE + (f + 1) * WIDTH
            outer = put_lane(jnp.where(lanes < at, low, high), at, 0)
            return [field(f, h) for h in range(sides)] + [jnp.where(beyond, outer, 0.0)]

        levels = ring(0)
        deeps = [v * scale for v in levels]
        wets = [jnp.where(v > 0, 1.0, 0.0) for v in levels]
        nxt, prv = ring_shift(deeps, lanes)
        surfs, drives = ring(1), ring(4)
        cross, crosses = ring_shift([m * v for m, v in zip(wets, ring(3))], lanes)
        along = ring(2)
        for h in range(tiles):
            deep[h, to, :] = deeps[h]
            deep_n[h, to, :] = nxt[h]
            deep_s[h, to, :] = prv[h]
            coded[h, to, :] = levels[h] + CODE * wets[h]
            old[h, to, :] = surfs[h]
            flux[h, to, :] = wets[h] * along[h]
            part[h, to, :] = 0.5 * surfs[h] + drives[h] - 0.25 * (cross[h] - crosses[h])
        spread(now, to, [m * v for m, v in zip(wets, surfs)])

    fields = (depth, surf, flow_x, flow_y, force)
    half = rows // 2
    for ref, to, turn in ((west, SUB, 0), (east, rows + 2 * SUB, HALF)):
        tail = [message[pl.ds(half, SUB), :] for message in (south, north)]
        if turn:
            tail = [pltpu.roll(v, turn, 1) for v in tail]
        load_tile(
            pl.ds(to, SUB),
            lambda f, h, ref=ref: ref[pl.ds(BASE + f * SUB, SUB), pl.ds(h * LANES, LANES)],
            *tail,
        )
    size = rows // CHUNKS

    def load_chunk(i, carry):
        upper = i >= CHUNKS // 2
        turn = jnp.where(upper, HALF, 0)
        first_row = jnp.where(upper, i - CHUNKS // 2, i) * size
        for r in range(0, size, SUB):
            at = pl.ds(pl.multiple_of(i * size + r, SUB), SUB)
            line = pl.ds(pl.multiple_of(first_row + r, SUB), SUB)
            load_tile(
                pl.ds(pl.multiple_of(i * size + r + 2 * SUB, SUB), SUB),
                lambda f, h, at=at: fields[f][at, pl.ds(h * LANES, LANES)],
                *(pltpu.roll(message[line, :], turn, 1) for message in (south, north)),
            )
        return carry

    lax.fori_loop(0, CHUNKS, load_chunk, 0)

    count = rows // SUB + 2
    group = group_of(count)

    def over_tiles(body):
        def step(i, carry):
            window = pl.ds(pl.multiple_of(i * (group * SUB), SUB), (group + 2) * SUB)

            def view(ref, *index):
                return ref.at[(*index, window, slice(None))]

            for j in range(SUB, (group + 1) * SUB, SUB):
                body(view, j)
            return carry

        lax.fori_loop(0, count // group, step, 0)

    def nine(view, source, j, near, far):
        result = []
        for h in range(tiles):
            def value(i, shift):
                return view(source, i, h)[pl.ds(j + shift, SUB), :]

            side = near[h][0] * value(0, 1) + near[h][1] * value(0, -1)
            side = side + near[h][2] * value(1, 0) + near[h][3] * value(2, 0)
            corner = far[h][0] * value(1, 1) + far[h][1] * value(1, -1)
            corner = corner + far[h][2] * value(2, 1) + far[h][3] * value(2, -1)
            result.append(side + corner)
        return result

    def prepare(view, j):
        mixed, sides_of = [], []
        for h in range(tiles):
            code = view(coded, h)
            sides_of.append(code[pl.ds(j + 1, SUB), :] + code[pl.ds(j - 1, SUB), :])
            mixed.append(code[pl.ds(j, SUB), :] + 0.5 * sides_of[h])
        nxt, prv = ring_shift(mixed, lanes)
        near, far, inverses, masks = [], [], [], []
        for h in range(tiles):
            own = view(deep, h)[pl.ds(j, SUB), :]
            wet_sum, deep_sum = decode(sides_of[h] + (nxt[h] + prv[h]))
            wet = jnp.where(own > 0, 1.0, 0.0)
            diag = 0.5 + 2.0 * (own * wet_sum + wet * (deep_sum * scale))
            inverse = 1.0 / diag
            inverses.append(inverse)
            masks.append(wet)
            ease_h = wet * inverse
            view(ease, h)[pl.ds(j, SUB), :] = ease_h
            twice = own + own
            e = twice + 2.0 * view(deep, h)[pl.ds(j + 1, SUB), :]
            w = twice + 2.0 * view(deep, h)[pl.ds(j - 1, SUB), :]
            n = twice + 2.0 * view(deep_n, h)[pl.ds(j, SUB), :]
            s = twice + 2.0 * view(deep_s, h)[pl.ds(j, SUB), :]
            ne = own + view(deep_n, h)[pl.ds(j + 1, SUB), :]
            nw = own + view(deep_n, h)[pl.ds(j - 1, SUB), :]
            se = own + view(deep_s, h)[pl.ds(j + 1, SUB), :]
            sw = own + view(deep_s, h)[pl.ds(j - 1, SUB), :]
            for i, value in enumerate((e, n, s, ne, nw, se, sw)):
                view(pairs, i, h)[pl.ds(j, SUB), :] = value
            near.append((e, w, n, s))
            far.append((ne, nw, se, sw))
        sums = nine(view, now, j, near, far)
        firsts = []
        for h in range(tiles):
            e = view(old, h)[pl.ds(j, SUB), :]
            across = view(flux, h)[pl.ds(j + 1, SUB), :] - view(flux, h)[pl.ds(j - 1, SUB), :]
            drive = view(part, h)[pl.ds(j, SUB), :] - 0.25 * across
            z = drive * inverses[h] - e + masks[h] * inverses[h] * sums[h]
            view(total, h)[pl.ds(j, SUB), :] = e + weights[0] * z
            firsts.append(masks[h] * z)
        nxt, prv = ring_shift(firsts, lanes)
        for h in range(tiles):
            for i, value in enumerate((firsts[h], nxt[h], prv[h])):
                view(then, i, h)[pl.ds(j, SUB), :] = value

    over_tiles(prepare)

    source, target = then, now
    for k in range(1, ITERS):
        def apply(view, j, k=k, source=source, target=target):
            near, far = [], []
            for h in range(tiles):
                def pair(i, shift=0):
                    return view(pairs, i, h)[pl.ds(j + shift, SUB), :]

                near.append((pair(0), pair(0, -1), pair(1), pair(2)))
                far.append((pair(3), pair(4), pair(5), pair(6)))
            sums = nine(view, source, j, near, far)
            values = [view(ease, h)[pl.ds(j, SUB), :] * sums[h] for h in range(tiles)]
            for h in range(tiles):
                here = view(total, h)
                here[pl.ds(j, SUB), :] = here[pl.ds(j, SUB), :] + weights[k] * values[h]
            if k < ITERS - 1:
                nxt, prv = ring_shift(values, lanes)
                for h in range(tiles):
                    for i, value in enumerate((values[h], nxt[h], prv[h])):
                        view(target, i, h)[pl.ds(j, SUB), :] = value

        over_tiles(apply)
        source, target = target, source

    def results(i):
        part_of = pl.ds(pl.multiple_of(i * size, SUB), size)
        return [
            pltpu.make_async_copy(
                value.at[part_of, :], place.at[part_of, :], out_sem.at[n * CHUNKS + i]
            )
            for n, (value, place) in enumerate(
                ((surf_out, surf_hbm), (x_out, x_hbm), (y_out, y_hbm))
            )
        ]

    def finish(i, carry):
        window = pl.ds(pl.multiple_of(i * size + SUB, SUB), size + 2 * SUB)
        for r in range(0, size, SUB):
            j = r + SUB
            at = pl.ds(pl.multiple_of(i * size + r, SUB), SUB)
            views = [total.at[h, window, :] for h in range(tiles)]
            here = [v[pl.ds(j, SUB), :] for v in views]
            here[sides] = jnp.where(beyond, here[sides], 0.0)
            nxt, prv = ring_shift(here, lanes)
            for h in range(sides):
                span = pl.ds(h * LANES, LANES)
                wet = depth[at, span] > 0
                slope = views[h][pl.ds(j + 1, SUB), :] - views[h][pl.ds(j - 1, SUB), :]
                surf_out[at, span] = here[h]
                x_out[at, span] = jnp.where(wet, flow_x[at, span] - 0.25 * slope, 0.0)
                y_out[at, span] = jnp.where(
                    wet, flow_y[at, span] - 0.25 * (nxt[h] - prv[h]), 0.0
                )
        for copy in results(i):
            copy.start()
        return carry

    lax.fori_loop(0, CHUNKS, finish, 0)
    for i in range(CHUNKS):
        for copy in results(i):
            copy.wait()
    for copy in outward:
        copy.wait()


def solve_pass(last_part, made, placed, peak, depth, surf, flow_x, flow_y, force, west, east, south, north):
    rows, cols = depth.shape
    shape = (cols // LANES + 1, rows + 4 * SUB, LANES)
    ext = pltpu.VMEM(shape, F32)
    three = pltpu.VMEM((3, *shape), F32)
    plain = jax.ShapeDtypeStruct((rows, cols), F32)
    return pl.pallas_call(
        functools.partial(solve_kernel, last_part),
        in_specs=[IN_VMEM, IN_HBM] + [IN_VMEM] * 10,
        out_specs=[IN_HBM] * 4,
        out_shape=[jax.ShapeDtypeStruct(placed.shape, F32)] + [plain] * 3,
        input_output_aliases={1: 0},
        scratch_shapes=[pltpu.VMEM((rows, cols), F32)] * 3
        + [ext] * 8
        + [pltpu.VMEM((7, *shape), F32), three, three, ext]
        + [pltpu.SemaphoreType.DMA((2,)), pltpu.SemaphoreType.DMA((3 * CHUNKS,))],
        compiler_params=pltpu.CompilerParams(vmem_limit_bytes=VMEM_LIMIT),
        cost_estimate=pl.CostEstimate(
            flops=200 * depth.size, bytes_accessed=32 * depth.size, transcendentals=0
        ),
        name="solve",
    )(made, placed, peak, depth, surf, flow_x, flow_y, force, west, east, south, north)


def twin_pairs(axis):
    return [(i, i ^ 1) for i in range(lax.axis_size(axis))]


def other_x_pairs():
    size = lax.axis_size("gx")
    return [(i, (i + 1 if i % 2 else i - 1) % size) for i in range(size)]


def other_y_pairs():
    size_x, size_y = lax.axis_size("gx"), lax.axis_size("gy")
    pairs = []
    for i in range(size_x):
        for j in range(size_y):
            if j in (0, size_y - 1):
                target = (i ^ 1, j)
            else:
                target = (i, j + 1 if j % 2 else j - 1)
            pairs.append((i * size_y + j, target[0] * size_y + target[1]))
    return pairs


def spread_rounds(axis):
    size = lax.axis_size(axis)
    reach = 1
    while reach < size:
        if size & (size - 1) == 0:
            yield axis, [(i, i ^ reach) for i in range(size)]
        else:
            yield axis, [(i, (i + reach) % size) for i in range(size)]
        reach *= 2


def local(
    tracer, zonal_flow, meridional_flow, surface_prev, transport_x, transport_y, land_mask, levels
):
    count = tracer.shape[1]
    (
        force, depth, to_twin, to_other, tracer, surface_prev, transport_x, transport_y,
    ) = column_pass(tracer, land_mask, levels, surface_prev, transport_x, transport_y)
    fields = (depth, surface_prev, transport_x, transport_y, force)
    from_other = lax.ppermute(to_other, "gx", other_x_pairs())
    from_twin = lax.ppermute(to_twin, "gx", twin_pairs("gx"))
    to_south, to_north, zonal_flow, meridional_flow = strip_pass(
        zonal_flow, meridional_flow, tracer, *fields
    )
    to_twin, to_other, west, east = pack_pass(to_south, to_north, from_twin, from_other)
    from_twin = lax.ppermute(to_twin, "gy", twin_pairs("gy"))
    from_other = lax.ppermute(to_other, ("gx", "gy"), other_y_pairs())
    peak, south, north = peak_pass(depth, west, east, from_twin, from_other)
    halo = (west, east, south, north)
    rounds = [r for axis in ("gx", "gy") for r in spread_rounds(axis)]
    cuts = [count * i // PARTS for i in range(PARTS + 1)]
    parts = tuple(zip(cuts, cuts[1:]))
    first = len(rounds) - PARTS
    known, made, placed = (), None, None
    for turn, (axis, pairs) in enumerate(rounds):
        moved = lax.ppermute(peak, axis, pairs)
        if turn == 0:
            known = around_pass(depth, *halo)
            moved, known = lax.optimization_barrier((moved, known))
        if turn >= first:
            made, placed = tracer_pass(
                parts, turn - first, tracer, zonal_flow, meridional_flow, depth,
                west, east, known, made, placed,
            )
        peak = jnp.maximum(peak, moved)
        if first <= turn < len(rounds) - 1:
            peak, made = lax.optimization_barrier((peak, made))
    return solve_pass(parts[-1], made, placed, peak, *fields, *halo)


def solution(mesh):
    cell = P("gx", "gy")
    level = P(None, "gx", "gy")
    stack = P(None, None, "gx", "gy")
    return jax.shard_map(
        local,
        mesh=mesh,
        in_specs=(stack, level, level, cell, cell, cell, cell, cell),
        out_specs=(stack, cell, cell, cell),
        check_vma=False,
    )
```

```python
import functools

import jax
import jax.numpy as jnp
from jax import lax
from jax.experimental import pallas as pl
from jax.experimental.pallas import tpu as pltpu
from jax.sharding import PartitionSpec as P

ITERS = 4
WIDTH = ITERS + 1
LANES = 128
SUB = 8
HALF = LANES // 2
FIELDS = 5
F32 = jnp.float32
BF16 = jnp.bfloat16
VMEM_LIMIT = 12 * 1024 * 1024
LEVELS = 16
BASE = 2 * LEVELS
CODE = 1024.0
PARTS = 4
CHUNKS = 4


def lane_ids(rows):
    return lax.broadcasted_iota(jnp.int32, (rows, LANES), 1)


def put_lane(value, source, target):
    shift = (target - source) % LANES
    return pltpu.roll(value, shift, 1) if shift else value


def strip_pair(low, high, lanes, values):
    for f, (begin, end) in enumerate(values):
        at = BASE + (f + 1) * WIDTH
        turned = put_lane(jnp.where(lanes < HALF, begin, end), 0, at)
        low = jnp.where((lanes >= at) & (lanes < at + WIDTH), turned, low)
        high = jnp.where((lanes >= at - WIDTH) & (lanes < at), turned, high)
    return low, high


def slices_of(rows):
    tiles = rows // SUB
    return tiles // max(n for n in range(1, 5) if tiles % n == 0)


def column_kernel(
    tracer_hbm, land_hbm, levels_hbm, surf_hbm, flow_x_hbm, flow_y_hbm,
    force, depth, to_twin, to_other, tracer, surf, flow_x, flow_y,
    land, levels, flat_sem, chunk_sem,
):
    count = tracer.shape[1]
    rows, cols = land.shape
    sides = cols // LANES
    base = 2 * count
    slices = slices_of(rows)
    size = rows // slices

    def copy_in(i):
        part = pl.ds(pl.multiple_of(i * size, SUB), size)
        return pltpu.make_async_copy(
            tracer_hbm.at[:, :, part, :], tracer.at[:, :, part, :], chunk_sem.at[i]
        )

    flats = [
        pltpu.make_async_copy(source, target, flat_sem.at[i])
        for i, (source, target) in enumerate(
            (
                (land_hbm, land),
                (levels_hbm, levels),
                (surf_hbm, surf),
                (flow_x_hbm, flow_x),
                (flow_y_hbm, flow_y),
            )
        )
    ]
    for copy in flats[:2]:
        copy.start()
    for i in range(slices):
        copy_in(i).start()
    for copy in flats[2:]:
        copy.start()
    for copy in flats[:2]:
        copy.wait()

    def chunk(i, carry):
        copy_in(i).wait()
        for r in range(0, size, SUB):
            at = pl.ds(pl.multiple_of(i * size + r, SUB), SUB)
            for h in range(sides):
                span = pl.ds(h * LANES, LANES)
                deep = (land[at, span] * levels[at, span]).astype(F32)
                total = jnp.zeros((SUB, LANES), F32)
                for k in range(count):
                    gain = jnp.maximum(deep - k, 0.0)
                    total = total + gain * (
                        tracer[0, k, at, span] - 0.75 * tracer[1, k, at, span]
                    )
                force[at, span] = total * (0.8 / count)
                depth[at, span] = deep
        return carry

    lax.fori_loop(0, slices, chunk, 0)
    for copy in flats[2:]:
        copy.wait()

    def edge_rows(out, line, tile):
        for h in range(sides):
            span = pl.ds(h * LANES, LANES)
            deep = depth[pl.ds(line, 1), span]
            for c in range(2):
                for k in range(count):
                    out[pl.ds(c * count + k, 1), span] = jnp.where(
                        deep > k, tracer[c, k, pl.ds(line, 1), span], 0.0
                    )
            for f, ref in enumerate((depth, surf, flow_x, flow_y, force)):
                out[pl.ds(base + f * SUB, SUB), span] = ref[pl.ds(tile, SUB), span]

    even = is_even("gx")

    @pl.when(even)
    def _():
        edge_rows(to_twin, rows - 1, rows - SUB)
        edge_rows(to_other, 0, 0)

    @pl.when(jnp.logical_not(even))
    def _():
        edge_rows(to_twin, 0, 0)
        edge_rows(to_other, rows - 1, rows - SUB)


def is_even(axis):
    return lax.rem(lax.axis_index(axis), 2) == 0


IN_HBM = pl.BlockSpec(memory_space=pltpu.HBM)
IN_VMEM = pl.BlockSpec(memory_space=pltpu.VMEM)


def column_pass(tracer, land, levels, surf, flow_x, flow_y):
    two, count, rows, cols = tracer.shape
    lines = (two * count + FIELDS * SUB, cols)
    plain = (rows, cols)
    shapes = [plain, plain, lines, lines, tracer.shape, plain, plain, plain]
    return pl.pallas_call(
        column_kernel,
        in_specs=[IN_HBM] * 6,
        out_specs=[IN_VMEM] * len(shapes),
        out_shape=[jax.ShapeDtypeStruct(shape, F32) for shape in shapes],
        scratch_shapes=[
            pltpu.VMEM(plain, jnp.int32),
            pltpu.VMEM(plain, jnp.int32),
            pltpu.SemaphoreType.DMA((5,)),
            pltpu.SemaphoreType.DMA((slices_of(rows),)),
        ],
        compiler_params=pltpu.CompilerParams(vmem_limit_bytes=VMEM_LIMIT),
        cost_estimate=pl.CostEstimate(
            flops=6 * tracer.size, bytes_accessed=4 * tracer.size, transcendentals=0
        ),
        name="columns",
    )(
        *(
            pltpu.with_memory_space_constraint(value, pltpu.HBM)
            for value in (tracer, land, levels, surf, flow_x, flow_y)
        )
    )


def strip_kernel(
    tracer, depth, surf, flow_x, flow_y, force, zonal_hbm, merid_hbm,
    to_south, to_north, zonal, merid, sem,
):
    flows = [
        pltpu.make_async_copy(source, target, sem.at[i])
        for i, (source, target) in enumerate(((zonal_hbm, zonal), (merid_hbm, merid)))
    ]
    for copy in flows:
        copy.start()
    count = tracer.shape[1]
    rows, cols = depth.shape
    base = 2 * count
    lanes = lane_ids(SUB)
    size = rows // CHUNKS
    low_kind = jnp.where((lanes >= 1) & (lanes <= base), lax.rem(lanes - 1 + count, count), -1)
    low_kind = low_kind.astype(F32)
    high_kind = jnp.where(lanes < base, lax.rem(lanes, count), -1).astype(F32)
    odd = (lanes & 1) == 1
    ends = [pl.ds(0, LANES), pl.ds(cols - LANES, LANES)]

    def chunk(i, carry):
        upper = i >= CHUNKS // 2
        turn = jnp.where(upper, HALF, 0)
        keep = (lanes < HALF) & upper
        first_row = jnp.where(upper, i - CHUNKS // 2, i) * size
        for r in range(0, size, SUB):
            at = pl.ds(pl.multiple_of(i * size + r, SUB), SUB)
            packed = [jnp.zeros((SUB, LANES), F32)] * 2
            for line in range(base):
                c, k = divmod(line, count)
                both = jnp.where(lanes < HALF, tracer[c, k, at, ends[0]], tracer[c, k, at, ends[1]])
                both = put_lane(both, 0, line + 1)
                packed[line % 2] = jnp.where(
                    (lanes == line) | (lanes == line + 1), both, packed[line % 2]
                )
            pairs = [
                tuple(ref[at, span] for span in ends)
                for ref in (depth, surf, flow_x, flow_y, force)
            ]
            low = jnp.where(odd, packed[0], packed[1])
            high = jnp.where(odd, packed[1], packed[0])
            low = jnp.where(pairs[0][0][:, 0:1] > low_kind, low, 0.0)
            high = jnp.where(pairs[0][1][:, LANES - 1 : LANES] > high_kind, high, 0.0)
            low, high = strip_pair(low, high, lanes, pairs)
            to = pl.ds(pl.multiple_of(first_row + r, SUB), SUB)
            for out, value in ((to_south, low), (to_north, high)):
                out[to, :] = jnp.where(keep, out[to, :], pltpu.roll(value, turn, 1))
        return carry

    lax.fori_loop(0, CHUNKS, chunk, 0)
    for out in (to_south, to_north):
        out[pl.ds(rows // 2, SUB), :] = jnp.zeros((SUB, LANES), F32)
    for copy in flows:
        copy.wait()


def strip_pass(zonal, merid, tracer, depth, surf, flow_x, flow_y, force):
    shape = jax.ShapeDtypeStruct((depth.shape[0] // 2 + SUB, LANES), F32)
    return pl.pallas_call(
        strip_kernel,
        in_specs=[IN_VMEM] * 6 + [IN_HBM] * 2,
        out_specs=[IN_VMEM] * 4,
        out_shape=[shape, shape]
        + [jax.ShapeDtypeStruct(value.shape, BF16) for value in (zonal, merid)],
        scratch_shapes=[pltpu.SemaphoreType.DMA((2,))],
        compiler_params=pltpu.CompilerParams(vmem_limit_bytes=VMEM_LIMIT),
        cost_estimate=pl.CostEstimate(
            flops=6 * tracer.size, bytes_accessed=4 * tracer.size, transcendentals=0
        ),
        name="strips",
    )(
        tracer, depth, surf, flow_x, flow_y, force,
        *(pltpu.with_memory_space_constraint(value, pltpu.HBM) for value in (zonal, merid)),
    )


def pack_kernel(to_south, to_north, from_twin, from_other, to_twin, to_other, west, east):
    half = to_south.shape[0] - SUB
    sides = west.shape[1] // LANES
    lanes = lane_ids(SUB)
    even_x, even_y = is_even("gx"), is_even("gy")
    for r in range(0, west.shape[0], SUB):
        for h in range(sides):
            at = (pl.ds(r, SUB), pl.ds(h * LANES, LANES))
            first, second = from_twin[at], from_other[at]
            east[at] = jnp.where(even_x, first, second)
            west[at] = jnp.where(even_x, second, first)
    strips = []
    for ref in (west, east):
        zero = jnp.zeros((SUB, LANES), F32)
        ends = [pl.ds(0, LANES), pl.ds((sides - 1) * LANES, LANES)]
        values = [
            tuple(ref[pl.ds(BASE + f * SUB, SUB), span] for span in ends) for f in range(FIELDS)
        ]
        strips.append(strip_pair(zero, zero, lanes, values))
    for r in range(0, half + SUB, SUB):
        at = pl.ds(r, SUB)
        if r < half:
            low, high = to_south[at, :], to_north[at, :]
        else:
            low, high = (
                jnp.where(lanes < HALF, before, pltpu.roll(after, HALF, 1))
                for before, after in zip(*strips)
            )
        to_twin[at, :] = jnp.where(even_y, high, low)
        to_other[at, :] = jnp.where(even_y, low, high)


def pack_pass(to_south, to_north, from_twin, from_other):
    strip = jax.ShapeDtypeStruct(to_south.shape, F32)
    lines = jax.ShapeDtypeStruct(from_twin.shape, F32)
    return pl.pallas_call(
        pack_kernel,
        in_specs=[IN_VMEM] * 4,
        out_specs=[IN_VMEM] * 4,
        out_shape=[strip, strip, lines, lines],
        compiler_params=pltpu.CompilerParams(vmem_limit_bytes=VMEM_LIMIT),
        cost_estimate=pl.CostEstimate(
            flops=to_south.size, bytes_accessed=16 * to_south.size, transcendentals=0
        ),
        name="corners",
    )(to_south, to_north, from_twin, from_other)


def message_rows(ref, rows, r):
    half = rows // 2
    if r < 0:
        return ref[pl.ds(half, SUB), :]
    if r >= rows:
        return pltpu.roll(ref[pl.ds(half, SUB), :], HALF, 1)
    if r < half:
        return ref[pl.ds(r, SUB), :]
    return pltpu.roll(ref[pl.ds(r - half, SUB), :], HALF, 1)


def outer_tile(south, north, rows, r, f, open_south, open_north, lanes):
    at = BASE + (f + 1) * WIDTH
    mixed = jnp.where(lanes < at, message_rows(south, rows, r), message_rows(north, rows, r))
    mixed = put_lane(mixed, at, 0)
    valid = ((lanes < WIDTH) & open_north) | ((lanes >= LANES - WIDTH) & open_south)
    return jnp.where(valid, mixed, 0.0)


def extend(target, base, f, field, west, east, south, north, open_south, open_north):
    rows, cols = field.shape
    sides = cols // LANES
    lanes = lane_ids(SUB)
    for r in range(-SUB, rows + 1, SUB):
        to = pl.ds(SUB + r, SUB)
        for h in range(sides):
            span = pl.ds(h * LANES, LANES)
            if r < 0:
                target[h, to, :] = west[pl.ds(base + f * SUB, SUB), span]
            elif r >= rows:
                target[h, to, :] = east[pl.ds(base + f * SUB, SUB), span]
            else:
                target[h, to, :] = field[pl.ds(r, SUB), span]
        target[sides, to, :] = outer_tile(
            south, north, rows, r, f, open_south, open_north, lanes
        )


def latitude_ends():
    place, size = lax.axis_index("gy"), lax.axis_size("gy")
    return place > 0, place < size - 1


def ring_shift(tiles, lanes):
    size = len(tiles)
    after = [pltpu.roll(t, LANES - 1, 1) for t in tiles]
    before = [pltpu.roll(t, 1, 1) for t in tiles]
    nxt = [jnp.where(lanes == LANES - 1, after[(h + 1) % size], after[h]) for h in range(size)]
    prv = [jnp.where(lanes == 0, before[(h - 1) % size], before[h]) for h in range(size)]
    return nxt, prv


def nine_sum(ref, r, lanes):
    sides = [ref[h, pl.ds(r + 1, SUB), :] + ref[h, pl.ds(r - 1, SUB), :] for h in range(ref.shape[0])]
    mixed = [ref[h, pl.ds(r, SUB), :] + 0.5 * sides[h] for h in range(ref.shape[0])]
    nxt, prv = ring_shift(mixed, lanes)
    return [sides[h] + (nxt[h] + prv[h]) for h in range(ref.shape[0])]


def peak_kernel(depth, west, east, from_twin, from_other, peak, south, north, coded):
    rows, cols = depth.shape
    sides = cols // LANES
    lanes = lane_ids(SUB)
    open_south, open_north = latitude_ends()
    scale = 2.0 / (BASE // 2)
    even = is_even("gy")
    for r in range(0, south.shape[0], SUB):
        at = pl.ds(r, SUB)
        first, second = from_twin[at, :], from_other[at, :]
        north[at, :] = jnp.where(even, first, second)
        south[at, :] = jnp.where(even, second, first)
    extend(coded, BASE, 0, depth, west, east, south, north, open_south, open_north)
    for r in range(0, rows + 2 * SUB, SUB):
        for h in range(sides + 1):
            d = coded[h, pl.ds(r, SUB), :]
            coded[h, pl.ds(r, SUB), :] = d + jnp.where(d > 0, CODE, 0.0)
    best = jnp.full((SUB, LANES), 0.0, F32)
    for r in range(SUB, rows + SUB, SUB):
        sums = nine_sum(coded, r, lanes)
        for h in range(sides):
            wet, deep = decode(sums[h])
            d = depth[pl.ds(r - SUB, SUB), pl.ds(h * LANES, LANES)]
            best = jnp.maximum(best, d * wet + jnp.where(d > 0, deep, 0.0))
    best = jnp.max(jnp.max(best, axis=1, keepdims=True), axis=0, keepdims=True)
    peak[...] = jnp.broadcast_to(0.5 + scale * best, (SUB, LANES))


def decode(sums):
    wet = jnp.floor(sums * (2.0 / CODE)) * 0.5
    return wet, sums - CODE * wet


def peak_pass(depth, west, east, from_twin, from_other):
    rows, cols = depth.shape
    strip = jax.ShapeDtypeStruct(from_twin.shape, F32)
    ext = pltpu.VMEM((cols // LANES + 1, rows + 2 * SUB, LANES), F32)
    return pl.pallas_call(
        peak_kernel,
        in_specs=[IN_VMEM] * 5,
        out_specs=[IN_VMEM] * 3,
        out_shape=[jax.ShapeDtypeStruct((SUB, LANES), F32), strip, strip],
        scratch_shapes=[ext],
        compiler_params=pltpu.CompilerParams(vmem_limit_bytes=VMEM_LIMIT),
        cost_estimate=pl.CostEstimate(
            flops=30 * depth.size, bytes_accessed=4 * depth.size, transcendentals=0
        ),
        name="peak",
    )(depth, west, east, from_twin, from_other)


def around_kernel(depth, west, east, south, north, edge_y, around, masked):
    rows, cols = depth.shape
    sides = cols // LANES
    lanes = lane_ids(SUB)
    spans = [pl.ds(h * LANES, LANES) for h in range(sides)]
    open_south, open_north = latitude_ends()
    for h in range(sides):
        masked[h, pl.ds(0, SUB), :] = west[pl.ds(BASE, SUB), spans[h]]
        masked[h, pl.ds(SUB, rows), :] = depth[:, spans[h]]
        masked[h, pl.ds(SUB + rows, SUB), :] = east[pl.ds(BASE, SUB), spans[h]]
    for big in range(0, rows, 2 * SUB):
        shifted = []
        for r in (big, big + SUB):
            low, high = message_rows(south, rows, r), message_rows(north, rows, r)
            edge_y[0, pl.ds(r, SUB), :] = jnp.where(open_south, low, 0.0)
            edge_y[1, pl.ds(r, SUB), :] = jnp.where(
                open_north, pltpu.roll(high, LANES - 2, 1), 0.0
            )
            tiles = [depth[pl.ds(r, SUB), span] for span in spans]
            tiles.append(outer_tile(south, north, rows, r, 0, open_south, open_north, lanes))
            shifted.append(ring_shift(tiles, lanes))
        at = pl.ds(big, 2 * SUB)
        for h in range(sides):
            around[0, h, at, :] = masked[h, pl.ds(SUB + big + 1, 2 * SUB), :].astype(BF16)
            around[1, h, at, :] = masked[h, pl.ds(SUB + big - 1, 2 * SUB), :].astype(BF16)
            for n in range(2):
                pair = jnp.concatenate([shifted[0][n][h], shifted[1][n][h]], 0)
                around[2 + n, h, at, :] = pair.astype(BF16)


def around_pass(depth, west, east, south, north):
    rows, cols = depth.shape
    sides = cols // LANES
    return pl.pallas_call(
        around_kernel,
        in_specs=[IN_VMEM] * 5,
        out_specs=[IN_VMEM] * 2,
        out_shape=[
            jax.ShapeDtypeStruct((2, rows, LANES), F32),
            jax.ShapeDtypeStruct((4, sides, rows, LANES), BF16),
        ],
        scratch_shapes=[pltpu.VMEM((sides, rows + 2 * SUB, LANES), F32)],
        compiler_params=pltpu.CompilerParams(vmem_limit_bytes=VMEM_LIMIT),
        cost_estimate=pl.CostEstimate(
            flops=30 * depth.size, bytes_accessed=16 * depth.size, transcendentals=0
        ),
        name="around",
    )(depth, west, east, south, north)


def tracer_kernel(parts, index, tracer, zonal, merid, depth, west, east, edge_y, around, *rest):
    start, stop = parts[index]
    copies = []
    if index:
        earlier, placed = rest[0], rest[-3]
        first, last = parts[index - 1]
        for c in range(2):
            target = placed.at[c, pl.ds(first, last - first)]
            copies.append(pltpu.make_async_copy(earlier.at[c], target, rest[-1].at[c]))
    out, masked = rest[-4 if index else -3], rest[-2]
    for copy in copies:
        copy.start()
    rows, cols = depth.shape
    sides = cols // LANES
    count = BASE // 2
    lanes = lane_ids(SUB)
    spans = [pl.ds(h * LANES, LANES) for h in range(sides)]

    def one_level(level, carry):
        mark = lax.convert_element_type(level, F32)
        for c in range(2):
            line = c * count + level
            group = pl.multiple_of(lax.div(line, SUB) * SUB, SUB)
            place = lax.rem(line, SUB)
            for h in range(sides):
                before = west[pl.ds(group, SUB), spans[h]]
                masked[c, h, pl.ds(0, SUB), :] = pltpu.roll(before, SUB - 1 - place, 0)
                after = east[pl.ds(group, SUB), spans[h]]
                masked[c, h, pl.ds(SUB + rows, SUB), :] = pltpu.roll(after, lax.rem(SUB - place, SUB), 0)
        for r in range(0, rows, SUB):
            for h in range(sides):
                here = depth[pl.ds(r, SUB), spans[h]] > mark
                for c in range(2):
                    masked[c, h, pl.ds(SUB + r, SUB), :] = jnp.where(
                        here, tracer[c, level, pl.ds(r, SUB), spans[h]], 0.0
                    )
        mark_pair = jnp.full((2 * SUB, LANES), mark, F32).astype(BF16)
        one, none = jnp.ones((2 * SUB, LANES), BF16), jnp.zeros((2 * SUB, LANES), BF16)
        quarter = jnp.full((2 * SUB, LANES), 0.25, BF16)
        picks = []
        for c in range(2):
            line = c * count + level
            picks.append(((lanes >= line) & (lanes < line + HALF), lax.rem(LANES - line, LANES)))
        for big in range(0, rows, 2 * SUB):
            wide = pl.ds(big, 2 * SUB)
            pairs = []
            for h in range(sides):
                near = none
                for n in range(4):
                    near = near + jnp.where(around[n, h, wide, :] > mark_pair, one, none)
                pairs.append(
                    (
                        1.0 - 0.2 * near.astype(F32),
                        (zonal[level, wide, spans[h]] * quarter).astype(F32),
                        (merid[level, wide, spans[h]] * quarter).astype(F32),
                    )
                )
            for sub in range(2):
                r = big + sub * SUB
                at = pl.ds(r, SUB)
                part = slice(sub * SUB, (sub + 1) * SUB)
                factors = []
                for h in range(sides):
                    own, u, v = (value[part] for value in pairs[h])
                    here = depth[at, spans[h]] > mark
                    factors.append((here, own, 0.2 - u, 0.2 + u, 0.2 - v, 0.2 + v))
                for c in range(2):
                    tiles = [masked[c, h, pl.ds(SUB + r, SUB), :] for h in range(sides)]
                    pick, turn = picks[c]
                    outer = pltpu.roll(jnp.where(pick, edge_y[0, at, :], edge_y[1, at, :]), turn, 1)
                    after = [pltpu.roll(t, LANES - 1, 1) for t in tiles] + [outer]
                    before = [outer] + [pltpu.roll(t, 1, 1) for t in tiles]
                    for h in range(sides):
                        here, own, to_e, to_w, to_n, to_s = factors[h]
                        nxt = jnp.where(lanes == LANES - 1, after[h + 1], after[h])
                        prv = jnp.where(lanes == 0, before[h], before[h + 1])
                        value = own * tiles[h] + to_n * nxt + to_s * prv
                        value = value + to_e * masked[c, h, pl.ds(SUB + r + 1, SUB), :]
                        value = value + to_w * masked[c, h, pl.ds(SUB + r - 1, SUB), :]
                        out[c, level - start, at, spans[h]] = jnp.where(
                            here, value, tracer[c, level, at, spans[h]]
                        )
        return carry

    lax.fori_loop(start, stop, one_level, 0)
    for copy in copies:
        copy.wait()


def tracer_pass(parts, index, tracer, zonal, merid, depth, west, east, known, earlier, placed):
    two, count, rows, cols = tracer.shape
    sides = cols // LANES
    part = parts[index][1] - parts[index][0]
    operands = [tracer, zonal, merid, depth, west, east, *known]
    specs = [IN_VMEM] * len(operands)
    shapes = [jax.ShapeDtypeStruct((two, part, rows, cols), F32)]
    outs = [IN_VMEM]
    aliases = {}
    if index:
        operands.append(earlier)
        specs.append(IN_VMEM)
        if index > 1:
            aliases = {len(operands): len(shapes)}
            operands.append(placed)
            specs.append(IN_HBM)
        shapes.append(jax.ShapeDtypeStruct(tracer.shape, F32))
        outs.append(IN_HBM)
    results = pl.pallas_call(
        functools.partial(tracer_kernel, parts, index),
        in_specs=specs,
        out_specs=outs,
        out_shape=shapes,
        scratch_shapes=[
            pltpu.VMEM((2, sides, rows + 2 * SUB, LANES), F32),
            pltpu.SemaphoreType.DMA((2,)),
        ],
        input_output_aliases=aliases,
        compiler_params=pltpu.CompilerParams(vmem_limit_bytes=VMEM_LIMIT),
        cost_estimate=pl.CostEstimate(
            flops=40 * tracer.size * part // count,
            bytes_accessed=10 * tracer.size * part // count,
            transcendentals=0,
        ),
        name="tracers",
    )(*operands)
    return results if index else (results[0], None)


def group_of(tiles):
    return max(n for n in range(1, 17) if tiles % n == 0)


def solve_kernel(
    last_part, tracer_in, _, peak, depth, surf, flow_x, flow_y, force, west, east, south, north,
    tracer_hbm, surf_hbm, x_hbm, y_hbm,
    surf_out, x_out, y_out, old, deep, deep_n, deep_s, coded, flux, part, ease, pairs, now, then, total, sem, out_sem,
):
    rows, cols = depth.shape
    sides = cols // LANES
    tiles = sides + 1
    lanes = lane_ids(SUB)
    scale = 2.0 / BASE
    open_south, open_north = latitude_ends()
    beyond = ((lanes < WIDTH) & open_north) | ((lanes >= LANES - WIDTH) & open_south)
    part_at = pl.ds(last_part[0], last_part[1] - last_part[0])
    outward = [
        pltpu.make_async_copy(tracer_in.at[c], tracer_hbm.at[c, part_at], sem.at[c])
        for c in range(2)
    ]
    for copy in outward:
        copy.start()

    lowest = 0.5 / peak[...]
    shrink = (1.0 - lowest) * (1.0 - lowest)
    omega = jnp.full((SUB, LANES), 2.0, F32)
    weights, change = [jnp.ones((SUB, LANES), F32)], [jnp.ones((SUB, LANES), F32)]
    for _ in range(1, ITERS):
        omega = 1.0 / (1.0 - omega * shrink * 0.25)
        resid = [1.0 - weights[0]] + [p - w for p, w in zip(weights, weights[1:])] + [weights[-1]]
        held = change + [jnp.zeros((SUB, LANES), F32)]
        change = [omega * y + (omega - 1.0) * d for y, d in zip(resid, held)]
        weights = [w + d for w, d in zip(weights + [jnp.zeros((SUB, LANES), F32)], change)]

    edge = (pl.ds(0, SUB), pl.ds(rows + 3 * SUB, SUB))
    for ref in (deep, deep_n, deep_s, coded, flux):
        for at in edge:
            for h in range(tiles):
                ref[h, at, :] = jnp.zeros((SUB, LANES), F32)
    for ref in (pairs, now, then):
        for i in range(ref.shape[0]):
            for at in edge:
                for h in range(tiles):
                    ref[i, h, at, :] = jnp.zeros((SUB, LANES), F32)

    def spread(ref, at, values):
        nxt, prv = ring_shift(values, lanes)
        for h in range(tiles):
            ref[0, h, at, :] = values[h]
            ref[1, h, at, :] = nxt[h]
            ref[2, h, at, :] = prv[h]

    def load_tile(to, field, low, high):
        def ring(f):
            at = BASE + (f + 1) * WIDTH
            outer = put_lane(jnp.where(lanes < at, low, high), at, 0)
            return [field(f, h) for h in range(sides)] + [jnp.where(beyond, outer, 0.0)]

        levels = ring(0)
        deeps = [v * scale for v in levels]
        wets = [jnp.where(v > 0, 1.0, 0.0) for v in levels]
        nxt, prv = ring_shift(deeps, lanes)
        surfs, drives = ring(1), ring(4)
        cross, crosses = ring_shift([m * v for m, v in zip(wets, ring(3))], lanes)
        along = ring(2)
        for h in range(tiles):
            deep[h, to, :] = deeps[h]
            deep_n[h, to, :] = nxt[h]
            deep_s[h, to, :] = prv[h]
            coded[h, to, :] = levels[h] + CODE * wets[h]
            old[h, to, :] = surfs[h]
            flux[h, to, :] = wets[h] * along[h]
            part[h, to, :] = 0.5 * surfs[h] + drives[h] - 0.25 * (cross[h] - crosses[h])
        spread(now, to, [m * v for m, v in zip(wets, surfs)])

    fields = (depth, surf, flow_x, flow_y, force)
    half = rows // 2
    for ref, to, turn in ((west, SUB, 0), (east, rows + 2 * SUB, HALF)):
        tail = [message[pl.ds(half, SUB), :] for message in (south, north)]
        if turn:
            tail = [pltpu.roll(v, turn, 1) for v in tail]
        load_tile(
            pl.ds(to, SUB),
            lambda f, h, ref=ref: ref[pl.ds(BASE + f * SUB, SUB), pl.ds(h * LANES, LANES)],
            *tail,
        )
    size = rows // CHUNKS

    def load_chunk(i, carry):
        upper = i >= CHUNKS // 2
        turn = jnp.where(upper, HALF, 0)
        first_row = jnp.where(upper, i - CHUNKS // 2, i) * size
        for r in range(0, size, SUB):
            at = pl.ds(pl.multiple_of(i * size + r, SUB), SUB)
            line = pl.ds(pl.multiple_of(first_row + r, SUB), SUB)
            load_tile(
                pl.ds(pl.multiple_of(i * size + r + 2 * SUB, SUB), SUB),
                lambda f, h, at=at: fields[f][at, pl.ds(h * LANES, LANES)],
                *(pltpu.roll(message[line, :], turn, 1) for message in (south, north)),
            )
        return carry

    lax.fori_loop(0, CHUNKS, load_chunk, 0)

    count = rows // SUB + 2
    group = group_of(count)

    def over_tiles(body):
        def step(i, carry):
            window = pl.ds(pl.multiple_of(i * (group * SUB), SUB), (group + 2) * SUB)

            def view(ref, *index):
                return ref.at[(*index, window, slice(None))]

            for j in range(SUB, (group + 1) * SUB, SUB):
                body(view, j)
            return carry

        lax.fori_loop(0, count // group, step, 0)

    def nine(view, source, j, near, far):
        result = []
        for h in range(tiles):
            def value(i, shift):
                return view(source, i, h)[pl.ds(j + shift, SUB), :]

            side = near[h][0] * value(0, 1) + near[h][1] * value(0, -1)
            side = side + near[h][2] * value(1, 0) + near[h][3] * value(2, 0)
            corner = far[h][0] * value(1, 1) + far[h][1] * value(1, -1)
            corner = corner + far[h][2] * value(2, 1) + far[h][3] * value(2, -1)
            result.append(side + corner)
        return result

    def prepare(view, j):
        mixed, sides_of = [], []
        for h in range(tiles):
            code = view(coded, h)
            sides_of.append(code[pl.ds(j + 1, SUB), :] + code[pl.ds(j - 1, SUB), :])
            mixed.append(code[pl.ds(j, SUB), :] + 0.5 * sides_of[h])
        nxt, prv = ring_shift(mixed, lanes)
        near, far, inverses, masks = [], [], [], []
        for h in range(tiles):
            own = view(deep, h)[pl.ds(j, SUB), :]
            wet_sum, deep_sum = decode(sides_of[h] + (nxt[h] + prv[h]))
            wet = jnp.where(own > 0, 1.0, 0.0)
            diag = 0.5 + 2.0 * (own * wet_sum + wet * (deep_sum * scale))
            inverse = 1.0 / diag
            inverses.append(inverse)
            masks.append(wet)
            ease_h = wet * inverse
            view(ease, h)[pl.ds(j, SUB), :] = ease_h
            twice = own + own
            e = twice + 2.0 * view(deep, h)[pl.ds(j + 1, SUB), :]
            w = twice + 2.0 * view(deep, h)[pl.ds(j - 1, SUB), :]
            n = twice + 2.0 * view(deep_n, h)[pl.ds(j, SUB), :]
            s = twice + 2.0 * view(deep_s, h)[pl.ds(j, SUB), :]
            ne = own + view(deep_n, h)[pl.ds(j + 1, SUB), :]
            nw = own + view(deep_n, h)[pl.ds(j - 1, SUB), :]
            se = own + view(deep_s, h)[pl.ds(j + 1, SUB), :]
            sw = own + view(deep_s, h)[pl.ds(j - 1, SUB), :]
            for i, value in enumerate((e, n, s, ne, nw, se, sw)):
                view(pairs, i, h)[pl.ds(j, SUB), :] = value
            near.append((e, w, n, s))
            far.append((ne, nw, se, sw))
        sums = nine(view, now, j, near, far)
        firsts = []
        for h in range(tiles):
            e = view(old, h)[pl.ds(j, SUB), :]
            across = view(flux, h)[pl.ds(j + 1, SUB), :] - view(flux, h)[pl.ds(j - 1, SUB), :]
            drive = view(part, h)[pl.ds(j, SUB), :] - 0.25 * across
            z = drive * inverses[h] - e + masks[h] * inverses[h] * sums[h]
            view(total, h)[pl.ds(j, SUB), :] = e + weights[0] * z
            firsts.append(masks[h] * z)
        nxt, prv = ring_shift(firsts, lanes)
        for h in range(tiles):
            for i, value in enumerate((firsts[h], nxt[h], prv[h])):
                view(then, i, h)[pl.ds(j, SUB), :] = value

    over_tiles(prepare)

    source, target = then, now
    for k in range(1, ITERS):
        def apply(view, j, k=k, source=source, target=target):
            near, far = [], []
            for h in range(tiles):
                def pair(i, shift=0):
                    return view(pairs, i, h)[pl.ds(j + shift, SUB), :]

                near.append((pair(0), pair(0, -1), pair(1), pair(2)))
                far.append((pair(3), pair(4), pair(5), pair(6)))
            sums = nine(view, source, j, near, far)
            values = [view(ease, h)[pl.ds(j, SUB), :] * sums[h] for h in range(tiles)]
            for h in range(tiles):
                here = view(total, h)
                here[pl.ds(j, SUB), :] = here[pl.ds(j, SUB), :] + weights[k] * values[h]
            if k < ITERS - 1:
                nxt, prv = ring_shift(values, lanes)
                for h in range(tiles):
                    for i, value in enumerate((values[h], nxt[h], prv[h])):
                        view(target, i, h)[pl.ds(j, SUB), :] = value

        over_tiles(apply)
        source, target = target, source

    def results(i):
        part_of = pl.ds(pl.multiple_of(i * size, SUB), size)
        return [
            pltpu.make_async_copy(
                value.at[part_of, :], place.at[part_of, :], out_sem.at[n * CHUNKS + i]
            )
            for n, (value, place) in enumerate(
                ((surf_out, surf_hbm), (x_out, x_hbm), (y_out, y_hbm))
            )
        ]

    def finish(i, carry):
        window = pl.ds(pl.multiple_of(i * size + SUB, SUB), size + 2 * SUB)
        for r in range(0, size, SUB):
            j = r + SUB
            at = pl.ds(pl.multiple_of(i * size + r, SUB), SUB)
            views = [total.at[h, window, :] for h in range(tiles)]
            here = [v[pl.ds(j, SUB), :] for v in views]
            here[sides] = jnp.where(beyond, here[sides], 0.0)
            nxt, prv = ring_shift(here, lanes)
            for h in range(sides):
                span = pl.ds(h * LANES, LANES)
                wet = depth[at, span] > 0
                slope = views[h][pl.ds(j + 1, SUB), :] - views[h][pl.ds(j - 1, SUB), :]
                surf_out[at, span] = here[h]
                x_out[at, span] = jnp.where(wet, flow_x[at, span] - 0.25 * slope, 0.0)
                y_out[at, span] = jnp.where(
                    wet, flow_y[at, span] - 0.25 * (nxt[h] - prv[h]), 0.0
                )
        for copy in results(i):
            copy.start()
        return carry

    lax.fori_loop(0, CHUNKS, finish, 0)
    for i in range(CHUNKS):
        for copy in results(i):
            copy.wait()
    for copy in outward:
        copy.wait()


def solve_pass(last_part, made, placed, peak, depth, surf, flow_x, flow_y, force, west, east, south, north):
    rows, cols = depth.shape
    shape = (cols // LANES + 1, rows + 4 * SUB, LANES)
    ext = pltpu.VMEM(shape, F32)
    three = pltpu.VMEM((3, *shape), F32)
    plain = jax.ShapeDtypeStruct((rows, cols), F32)
    return pl.pallas_call(
        functools.partial(solve_kernel, last_part),
        in_specs=[IN_VMEM, IN_HBM] + [IN_VMEM] * 10,
        out_specs=[IN_HBM] * 4,
        out_shape=[jax.ShapeDtypeStruct(placed.shape, F32)] + [plain] * 3,
        input_output_aliases={1: 0},
        scratch_shapes=[pltpu.VMEM((rows, cols), F32)] * 3
        + [ext] * 8
        + [pltpu.VMEM((7, *shape), F32), three, three, ext]
        + [pltpu.SemaphoreType.DMA((2,)), pltpu.SemaphoreType.DMA((3 * CHUNKS,))],
        compiler_params=pltpu.CompilerParams(vmem_limit_bytes=VMEM_LIMIT),
        cost_estimate=pl.CostEstimate(
            flops=200 * depth.size, bytes_accessed=32 * depth.size, transcendentals=0
        ),
        name="solve",
    )(made, placed, peak, depth, surf, flow_x, flow_y, force, west, east, south, north)


def twin_pairs(axis):
    return [(i, i ^ 1) for i in range(lax.axis_size(axis))]


def other_x_pairs():
    size = lax.axis_size("gx")
    return [(i, (i + 1 if i % 2 else i - 1) % size) for i in range(size)]


def other_y_pairs():
    size_x, size_y = lax.axis_size("gx"), lax.axis_size("gy")
    pairs = []
    for i in range(size_x):
        for j in range(size_y):
            if j in (0, size_y - 1):
                target = (i ^ 1, j)
            else:
                target = (i, j + 1 if j % 2 else j - 1)
            pairs.append((i * size_y + j, target[0] * size_y + target[1]))
    return pairs


def spread_rounds(axis):
    size = lax.axis_size(axis)
    reach = 1
    while reach < size:
        if size & (size - 1) == 0:
            yield axis, [(i, i ^ reach) for i in range(size)]
        else:
            yield axis, [(i, (i + reach) % size) for i in range(size)]
        reach *= 2


def local(
    tracer, zonal_flow, meridional_flow, surface_prev, transport_x, transport_y, land_mask, levels
):
    count = tracer.shape[1]
    (
        force, depth, to_twin, to_other, tracer, surface_prev, transport_x, transport_y,
    ) = column_pass(tracer, land_mask, levels, surface_prev, transport_x, transport_y)
    fields = (depth, surface_prev, transport_x, transport_y, force)
    from_other = lax.ppermute(to_other, "gx", other_x_pairs())
    from_twin = lax.ppermute(to_twin, "gx", twin_pairs("gx"))
    to_south, to_north, zonal_flow, meridional_flow = strip_pass(
        zonal_flow, meridional_flow, tracer, *fields
    )
    to_twin, to_other, west, east = pack_pass(to_south, to_north, from_twin, from_other)
    from_twin = lax.ppermute(to_twin, "gy", twin_pairs("gy"))
    from_other = lax.ppermute(to_other, ("gx", "gy"), other_y_pairs())
    peak, south, north = peak_pass(depth, west, east, from_twin, from_other)
    halo = (west, east, south, north)
    rounds = [r for axis in ("gx", "gy") for r in spread_rounds(axis)]
    cuts = [count * i // PARTS for i in range(PARTS + 1)]
    parts = tuple(zip(cuts, cuts[1:]))
    first = len(rounds) - PARTS
    known, made, placed = (), None, None
    for turn, (axis, pairs) in enumerate(rounds):
        moved = lax.ppermute(peak, axis, pairs)
        if turn == 0:
            known = around_pass(depth, *halo)
            moved, known = lax.optimization_barrier((moved, known))
        if turn >= first:
            made, placed = tracer_pass(
                parts, turn - first, tracer, zonal_flow, meridional_flow, depth,
                west, east, known, made, placed,
            )
        peak = jnp.maximum(peak, moved)
        if first <= turn < len(rounds) - 1:
            peak, made = lax.optimization_barrier((peak, made))
    return solve_pass(parts[-1], made, placed, peak, *fields, *halo)


def solution(mesh):
    cell = P("gx", "gy")
    level = P(None, "gx", "gy")
    stack = P(None, None, "gx", "gy")
    return jax.shard_map(
        local,
        mesh=mesh,
        in_specs=(stack, level, level, cell, cell, cell, cell, cell),
        out_specs=(stack, cell, cell, cell),
        check_vma=False,
    )
```
